32 devices in a mesh: grp: 2 (over y), gx: 8 (over z, x), rep: 2 (over core).
Axes of the slice: x: 2, y: 2, z: 4, core: 2. Of those that a mesh axis runs over, the one named last changes fastest.
Arguments:
- fields: bfloat16 [4, 128, 32, 128, 128], P(('grp', 'rep'), 'gx'), parts along dimension 0, may hold values from -6 to 6
- targets: bfloat16 [4, 128, 3, 128, 128], P(('grp', 'rep'), 'gx'), parts along dimension 0, may hold values from -3 to 3
- multipliers: int32 [4, 128, 128, 128], P(('grp', 'rep'), 'gx'), parts along dimension 0, may hold values from -256 to 256
- local_weight: bfloat16 [32, 32], replicated, may hold values from -1 to 1
- proj_weight: bfloat16 [32, 3], replicated, may hold values from -1 to 1
- spectral_weight: bfloat16 [16, 256, 2, 32, 32], P('rep', 'gx'), may hold values from -9 to 9
Outputs:
- new_multipliers: float32 [4, 128, 128, 128], P(('grp', 'rep'), 'gx'), parts along dimension 0
- grad_spectral: float32 [32, 256, 2, 32, 32], P(('grp', 'rep'), 'gx'), parts along dimension 0
- grad_local: float32 [64, 32], P('grp'), parts along dimension 0
- grad_proj: float32 [64, 3], P('grp'), parts along dimension 0
- loss: float32 [2], P('grp'), parts along dimension 0
The draws below stay inside these ranges and needn't reach their ends.
There are 2 independent parts, one for each index of `grp`. The reference program is written for one: setup_inputs(seed, part) draws one part's arguments, and reference() takes and returns one part's arrays. A program takes and returns all parts, laid end to end along the dimension named above; an argument that names none is the same for every part. Nothing has to cross between parts.
All inputs are finite; a program needn't handle non-finite values.
Results may differ from the reference program's by a relative error of at most 0.0005.
The reference program's roundings to bfloat16 on the way count: a program that leaves them out, or rounds other values in their place, can miss the bound.
Values may be sent and summed in bfloat16 or wider, within the bound.
A program may use at most 256 MiB of HBM per device.

```python
import math
import jax
import jax.numpy as jnp
from jax import lax

C = 32
NX = 128
NY = 128
NZ = 128
MX = 16
MY = 16
MZ = 16
BATCH = 2
PAIRS = 256


def set_ends(result, own_key, low, top_value):
    longest = result.shape.index(max(result.shape))
    spots = []
    for shift in (0, 1):
        where = [jax.random.randint(jax.random.fold_in(own_key, axis), (), 0, length) for axis, length in enumerate(result.shape)]
        where[longest] = (where[longest] + shift) % result.shape[longest]
        spots.append(tuple(where))
    return result.at[spots[0]].set(low).at[spots[1]].set(top_value)


def levels(own_key, extent, shards, smallest, high):
    level, own = 1.0, jax.random.fold_in(own_key, 6)
    for dim, shards_of in shards:
        steps = jnp.exp(jax.random.uniform(jax.random.fold_in(own, dim), (shards_of,), jnp.float32, smallest / len(shards), high / len(shards)))
        level = level * jnp.repeat(steps, extent[dim] // shards_of).reshape([-1 if axis == dim else 1 for axis in range(len(extent))])
    return level


def centred(stream_key, shape, deviation, reach, split=(), held_as=jnp.bfloat16):
    level = levels(stream_key, shape, split, -0.22, 0.18) if split else 1.0
    drawn = jax.random.normal(stream_key, shape, jnp.float32) * deviation * level
    return jnp.minimum(jnp.maximum(drawn, -reach), reach).astype(held_as)


def setup_inputs(seed: int = 0, part: int = 0) -> dict:
    streams_of = jax.random.split(jax.random.key(seed), 7)
    part_keys = jax.random.split(jax.random.fold_in(streams_of[6], part), 7)
    return {
        "fields": centred(part_keys[0], (BATCH, NX, C, NY, NZ), 1.0, 6.0, ((0, 2), (1, 8))),
        "targets": centred(part_keys[1], (BATCH, NX, 3, NY, NZ), 0.5, 3.0, ((0, 2), (1, 8))),
        "multipliers": set_ends(jax.random.randint(part_keys[2], (BATCH, NX, NY, NZ), -256, 257), jax.random.fold_in(part_keys[2], 1), -256, 256).astype(jnp.int32),
        "local_weight": centred(streams_of[3], (C, C), C ** -0.5, 1.0),
        "proj_weight": centred(streams_of[4], (C, 3), C ** -0.5, 1.0),
        "spectral_weight": centred(streams_of[5], (MX, PAIRS, 2, C, C), 1.5, 9.0, ((0, 2), (1, 8))),
    }


penalty_weight = 0.5
precise = lax.Precision.HIGHEST

def widen(values):
    return lax.optimization_barrier(values).astype(jnp.float32)

def mode_numbers(count):
    position = jnp.arange(count, dtype=jnp.int32)
    return jnp.where(position < count // 2, position, position - count)

def fourier_tables(length, count):
    cells = jnp.arange(length, dtype=jnp.int32)
    phase = jnp.mod(cells[:, None] * mode_numbers(count)[None, :], length)
    angle = phase.astype(jnp.float32) * (2.0 * math.pi / length)
    return (jnp.cos(angle), jnp.sin(angle))

def to_last(values, table):
    return jnp.einsum('...kz,zm->...km', values, table, precision=precise)

def from_last(values, table):
    return jnp.einsum('...km,zm->...kz', values, table, precision=precise)

def forward_plane(field):
    cos_y, sin_y = fourier_tables(NY, MY)
    lookup_table_y = jnp.stack([cos_y, -sin_y], axis=1).astype(jnp.bfloat16)
    partial_value = jnp.einsum('...cyz,yrk->...crkz', widen(field), widen(lookup_table_y), precision=precise)
    cos_z, sin_z = fourier_tables(NZ, MZ)
    real_part = partial_value[..., 0, :, :]
    imag_part = partial_value[..., 1, :, :]
    spec_re = to_last(real_part, cos_z) + to_last(imag_part, sin_z)
    spec_im = to_last(imag_part, cos_z) - to_last(real_part, sin_z)
    stacked = jnp.stack([spec_re, spec_im], axis=-3)
    return stacked.reshape(stacked.shape[:-2] + (MY * MZ,))

def forward_x(slab, normalize_scale):
    cos_x, sin_x = fourier_tables(NX, MX)
    real_part = slab[:, :, :, 0]
    imag_part = slab[:, :, :, 1]
    spec_re = jnp.einsum('bxcp,xm->bmcp', real_part, cos_x, precision=precise) + jnp.einsum('bxcp,xm->bmcp', imag_part, sin_x, precision=precise)
    spec_im = jnp.einsum('bxcp,xm->bmcp', imag_part, cos_x, precision=precise) - jnp.einsum('bxcp,xm->bmcp', real_part, sin_x, precision=precise)
    return jnp.stack([spec_re, spec_im], axis=3) * normalize_scale

def multiply(weights, spectrum):
    w_re = weights[:, :, 0]
    w_im = weights[:, :, 1]
    s_re = spectrum[:, :, :, 0]
    s_im = spectrum[:, :, :, 1]
    t_re = jnp.einsum('mpoc,bmcp->bmop', w_re, s_re, precision=precise) - jnp.einsum('mpoc,bmcp->bmop', w_im, s_im, precision=precise)
    t_im = jnp.einsum('mpoc,bmcp->bmop', w_re, s_im, precision=precise) + jnp.einsum('mpoc,bmcp->bmop', w_im, s_re, precision=precise)
    return jnp.stack([t_re, t_im], axis=3)

def inverse_x(modes):
    cos_x, sin_x = fourier_tables(NX, MX)
    t_re = modes[:, :, :, 0]
    t_im = modes[:, :, :, 1]
    out_re = jnp.einsum('bmop,xm->bxop', t_re, cos_x, precision=precise) - jnp.einsum('bmop,xm->bxop', t_im, sin_x, precision=precise)
    output_imaginary = jnp.einsum('bmop,xm->bxop', t_im, cos_x, precision=precise) + jnp.einsum('bmop,xm->bxop', t_re, sin_x, precision=precise)
    return jnp.stack([out_re, output_imaginary], axis=3)

def inverse_plane(wave, normalize_scale):
    reshaped_array = wave.reshape(wave.shape[:-1] + (MY, MZ))
    w_re = reshaped_array[..., 0, :, :]
    w_im = reshaped_array[..., 1, :, :]
    cos_z, sin_z = fourier_tables(NZ, MZ)
    q_re = from_last(w_re, cos_z) - from_last(w_im, sin_z)
    q_im = from_last(w_im, cos_z) + from_last(w_re, sin_z)
    rounded = jnp.stack([q_re, q_im], axis=-3).astype(jnp.bfloat16)
    cos_y, sin_y = fourier_tables(NY, MY)
    lookup_table_y = jnp.stack([cos_y.T, -sin_y.T]).astype(jnp.bfloat16)
    return jnp.einsum('...orkz,rky->...oyz', widen(rounded), widen(lookup_table_y), precision=precise) * normalize_scale

def mode_grads(grads, spectrum):
    g_re = grads[:, :, :, 0]
    g_im = grads[:, :, :, 1]
    s_re = spectrum[:, :, :, 0]
    s_im = spectrum[:, :, :, 1]
    d_re = jnp.einsum('bmop,bmcp->mpoc', g_re, s_re, precision=precise) + jnp.einsum('bmop,bmcp->mpoc', g_im, s_im, precision=precise)
    d_im = jnp.einsum('bmop,bmcp->mpoc', g_im, s_re, precision=precise) - jnp.einsum('bmop,bmcp->mpoc', g_re, s_im, precision=precise)
    return jnp.stack([d_re, d_im], axis=2)

def central(values, axis):
    return (jnp.roll(values, -1, axis) - jnp.roll(values, 1, axis)) * 0.5

def reference(fields, targets, multipliers, local_weight, proj_weight, spectral_weight):
    normalize_scale = 1.0 / math.sqrt(NX * NY * NZ)
    weights = widen(spectral_weight)
    w_local = widen(local_weight)
    w_proj = widen(proj_weight)

    def plane_forward(plane, wave):
        preact = jnp.einsum('cyz,co->oyz', widen(plane), w_local, precision=precise) + inverse_plane(wave, normalize_scale)
        hidden = jax.nn.gelu(preact).astype(jnp.bfloat16)
        velocity = jnp.einsum('oyz,oj->jyz', widen(hidden), w_proj, precision=precise)
        return (preact, hidden, velocity)

    def plane_backward(sums, inputs):
        plane, wave, grad_vel = inputs
        preact, hidden, unused = plane_forward(plane, wave)
        grad_hidden = jnp.einsum('jyz,oj->oyz', widen(grad_vel), w_proj, precision=precise)
        grad_pre = jax.vjp(jax.nn.gelu, preact)[1](grad_hidden)[0].astype(jnp.bfloat16)
        grad_w = sums[0] + jnp.einsum('cyz,oyz->co', widen(plane), widen(grad_pre), precision=precise)
        grad_q = sums[1] + jnp.einsum('oyz,jyz->oj', widen(hidden), widen(grad_vel), precision=precise)
        return ((grad_w, grad_q), forward_plane(grad_pre))

    def single_example(total_sums, inputs):
        field, target, multiplier = inputs
        slab = lax.map(forward_plane, field)
        spectrum = forward_x(slab[None], normalize_scale)
        back = inverse_x(multiply(weights, spectrum))[0]
        velocity = lax.map(lambda pair: plane_forward(pair[0], pair[1])[2], (field, back))
        divergence = central(velocity[:, 0], 0) + central(velocity[:, 1], 1) + central(velocity[:, 2], 2)
        lam = multiplier.astype(jnp.float32) / 64.0
        penalty = lam + penalty_weight * divergence
        misfit = velocity - widen(target)
        loss_sum = jnp.sum(misfit * misfit) + jnp.sum(lam * divergence) + 0.5 * penalty_weight * jnp.sum(divergence * divergence)
        slopes = jnp.stack([central(penalty, 0), central(penalty, 1), central(penalty, 2)], axis=1)
        grad_vel = ((2.0 * misfit - slopes) / BATCH).astype(jnp.bfloat16)
        zero_w = jnp.zeros((C, C), jnp.float32)
        zero_q = jnp.zeros((C, 3), jnp.float32)
        sums, grad_slab = lax.scan(plane_backward, (zero_w, zero_q), (field, back, grad_vel))
        grads = forward_x(grad_slab[None], normalize_scale)
        grad_r = mode_grads(grads, spectrum)
        return ((total_sums[0] + grad_r, total_sums[1] + sums[0], total_sums[2] + sums[1], total_sums[3] + loss_sum), penalty)
    start_offset = (jnp.zeros((MX, MY * MZ, 2, C, C), jnp.float32), jnp.zeros((C, C), jnp.float32), jnp.zeros((C, 3), jnp.float32), jnp.zeros((), jnp.float32))
    total_sums, penalty_terms = lax.scan(single_example, start_offset, (fields, targets, multipliers))
    loss = (total_sums[3] / (BATCH * NX * NY * NZ)).reshape(1)
    return (penalty_terms, total_sums[0], total_sums[1] * normalize_scale, total_sums[2] * normalize_scale, loss)
```

```python
import functools
import math

import jax
import jax.numpy as jnp
import ml_dtypes
import numpy as np
from jax import lax
from jax.experimental import pallas as pl
from jax.experimental.pallas import tpu as pltpu
from jax.sharding import PartitionSpec as P

MX = 16
MY = 16
MZ = 16
ROWS = 16

penalty_weight = 0.5
precise = lax.Precision.HIGHEST
bf16 = jnp.bfloat16
f32 = jnp.float32
ROOT = math.sqrt(2.0 / math.pi)


def fourier_tables(length, count):
    position = np.arange(count)
    modes = np.where(position < count // 2, position, position - count)
    phase = np.mod(np.arange(length)[:, None] * modes[None, :], length)
    angle = phase.astype(np.float32) * np.float32(2.0 * math.pi / length)
    return np.cos(angle), np.sin(angle)


def halves(table):
    high = table.astype(ml_dtypes.bfloat16)
    low = (table - high.astype(np.float32)).astype(ml_dtypes.bfloat16)
    return high, low


def split(value):
    high = value.astype(bf16)
    return high, (value - high.astype(f32)).astype(bf16)


def dot(a, b):
    return jnp.dot(a, b, preferred_element_type=f32)


def dot_nt(a, b):
    return lax.dot_general(a, b, (((1,), (1,)), ((), ())), preferred_element_type=f32)


def dot_tn(a, b):
    return lax.dot_general(a, b, (((0,), (0,)), ((), ())), preferred_element_type=f32)


def plane_modes(load, count, ty, zt):
    parts = []
    for c in range(0, count, 2):
        pair = dot(ty, jnp.concatenate([load(c), load(c + 1)], axis=1))
        nz = pair.shape[1] // 2
        parts += [pair[:, :nz], pair[:, nz:]]
    turned = jnp.swapaxes(jnp.stack(parts, axis=0), 0, 1)
    real = turned[:MY].reshape(MY * count, nz)
    imag = turned[MY:].reshape(MY * count, nz)
    high, low = split(jnp.concatenate([real, imag], axis=1))
    both = dot_nt(zt, high)
    n = 2 * MZ
    return both[:n] + both[n:] + dot_nt(zt[:n], low)


def store_modes(out_ref, modes):
    if len(out_ref.shape) == 3:
        out_ref[0] = modes
        return
    owners, _, _, high, lanes = out_ref.shape
    width = modes.shape[1] // owners
    rows = 2 * high
    for d in range(owners):
        parts = [
            modes[j * rows : (j + 1) * rows, d * width : (d + 1) * width]
            for j in range(lanes // width)
        ]
        out_ref[d, 0] = jnp.concatenate(parts, axis=1).reshape(2, high, lanes)


def load_modes(m_ref, columns):
    if len(m_ref.shape) == 3:
        return m_ref[0]
    owners, _, _, high, lanes = m_ref.shape
    width = columns // owners
    blocks = [m_ref[d, 0].reshape(2 * high, lanes) for d in range(owners)]
    rows = [
        jnp.concatenate([block[:, j * width : (j + 1) * width] for block in blocks], axis=1)
        for j in range(lanes // width)
    ]
    return jnp.concatenate(rows, axis=0)


def forward_body(f_ref, ty_ref, zt_ref, out_ref):
    count = f_ref.shape[1]
    store_modes(out_ref, plane_modes(lambda c: f_ref[0, c], count, ty_ref[...], zt_ref[...]))


MESH = pl.DeviceIdType.MESH
PIECES = 4


def place():
    me = lax.axis_index("gx")
    return me, me // 2, lax.rem(me, 2)


def greet():
    _, z, x = place()
    zn = lax.axis_size("gx") // 2
    barrier = pltpu.get_barrier_semaphore()
    pl.semaphore_signal(barrier, inc=1, device_id={"gx": z * 2 + 1 - x}, device_id_type=MESH)
    for j in range(1, zn):
        t = lax.rem(z + j, zn)
        pl.semaphore_signal(barrier, inc=1, device_id={"gx": t * 2 + x}, device_id_type=MESH)
    pl.semaphore_wait(barrier, zn)


def send(src, dst, sems, where):
    copy = pltpu.make_async_remote_copy(
        src, dst, sems[0], sems[1], device_id=where, device_id_type=MESH
    )
    copy.start()
    return copy


def scatter_sum(a_ref, o_ref, xbuf, sbuf, zbuf, xs, xr, zs, zr, extra=None):
    _, z, x = place()
    zn, rows = a_ref.shape[1], a_ref.shape[2]
    step = rows // PIECES
    to_x = {"gx": z * 2 + 1 - x}
    first, second = [], []
    if extra is not None:
        e_ref, ebuf, es, er = extra
        swap = send(e_ref, ebuf.at[0], (es.at[0], er.at[0]), to_x)
    for p in range(PIECES):
        part = pl.ds(p * step, step)
        first.append(send(a_ref.at[1 - x, :, part], xbuf.at[p], (xs.at[p], xr.at[p]), to_x))
    if extra is not None:
        swap.wait()
        e_ref[...] = e_ref[...] + ebuf[0]
        spread = [
            send(e_ref, ebuf.at[j], (es.at[j], er.at[j]), {"gx": lax.rem(z + j, zn) * 2 + x})
            for j in range(1, zn)
        ]
    for p in range(PIECES):
        part = pl.ds(p * step, step)
        first[p].wait_recv()
        for j in (2, 1, 3):
            t = lax.rem(z + j, zn)
            sbuf[p, j - 1] = a_ref[x, t, part] + xbuf[p, t]
            copy = send(
                sbuf.at[p, j - 1],
                zbuf.at[p, j - 1],
                (zs.at[p, j - 1], zr.at[p, j - 1]),
                {"gx": t * 2 + x},
            )
            second.append((p, copy))
        o_ref[part] = a_ref[x, z, part] + xbuf[p, z]
    for p in range(PIECES):
        part = pl.ds(p * step, step)
        for q, copy in second:
            if q == p:
                copy.wait_recv()
        o_ref[part] = o_ref[part] + ((zbuf[p, 0] + zbuf[p, 1]) + zbuf[p, 2])
    for copy in first + [copy for _, copy in second]:
        copy.wait_send()
    if extra is not None:
        for copy in spread:
            copy.wait()
        e_ref[...] = (e_ref[...] + ebuf[1]) + (ebuf[2] + ebuf[3])


def scatter_scratch(zn, rows):
    step = rows // PIECES
    dma = pltpu.SemaphoreType.DMA
    return [
        pltpu.VMEM((2, zn, rows, 128), f32),
        pltpu.VMEM((PIECES, zn, step, 128), f32),
        pltpu.VMEM((PIECES, zn - 1, step, 128), f32),
        pltpu.VMEM((PIECES, zn - 1, step, 128), f32),
        dma((PIECES,)),
        dma((PIECES,)),
        dma((PIECES, zn - 1)),
        dma((PIECES, zn - 1)),
    ]


def x_sum(slab_ref, table_ref, a_ref):
    owners, xl, _, high, lanes = slab_ref.shape
    rows = table_ref.shape[0]
    for d in range(owners):
        turned = jnp.swapaxes(slab_ref[d].reshape(2 * xl, high, lanes), 0, 1)
        for k in range(high):
            a_ref[d % 2, d // 2, k * rows : (k + 1) * rows] = jnp.dot(
                table_ref[...], turned[k], precision=precise, preferred_element_type=f32
            )


def x_spread(all_ref, table_ref, slab_ref):
    owners, xl, _, high, lanes = slab_ref.shape
    rows = table_ref.shape[1]
    for d in range(owners):
        parts = [
            jnp.dot(
                table_ref[...],
                all_ref[d % 2, d // 2, k * rows : (k + 1) * rows],
                precision=precise,
                preferred_element_type=f32,
            )
            for k in range(high)
        ]
        turned = jnp.swapaxes(jnp.stack(parts, axis=0), 0, 1)
        slab_ref[d] = turned.reshape(xl, 2, high, lanes)


def forward_sum_body(f_ref, ty_ref, zt_ref, xt_ref, out_ref, slab_ref, *scatter):
    i = pl.program_id(0)
    count = f_ref.shape[1]
    pl.when(i == 0)(greet)
    store_modes(
        slab_ref.at[:, pl.ds(i, 1)],
        plane_modes(lambda c: f_ref[0, c], count, ty_ref[...], zt_ref[...]),
    )

    @pl.when(i == pl.num_programs(0) - 1)
    def _():
        x_sum(slab_ref, xt_ref, scatter[0])
        scatter_sum(scatter[0], out_ref, *scatter[1:])


def local_gather_body(s_ref, f_ref, kw_ref, got_ref, out_ref, all_ref, zs, zr, xs, xr):
    i = pl.program_id(0)
    steps = pl.num_programs(0)
    _, z, x = place()
    zn, rows = all_ref.shape[1], all_ref.shape[2]
    step = rows // PIECES
    to_x = {"gx": z * 2 + 1 - x}

    def along(p, j):
        part = pl.ds(p * step, step)
        return pltpu.make_async_remote_copy(
            all_ref.at[x, z, part],
            all_ref.at[x, z, part],
            zs.at[p, j - 1],
            zr.at[p, j - 1],
            device_id={"gx": lax.rem(z + j, zn) * 2 + x},
            device_id_type=MESH,
        )

    def across(p, j):
        part = pl.ds(p * step, step)
        t = lax.rem(z - j + zn, zn)
        return pltpu.make_async_remote_copy(
            all_ref.at[x, t, part],
            all_ref.at[x, t, part],
            xs.at[p, j],
            xr.at[p, j],
            device_id=to_x,
            device_id_type=MESH,
        )

    @pl.when(i == 0)
    def _():
        all_ref[x, z] = s_ref[...]
        greet()
        for p in range(PIECES):
            for j in (2, 1, 3):
                along(p, j).start()
            across(p, 0).start()

    for p in range(PIECES):

        @pl.when(i == 4 + 3 * p)
        def _(p=p):
            for j in range(1, zn):
                along(p, j).wait_recv()
                across(p, j).start()

    for y0 in range(0, f_ref.shape[2], 2 * ROWS):
        put_pair(out_ref, y0, dot(kw_ref[...], tile_pair(f_ref, y0)))

    @pl.when(i == steps - 1)
    def _():
        for p in range(PIECES):
            for j in range(zn):
                across(p, j).wait()
            for j in range(1, zn):
                along(p, j).wait_send()
        got_ref[...] = all_ref[...]


def tile_pair(ref, y0):
    count, nz = ref.shape[1], ref.shape[3]
    one = ref[0, :, pl.ds(y0, ROWS), :].reshape(count * ROWS, nz)
    two = ref[0, :, pl.ds(y0 + ROWS, ROWS), :].reshape(count * ROWS, nz)
    return jnp.concatenate([one, two], axis=1)


def put_pair(ref, y0, value):
    count, nz = ref.shape[1], ref.shape[3]
    ref[0, :, pl.ds(y0, ROWS), :] = value[:, :nz].reshape(count, ROWS, nz)
    ref[0, :, pl.ds(y0 + ROWS, ROWS), :] = value[:, nz:].reshape(count, ROWS, nz)


def local_body(f_ref, kw_ref, out_ref):
    for y0 in range(0, f_ref.shape[2], 2 * ROWS):
        put_pair(out_ref, y0, dot(kw_ref[...], tile_pair(f_ref, y0)))


def middle_all_body(scale, l_ref, all_ref, xb_ref, zi_ref, yi_ref, kp_ref, pre_ref, vel_ref, slab_ref):
    i = pl.program_id(0)

    @pl.when(i == 0)
    def _():
        x_spread(all_ref, xb_ref, slab_ref)

    modes_ref = slab_ref.at[:, pl.ds(i, 1)]
    middle_body(scale, l_ref, modes_ref, zi_ref, yi_ref, kp_ref, pre_ref, vel_ref)


def middle_body(scale, l_ref, m_ref, zi_ref, yi_ref, kp_ref, pre_ref, vel_ref):
    count, ny, nz = l_ref.shape[1], l_ref.shape[2], l_ref.shape[3]
    high, low = split(load_modes(m_ref, MY * count))
    wave = dot_tn(jnp.concatenate([high, high, low], axis=0), zi_ref[...])
    turned = jnp.swapaxes(wave.reshape(MY, count, 2 * nz), 0, 1)
    yi = yi_ref[...]
    for o in range(0, count, 2):
        pair = [
            jnp.concatenate([turned[i, :, :nz], turned[i, :, nz:]], axis=0) for i in (o, o + 1)
        ]
        both = dot(yi, jnp.concatenate(pair, axis=1).astype(bf16))
        pre_ref[0, o] = l_ref[0, o] + both[:, :nz] * scale
        pre_ref[0, o + 1] = l_ref[0, o + 1] + both[:, nz:] * scale

    for y0 in range(0, ny, 2 * ROWS):
        x = tile_pair(pre_ref, y0)
        t = jnp.tanh(x * (ROOT + (0.044715 * ROOT) * (x * x)))
        half = 0.5 * x
        hidden = (half + half * t).astype(bf16)
        put_pair(vel_ref, y0, dot(kp_ref[...], hidden))


def backward_body(
    f_ref, pre_ref, gv_ref, ty_ref, zt_ref, kpt_ref, out_ref, gw_ref, gq_ref, gp_ref
):
    count, ny, nz = f_ref.shape[1], f_ref.shape[2], f_ref.shape[3]

    @pl.when(pl.program_id(0) == 0)
    def _():
        gw_ref[...] = jnp.zeros_like(gw_ref)
        gq_ref[...] = jnp.zeros_like(gq_ref)

    hiddens, grads, fields, slopes = [], [], [], []
    for y0 in range(0, ny, 2 * ROWS):
        gv = tile_pair(gv_ref, y0)
        x = tile_pair(pre_ref, y0)
        cubic = (0.044715 * ROOT) * (x * x)
        t = jnp.tanh(x * (ROOT + cubic))
        cdf = 0.5 + 0.5 * t
        hidden = (x * cdf).astype(bf16)
        slope = cdf + (x * (ROOT + 3.0 * cubic)) * (0.5 - 0.5 * (t * t))
        gp = (dot(kpt_ref[...], gv) * slope).astype(bf16)
        put_pair(gp_ref, y0, gp)
        hiddens.append(hidden)
        grads.append(gp)
        slopes.append(gv)
        fields.append(tile_pair(f_ref, y0))
    gw_ref[...] += dot_nt(jnp.concatenate(fields, axis=1), jnp.concatenate(grads, axis=1))
    gq_ref[...] += dot_nt(jnp.concatenate(hiddens, axis=1), jnp.concatenate(slopes, axis=1))

    store_modes(out_ref, plane_modes(lambda c: gp_ref[0, c], count, ty_ref[...], zt_ref[...]))


def fold(total, columns):
    rows, cols = total.shape
    row = lax.broadcasted_iota(jnp.int32, total.shape, 0) % ROWS
    col = lax.broadcasted_iota(jnp.int32, total.shape, 1) % ROWS
    kept = jnp.where(row == col, total, 0.0).reshape(rows // ROWS, ROWS, cols)
    lane = lax.broadcasted_iota(jnp.int32, (cols, 128), 1)
    block = lax.broadcasted_iota(jnp.int32, (cols, 128), 0) // ROWS
    gather = jnp.where(lane == block + columns, 1.0, 0.0)
    return jnp.dot(jnp.sum(kept, axis=1), gather, precision=precise, preferred_element_type=f32)


def backward_sum_body(
    f_ref, pre_ref, gv_ref, ty_ref, zt_ref, kpt_ref, xt_ref, loss_ref,
    out_ref, sums_ref, gp_ref, gw_ref, gq_ref, slab_ref, e_ref, ebuf, es, er, *scatter
):
    i = pl.program_id(0)
    pl.when(i == 0)(greet)
    backward_body(
        f_ref, pre_ref, gv_ref, ty_ref, zt_ref, kpt_ref,
        slab_ref.at[:, pl.ds(i, 1)], gw_ref, gq_ref, gp_ref,
    )

    @pl.when(i == pl.num_programs(0) - 1)
    def _():
        x_sum(slab_ref, xt_ref, scatter[0])
        count = f_ref.shape[1]
        lane = lax.broadcasted_iota(jnp.int32, (count, 128), 1)
        e_ref[...] = (
            fold(gw_ref[...], 0)
            + fold(gq_ref[...], count)
            + jnp.where(lane == count + 3, loss_ref[0, 0], 0.0)
        )
        scatter_sum(scatter[0], out_ref, *scatter[1:], extra=(e_ref, ebuf, es, er))
        sums_ref[...] = e_ref[...]


def whole(shape):
    return pl.BlockSpec(shape, lambda i: (0,) * len(shape))


def plane(shape):
    return pl.BlockSpec((1,) + tuple(shape), lambda i: (i,) + (0,) * len(shape))


params = pltpu.CompilerParams(
    dimension_semantics=("arbitrary",), vmem_limit_bytes=56 * 1024 * 1024
)


def extended(value, axis_name):
    count = lax.axis_size(axis_name)
    up = [(i, (i + 1) % count) for i in range(count)]
    down = [(j, i) for i, j in up]
    before = lax.ppermute(value[-1:], axis_name, up)
    after = lax.ppermute(value[:1], axis_name, down)
    return jnp.concatenate([before, value, after], axis=0)


def central(values, axis):
    return (jnp.roll(values, -1, axis) - jnp.roll(values, 1, axis)) * 0.5


def local(fields, targets, multipliers, local_weight, proj_weight, spectral_weight):
    gx = lax.axis_size("gx")
    rep = lax.axis_size("rep")
    _, xl, C, NY, NZ = fields.shape
    NX = xl * gx
    PL = MY * MZ // gx
    scale = 1.0 / math.sqrt(NX * NY * NZ)
    fields, targets, multipliers = fields[0], targets[0], multipliers[0]

    cos_y, sin_y = fourier_tables(NY, MY)
    ty = jnp.asarray(np.concatenate([cos_y.T, -sin_y.T], 0).astype(ml_dtypes.bfloat16))
    yi = jnp.asarray(np.concatenate([cos_y, -sin_y], 1).astype(ml_dtypes.bfloat16))
    cos_z, sin_z = fourier_tables(NZ, MZ)
    zt = np.concatenate(
        [np.concatenate([cos_z.T, sin_z.T], 1), np.concatenate([-sin_z.T, cos_z.T], 1)], 0
    )
    direct = gx == 8 and MY % gx == 0 and 128 % (MY // gx * C) == 0
    KY = MY // gx if direct else 0
    PK = 128 // (KY * C) if direct else 1
    HZ = MZ // PK
    order = np.arange(2 * MZ).reshape(2, HZ, PK).transpose(2, 0, 1).reshape(-1)
    zt = zt[order]
    zi_high, zi_low = halves(zt)
    zt = jnp.asarray(np.concatenate([zi_high, zi_low], 0))
    zi = jnp.asarray(np.concatenate([zi_high, zi_low, zi_high], 0))
    cos_x, sin_x = fourier_tables(NX, MX)
    xt = np.stack(
        [np.stack([cos_x.T, sin_x.T], 1), np.stack([-sin_x.T, cos_x.T], 1)], 1
    )
    xt = xt.reshape(MX, 2, 2, gx, xl).transpose((0, 1, 3, 4, 2) if direct else (0, 1, 3, 2, 4))
    xt = xt.reshape(2 * MX, 2 * NX)
    x_forward = jnp.asarray(xt * np.float32(scale))
    x_back = jnp.asarray(np.ascontiguousarray(xt.T))

    def spread(weight):
        rows, columns = weight.shape
        left = jnp.asarray(np.kron(np.eye(rows), np.ones((ROWS, 1))), dtype=bf16)
        right = jnp.asarray(np.kron(np.eye(columns), np.ones((1, ROWS))), dtype=bf16)
        diagonal = jnp.asarray(np.kron(np.ones((rows, columns)), np.eye(ROWS)), dtype=bf16)
        return dot(dot(left, weight).astype(bf16), right).astype(bf16) * diagonal

    kw = spread(local_weight.T)
    kp = spread(proj_weight.T)
    kpt = spread(proj_weight)

    field_spec = plane((C, NY, NZ))
    modes_shape = jax.ShapeDtypeStruct((xl, 2 * MZ, MY * C), f32)
    modes_spec = plane((2 * MZ, MY * C))
    vel_spec = plane((3, NY, NZ))

    def to_owner(slab):
        slab = slab.reshape(xl, 2, MZ, MY, C).transpose(3, 2, 1, 0, 4)
        slab = slab.reshape(gx, PL, 2, xl, C).transpose(0, 2, 3, 1, 4)
        slab = slab.reshape(gx, 2 * xl, PL * C)
        slab = lax.all_to_all(slab, "gx", split_axis=0, concat_axis=0, tiled=True)
        out = jnp.dot(x_forward, slab.reshape(2 * NX, PL * C), precision=precise)
        return out.reshape(MX, 2, PL, C)

    def to_planes(modes):
        out = jnp.dot(x_back, modes.reshape(2 * MX, PL * C), precision=precise)
        out = out.reshape(gx, 2 * xl, PL * C)
        out = lax.all_to_all(out, "gx", split_axis=0, concat_axis=0, tiled=True)
        out = out.reshape(gx, 2, xl, PL, C).transpose(0, 3, 1, 2, 4)
        out = out.reshape(MY, MZ, 2, xl, C).transpose(3, 2, 1, 0, 4)
        return out.reshape(xl, 2 * MZ, MY * C)

    def both_samples(modes):
        part = modes.reshape(rep, MX // rep, 2, PL, C)
        return lax.all_to_all(part, "rep", split_axis=0, concat_axis=0, tiled=True)

    ZN = gx // 2
    QR = HZ * 2 * MX
    slab_scratch = pltpu.VMEM((gx, xl, 2, HZ, 128), f32)
    dma = pltpu.SemaphoreType.DMA

    def comm(number):
        return pltpu.CompilerParams(
            dimension_semantics=("arbitrary",),
            vmem_limit_bytes=56 * 1024 * 1024,
            collective_id=number,
            has_side_effects=True,
        )

    def chunk_modes(chunk):
        out = chunk.reshape(HZ, MX, 2, PK, KY, C).transpose(1, 2, 4, 0, 3, 5)
        return out.reshape(MX, 2, PL, C)

    if direct:
        me = lax.axis_index("gx")
        x_own = lax.dynamic_index_in_dim(x_forward.reshape(2 * MX, gx, 2 * xl), me, 1, False)
        x_out = lax.dynamic_index_in_dim(x_back.reshape(gx, 2 * xl, 2 * MX), me, 0, False)
        slab = pl.pallas_call(
            forward_sum_body,
            grid=(xl,),
            out_shape=jax.ShapeDtypeStruct((QR, 128), f32),
            in_specs=[field_spec, whole(ty.shape), whole(zt.shape), whole(x_own.shape)],
            out_specs=whole((QR, 128)),
            scratch_shapes=[slab_scratch] + scatter_scratch(ZN, QR),
            compiler_params=comm(1),
        )(fields, ty, zt, x_own)
    else:
        slab = pl.pallas_call(
            forward_body,
            grid=(xl,),
            out_shape=modes_shape,
            in_specs=[field_spec, whole(ty.shape), whole(zt.shape)],
            out_specs=modes_spec,
            compiler_params=params,
        )(fields, ty, zt)
        mapped = pl.pallas_call(
            local_body,
            grid=(xl,),
            out_shape=jax.ShapeDtypeStruct((xl, C, NY, NZ), f32),
            in_specs=[field_spec, whole(kw.shape)],
            out_specs=field_spec,
            compiler_params=pltpu.CompilerParams(vmem_limit_bytes=20 * 1024 * 1024),
        )(fields, kw)
    weights = spectral_weight
    weights = weights.transpose(2, 3, 4, 0, 1).reshape(1, 2, C, C, MX // rep * PL)
    weights = lax.all_gather(weights, "rep", axis=0, tiled=True)
    spectrum = chunk_modes(slab) if direct else to_owner(slab)
    KX = MX // rep
    turned = spectrum.reshape(rep, KX, 2, PL, C).transpose(0, 2, 4, 1, 3)
    turned = turned.reshape(rep, 2, 1, C, KX * PL)
    w_re, w_im = weights[:, 0].astype(f32), weights[:, 1].astype(f32)
    s_re, s_im = turned[:, 0], turned[:, 1]
    product = jnp.stack(
        [jnp.sum(w_re * s_re - w_im * s_im, axis=2), jnp.sum(w_re * s_im + w_im * s_re, axis=2)],
        axis=1,
    )
    product = product.reshape(rep, 2, C, KX, PL).transpose(0, 3, 1, 4, 2)
    product = product.reshape(MX, 2, PL, C)
    spectra = both_samples(spectrum)
    middle_shape = (
        jax.ShapeDtypeStruct((xl, C, NY, NZ), f32),
        jax.ShapeDtypeStruct((xl, 3, NY, NZ), f32),
    )
    if direct:
        part = product.reshape(MX, 2, KY, HZ, PK, C).transpose(3, 0, 1, 4, 2, 5)
        gathered, mapped = pl.pallas_call(
            local_gather_body,
            grid=(xl,),
            out_shape=(
                jax.ShapeDtypeStruct((2, ZN, QR, 128), f32),
                jax.ShapeDtypeStruct((xl, C, NY, NZ), f32),
            ),
            in_specs=[whole((QR, 128)), field_spec, whole(kw.shape)],
            out_specs=(whole((2, ZN, QR, 128)), field_spec),
            scratch_shapes=[pltpu.VMEM((2, ZN, QR, 128), f32)]
            + [dma((PIECES, ZN - 1))] * 2
            + [dma((PIECES, ZN))] * 2,
            compiler_params=comm(2),
        )(part.reshape(QR, 128), fields, kw)
        pre, velocity = pl.pallas_call(
            functools.partial(middle_all_body, scale),
            grid=(xl,),
            out_shape=middle_shape,
            in_specs=[field_spec, whole(gathered.shape), whole(x_out.shape)]
            + [whole(zi.shape), whole(yi.shape), whole(kp.shape)],
            out_specs=(field_spec, vel_spec),
            scratch_shapes=[slab_scratch],
            compiler_params=params,
        )(mapped, gathered, x_out, zi, yi, kp)
    else:
        wave = to_planes(product)
        pre, velocity = pl.pallas_call(
            functools.partial(middle_body, scale),
            grid=(xl,),
            out_shape=middle_shape,
            in_specs=[field_spec, modes_spec, whole(zi.shape), whole(yi.shape), whole(kp.shape)],
            out_specs=(field_spec, vel_spec),
            compiler_params=params,
        )(mapped, wave, zi, yi, kp)

    padded = extended(velocity[:, 0].astype(bf16), "gx").astype(f32)
    slope_x = (padded[2:] - padded[:-2]) * 0.5
    divergence = slope_x + central(velocity[:, 1], 1) + central(velocity[:, 2], 2)
    lam = multipliers.astype(f32) / 64.0
    penalty = lam + penalty_weight * divergence
    misfit = velocity - targets.astype(f32)
    loss_sum = (
        jnp.sum(misfit * misfit)
        + jnp.sum(lam * divergence)
        + 0.5 * penalty_weight * jnp.sum(divergence * divergence)
    )
    padded = extended(penalty.astype(bf16), "gx").astype(f32)
    pen_x = (padded[2:] - padded[:-2]) * 0.5
    slopes = jnp.stack([pen_x, central(penalty, 1), central(penalty, 2)], axis=1)
    grad_vel = ((2.0 * misfit - slopes) / rep).astype(bf16)

    wide = C * ROWS
    if direct:
        chunk, sums = pl.pallas_call(
            backward_sum_body,
            grid=(xl,),
            out_shape=(
                jax.ShapeDtypeStruct((QR, 128), f32),
                jax.ShapeDtypeStruct((C, 128), f32),
            ),
            in_specs=[field_spec, field_spec, vel_spec]
            + [whole(ty.shape), whole(zt.shape), whole(kpt.shape), whole(x_own.shape)]
            + [pl.BlockSpec(memory_space=pltpu.SMEM)],
            out_specs=(whole((QR, 128)), whole((C, 128))),
            scratch_shapes=[
                pltpu.VMEM((1, C, NY, NZ), bf16),
                pltpu.VMEM((wide, wide), f32),
                pltpu.VMEM((wide, 3 * ROWS), f32),
                slab_scratch,
                pltpu.VMEM((C, 128), f32),
                pltpu.VMEM((ZN, C, 128), f32),
                dma((ZN,)),
                dma((ZN,)),
            ]
            + scatter_scratch(ZN, QR),
            compiler_params=comm(3),
        )(fields, pre, grad_vel, ty, zt, kpt, x_own, loss_sum.reshape(1, 1))
        grads = chunk_modes(chunk)
        both = jnp.concatenate(
            [grads.reshape(rep, -1), jnp.broadcast_to(sums.reshape(1, -1), (rep, sums.size))],
            axis=1,
        )
        both = lax.all_to_all(both, "rep", split_axis=0, concat_axis=0, tiled=True)
        size = grads.size // rep
        grads = both[:, :size].reshape(rep, MX // rep, 2, PL, C)
        sums = jnp.sum(both[:, size:], axis=0).reshape(C, 128)
        grad_w, grad_q, loss = sums[:, :C], sums[:, C : C + 3], sums[0, C + 3 : C + 4]
    else:
        grad_slab, gw, gq = pl.pallas_call(
            backward_body,
            grid=(xl,),
            out_shape=(
                modes_shape,
                jax.ShapeDtypeStruct((wide, wide), f32),
                jax.ShapeDtypeStruct((wide, 3 * ROWS), f32),
            ),
            in_specs=[field_spec, field_spec, vel_spec]
            + [whole(ty.shape), whole(zt.shape), whole(kpt.shape)],
            out_specs=(modes_spec, whole((wide, wide)), whole((wide, 3 * ROWS))),
            scratch_shapes=[pltpu.VMEM((1, C, NY, NZ), bf16)],
            compiler_params=params,
        )(fields, pre, grad_vel, ty, zt, kpt)
        gather = jnp.asarray(np.kron(np.eye(C), np.ones((1, ROWS))).astype(np.float32))
        gather_q = jnp.asarray(np.kron(np.eye(3), np.ones((ROWS, 1))).astype(np.float32))
        mask = jnp.asarray(np.kron(np.ones((C, C)), np.eye(ROWS)).astype(np.float32))
        mask_q = jnp.asarray(np.kron(np.ones((C, 3)), np.eye(ROWS)).astype(np.float32))
        grad_w = jnp.dot(gather, gw * mask, precision=precise)
        grad_w = jnp.dot(grad_w, gather.T, precision=precise)
        grad_q = jnp.dot(gather, gq * mask_q, precision=precise)
        grad_q = jnp.dot(grad_q, gather_q, precision=precise)
        grads = both_samples(to_owner(grad_slab))
        packed = jnp.concatenate([grad_w.reshape(-1), grad_q.reshape(-1), loss_sum.reshape(1)])
        packed = lax.psum(packed, ("gx", "rep"))
        grad_w = packed[: C * C].reshape(C, C)
        grad_q = packed[C * C : C * C + 3 * C].reshape(C, 3)
        loss = packed[-1:]
    loss = loss / (rep * NX * NY * NZ)

    g_re, g_im = grads[:, :, 0], grads[:, :, 1]
    across = jnp.stack([jnp.stack([g_re, g_im], 3), jnp.stack([g_im, -g_re], 3)], 1)
    terms = [
        across[b, t][..., None] * spectra[b, :, t][:, :, None, None, :]
        for b in range(rep)
        for t in range(2)
    ]
    grad_r = sum(terms[1:], terms[0])
    return (penalty[None], grad_r, grad_w * scale, grad_q * scale, loss)


def solution(mesh):
    in_specs = (
        P(("grp", "rep"), "gx", None, None, None),
        P(("grp", "rep"), "gx", None, None, None),
        P(("grp", "rep"), "gx", None, None),
        P(),
        P(),
        P("rep", "gx", None, None, None),
    )
    out_specs = (
        P(("grp", "rep"), "gx", None, None),
        P(("grp", "rep"), "gx", None, None, None),
        P("grp", None),
        P("grp", None),
        P("grp"),
    )
    return jax.shard_map(local, mesh=mesh, in_specs=in_specs, out_specs=out_specs, check_vma=False)
```

```python
import functools
import math

import jax
import jax.numpy as jnp
import ml_dtypes
import numpy as np
from jax import lax
from jax.experimental import pallas as pl
from jax.experimental.pallas import tpu as pltpu
from jax.sharding import PartitionSpec as P

MX = 16
MY = 16
MZ = 16
ROWS = 16

penalty_weight = 0.5
precise = lax.Precision.HIGHEST
bf16 = jnp.bfloat16
f32 = jnp.float32
ROOT = math.sqrt(2.0 / math.pi)


def fourier_tables(length, count):
    position = np.arange(count)
    modes = np.where(position < count // 2, position, position - count)
    phase = np.mod(np.arange(length)[:, None] * modes[None, :], length)
    angle = phase.astype(np.float32) * np.float32(2.0 * math.pi / length)
    return np.cos(angle), np.sin(angle)


def halves(table):
    high = table.astype(ml_dtypes.bfloat16)
    low = (table - high.astype(np.float32)).astype(ml_dtypes.bfloat16)
    return high, low


def split(value):
    high = value.astype(bf16)
    return high, (value - high.astype(f32)).astype(bf16)


def dot(a, b):
    return jnp.dot(a, b, preferred_element_type=f32)


def dot_nt(a, b):
    return lax.dot_general(a, b, (((1,), (1,)), ((), ())), preferred_element_type=f32)


def dot_tn(a, b):
    return lax.dot_general(a, b, (((0,), (0,)), ((), ())), preferred_element_type=f32)


def plane_modes(load, count, ty, zt):
    parts = []
    for c in range(0, count, 2):
        pair = dot(ty, jnp.concatenate([load(c), load(c + 1)], axis=1))
        nz = pair.shape[1] // 2
        parts += [pair[:, :nz], pair[:, nz:]]
    turned = jnp.swapaxes(jnp.stack(parts, axis=0), 0, 1)
    real = turned[:MY].reshape(MY * count, nz)
    imag = turned[MY:].reshape(MY * count, nz)
    high, low = split(jnp.concatenate([real, imag], axis=1))
    both = dot_nt(zt, high)
    n = 2 * MZ
    return both[:n] + both[n:] + dot_nt(zt[:n], low)


def store_modes(out_ref, modes):
    if len(out_ref.shape) == 3:
        out_ref[0] = modes
        return
    owners, _, _, high, lanes = out_ref.shape
    width = modes.shape[1] // owners
    rows = 2 * high
    for d in range(owners):
        parts = [
            modes[j * rows : (j + 1) * rows, d * width : (d + 1) * width]
            for j in range(lanes // width)
        ]
        out_ref[d, 0] = jnp.concatenate(parts, axis=1).reshape(2, high, lanes)


def load_modes(m_ref, columns):
    if len(m_ref.shape) == 3:
        return m_ref[0]
    owners, _, _, high, lanes = m_ref.shape
    width = columns // owners
    blocks = [m_ref[d, 0].reshape(2 * high, lanes) for d in range(owners)]
    rows = [
        jnp.concatenate([block[:, j * width : (j + 1) * width] for block in blocks], axis=1)
        for j in range(lanes // width)
    ]
    return jnp.concatenate(rows, axis=0)


def forward_body(f_ref, ty_ref, zt_ref, out_ref):
    count = f_ref.shape[1]
    store_modes(out_ref, plane_modes(lambda c: f_ref[0, c], count, ty_ref[...], zt_ref[...]))


MESH = pl.DeviceIdType.MESH
PIECES = 4


def place():
    me = lax.axis_index("gx")
    return me, me // 2, lax.rem(me, 2)


def greet(ring=False):
    _, z, x = place()
    zn = lax.axis_size("gx") // 2
    barrier = pltpu.get_barrier_semaphore()
    pl.semaphore_signal(barrier, inc=1, device_id={"gx": z * 2 + 1 - x}, device_id_type=MESH)
    for j in range(1, zn):
        t = lax.rem(z + j, zn)
        pl.semaphore_signal(barrier, inc=1, device_id={"gx": t * 2 + x}, device_id_type=MESH)
    if ring:
        me = z * 2 + x
        t = lax.rem(me + 2 * x - 1 + 2 * zn, 2 * zn)
        pl.semaphore_signal(barrier, inc=1, device_id={"gx": t}, device_id_type=MESH)
    pl.semaphore_wait(barrier, zn + (1 if ring else 0))


def send(src, dst, sems, where):
    copy = pltpu.make_async_remote_copy(
        src, dst, sems[0], sems[1], device_id=where, device_id_type=MESH
    )
    copy.start()
    return copy


def scatter_sum(a_ref, o_ref, xbuf, sbuf, zbuf, xs, xr, zs, zr, extra=None):
    _, z, x = place()
    zn, rows = a_ref.shape[1], a_ref.shape[2]
    step = rows // PIECES
    to_x = {"gx": z * 2 + 1 - x}
    first, second = [], []
    if extra is not None:
        e_ref, ebuf, es, er = extra
        swap = send(e_ref, ebuf.at[0], (es.at[0], er.at[0]), to_x)
    for p in range(PIECES):
        part = pl.ds(p * step, step)
        first.append(send(a_ref.at[1 - x, :, part], xbuf.at[p], (xs.at[p], xr.at[p]), to_x))
    if extra is not None:
        swap.wait()
        e_ref[...] = e_ref[...] + ebuf[0]
        spread = [
            send(e_ref, ebuf.at[j], (es.at[j], er.at[j]), {"gx": lax.rem(z + j, zn) * 2 + x})
            for j in range(1, zn)
        ]
    for p in range(PIECES):
        part = pl.ds(p * step, step)
        first[p].wait_recv()
        for j in (2, 1, 3):
            t = lax.rem(z + j, zn)
            sbuf[p, j - 1] = a_ref[x, t, part] + xbuf[p, t]
            copy = send(
                sbuf.at[p, j - 1],
                zbuf.at[p, j - 1],
                (zs.at[p, j - 1], zr.at[p, j - 1]),
                {"gx": t * 2 + x},
            )
            second.append((p, copy))
        o_ref[part] = a_ref[x, z, part] + xbuf[p, z]
    for p in range(PIECES):
        part = pl.ds(p * step, step)
        for q, copy in second:
            if q == p:
                copy.wait_recv()
        o_ref[part] = o_ref[part] + ((zbuf[p, 0] + zbuf[p, 1]) + zbuf[p, 2])
    for copy in first + [copy for _, copy in second]:
        copy.wait_send()
    if extra is not None:
        for copy in spread:
            copy.wait()
        e_ref[...] = (e_ref[...] + ebuf[1]) + (ebuf[2] + ebuf[3])


def scatter_scratch(zn, rows):
    step = rows // PIECES
    dma = pltpu.SemaphoreType.DMA
    return [
        pltpu.VMEM((2, zn, rows, 128), f32),
        pltpu.VMEM((PIECES, zn, step, 128), f32),
        pltpu.VMEM((PIECES, zn - 1, step, 128), f32),
        pltpu.VMEM((PIECES, zn - 1, step, 128), f32),
        dma((PIECES,)),
        dma((PIECES,)),
        dma((PIECES, zn - 1)),
        dma((PIECES, zn - 1)),
    ]


def x_sum(slab_ref, table_ref, a_ref):
    owners, xl, _, high, lanes = slab_ref.shape
    rows = table_ref.shape[0]
    for d in range(owners):
        turned = jnp.swapaxes(slab_ref[d].reshape(2 * xl, high, lanes), 0, 1)
        for k in range(high):
            a_ref[d % 2, d // 2, k * rows : (k + 1) * rows] = jnp.dot(
                table_ref[...], turned[k], precision=precise, preferred_element_type=f32
            )


def x_spread(all_ref, table_ref, slab_ref):
    owners, xl, _, high, lanes = slab_ref.shape
    rows = table_ref.shape[1]
    for d in range(owners):
        parts = [
            jnp.dot(
                table_ref[...],
                all_ref[d % 2, d // 2, k * rows : (k + 1) * rows],
                precision=precise,
                preferred_element_type=f32,
            )
            for k in range(high)
        ]
        turned = jnp.swapaxes(jnp.stack(parts, axis=0), 0, 1)
        slab_ref[d] = turned.reshape(xl, 2, high, lanes)


def forward_sum_body(f_ref, ty_ref, zt_ref, xt_ref, out_ref, slab_ref, *scatter):
    i = pl.program_id(0)
    count = f_ref.shape[1]
    pl.when(i == 0)(greet)
    store_modes(
        slab_ref.at[:, pl.ds(i, 1)],
        plane_modes(lambda c: f_ref[0, c], count, ty_ref[...], zt_ref[...]),
    )

    @pl.when(i == pl.num_programs(0) - 1)
    def _():
        x_sum(slab_ref, xt_ref, scatter[0])
        scatter_sum(scatter[0], out_ref, *scatter[1:])


def forward_body(f_ref, ty_ref, zt_ref, out_ref):
    count = f_ref.shape[1]
    store_modes(out_ref, plane_modes(lambda c: f_ref[0, c], count, ty_ref[...], zt_ref[...]))


MESH = pl.DeviceIdType.MESH
PIECES = 4


def place():
    me = lax.axis_index("gx")
    return me, me // 2, lax.rem(me, 2)


def greet(ring=False):
    _, z, x = place()
    zn = lax.axis_size("gx") // 2
    barrier = pltpu.get_barrier_semaphore()
    pl.semaphore_signal(barrier, inc=1, device_id={"gx": z * 2 + 1 - x}, device_id_type=MESH)
    for j in range(1, zn):
        t = lax.rem(z + j, zn)
        pl.semaphore_signal(barrier, inc=1, device_id={"gx": t * 2 + x}, device_id_type=MESH)
    if ring:
        me = z * 2 + x
        t = lax.rem(me + 2 * x - 1 + 2 * zn, 2 * zn)
        pl.semaphore_signal(barrier, inc=1, device_id={"gx": t}, device_id_type=MESH)
    pl.semaphore_wait(barrier, zn + (1 if ring else 0))


def send(src, dst, sems, where):
    copy = pltpu.make_async_remote_copy(
        src, dst, sems[0], sems[1], device_id=where, device_id_type=MESH
    )
    copy.start()
    return copy


def scatter_sum(a_ref, o_ref, xbuf, sbuf, zbuf, xs, xr, zs, zr, extra=None):
    _, z, x = place()
    zn, rows = a_ref.shape[1], a_ref.shape[2]
    step = rows // PIECES
    to_x = {"gx": z * 2 + 1 - x}
    first, second = [], []
    if extra is not None:
        e_ref, ebuf, es, er = extra
        swap = send(e_ref, ebuf.at[0], (es.at[0], er.at[0]), to_x)
    for p in range(PIECES):
        part = pl.ds(p * step, step)
        first.append(send(a_ref.at[1 - x, :, part], xbuf.at[p], (xs.at[p], xr.at[p]), to_x))
    if extra is not None:
        swap.wait()
        e_ref[...] = e_ref[...] + ebuf[0]
        spread = [
            send(e_ref, ebuf.at[j], (es.at[j], er.at[j]), {"gx": lax.rem(z + j, zn) * 2 + x})
            for j in range(1, zn)
        ]
    for p in range(PIECES):
        part = pl.ds(p * step, step)
        first[p].wait_recv()
        for j in (2, 1, 3):
            t = lax.rem(z + j, zn)
            sbuf[p, j - 1] = a_ref[x, t, part] + xbuf[p, t]
            copy = send(
                sbuf.at[p, j - 1],
                zbuf.at[p, j - 1],
                (zs.at[p, j - 1], zr.at[p, j - 1]),
                {"gx": t * 2 + x},
            )
            second.append((p, copy))
        o_ref[part] = a_ref[x, z, part] + xbuf[p, z]
    for p in range(PIECES):
        part = pl.ds(p * step, step)
        for q, copy in second:
            if q == p:
                copy.wait_recv()
        o_ref[part] = o_ref[part] + ((zbuf[p, 0] + zbuf[p, 1]) + zbuf[p, 2])
    for copy in first + [copy for _, copy in second]:
        copy.wait_send()
    if extra is not None:
        for copy in spread:
            copy.wait()
        e_ref[...] = (e_ref[...] + ebuf[1]) + (ebuf[2] + ebuf[3])


def scatter_scratch(zn, rows):
    step = rows // PIECES
    dma = pltpu.SemaphoreType.DMA
    return [
        pltpu.VMEM((2, zn, rows, 128), f32),
        pltpu.VMEM((PIECES, zn, step, 128), f32),
        pltpu.VMEM((PIECES, zn - 1, step, 128), f32),
        pltpu.VMEM((PIECES, zn - 1, step, 128), f32),
        dma((PIECES,)),
        dma((PIECES,)),
        dma((PIECES, zn - 1)),
        dma((PIECES, zn - 1)),
    ]


def x_sum(slab_ref, table_ref, a_ref):
    owners, xl, _, high, lanes = slab_ref.shape
    rows = table_ref.shape[0]
    for d in range(owners):
        turned = jnp.swapaxes(slab_ref[d].reshape(2 * xl, high, lanes), 0, 1)
        for k in range(high):
            a_ref[d % 2, d // 2, k * rows : (k + 1) * rows] = jnp.dot(
                table_ref[...], turned[k], precision=precise, preferred_element_type=f32
            )


def x_spread(all_ref, table_ref, slab_ref):
    owners, xl, _, high, lanes = slab_ref.shape
    rows = table_ref.shape[1]
    for d in range(owners):
        parts = [
            jnp.dot(
                table_ref[...],
                all_ref[d % 2, d // 2, k * rows : (k + 1) * rows],
                precision=precise,
                preferred_element_type=f32,
            )
            for k in range(high)
        ]
        turned = jnp.swapaxes(jnp.stack(parts, axis=0), 0, 1)
        slab_ref[d] = turned.reshape(xl, 2, high, lanes)


def forward_sum_body(f_ref, ty_ref, zt_ref, xt_ref, out_ref, slab_ref, *scatter):
    i = pl.program_id(0)
    count = f_ref.shape[1]
    pl.when(i == 0)(greet)
    store_modes(
        slab_ref.at[:, pl.ds(i, 1)],
        plane_modes(lambda c: f_ref[0, c], count, ty_ref[...], zt_ref[...]),
    )

    @pl.when(i == pl.num_programs(0) - 1)
    def _():
        x_sum(slab_ref, xt_ref, scatter[0])
        scatter_sum(scatter[0], out_ref, *scatter[1:])


def local_gather_body(s_ref, f_ref, kw_ref, got_ref, out_ref, all_ref, zs, zr, xs, xr):
    i = pl.program_id(0)
    steps = pl.num_programs(0)
    _, z, x = place()
    zn, rows = all_ref.shape[1], all_ref.shape[2]
    step = rows // PIECES
    to_x = {"gx": z * 2 + 1 - x}

    def along(p, j):
        part = pl.ds(p * step, step)
        return pltpu.make_async_remote_copy(
            all_ref.at[x, z, part],
            all_ref.at[x, z, part],
            zs.at[p, j - 1],
            zr.at[p, j - 1],
            device_id={"gx": lax.rem(z + j, zn) * 2 + x},
            device_id_type=MESH,
        )

    def across(p, j):
        part = pl.ds(p * step, step)
        t = lax.rem(z - j + zn, zn)
        return pltpu.make_async_remote_copy(
            all_ref.at[x, t, part],
            all_ref.at[x, t, part],
            xs.at[p, j],
            xr.at[p, j],
            device_id=to_x,
            device_id_type=MESH,
        )

    @pl.when(i == 0)
    def _():
        all_ref[x, z] = s_ref[...]
        greet()
        for p in range(PIECES):
            for j in (2, 1, 3):
                along(p, j).start()
            across(p, 0).start()

    for p in range(PIECES):

        @pl.when(i == 4 + 3 * p)
        def _(p=p):
            for j in range(1, zn):
                along(p, j).wait_recv()
                across(p, j).start()

    for y0 in range(0, f_ref.shape[2], 2 * ROWS):
        put_pair(out_ref, y0, dot(kw_ref[...], tile_pair(f_ref, y0)))

    @pl.when(i == steps - 1)
    def _():
        for p in range(PIECES):
            for j in range(zn):
                across(p, j).wait()
            for j in range(1, zn):
                along(p, j).wait_send()
        got_ref[...] = all_ref[...]


def tile_pair(ref, y0):
    count, nz = ref.shape[1], ref.shape[3]
    one = ref[0, :, pl.ds(y0, ROWS), :].reshape(count * ROWS, nz)
    two = ref[0, :, pl.ds(y0 + ROWS, ROWS), :].reshape(count * ROWS, nz)
    return jnp.concatenate([one, two], axis=1)


def put_pair(ref, y0, value):
    count, nz = ref.shape[1], ref.shape[3]
    ref[0, :, pl.ds(y0, ROWS), :] = value[:, :nz].reshape(count, ROWS, nz)
    ref[0, :, pl.ds(y0 + ROWS, ROWS), :] = value[:, nz:].reshape(count, ROWS, nz)


def local_body(f_ref, kw_ref, out_ref):
    for y0 in range(0, f_ref.shape[2], 2 * ROWS):
        put_pair(out_ref, y0, dot(kw_ref[...], tile_pair(f_ref, y0)))


def middle_body(scale, l_ref, m_ref, zi_ref, yi_ref, kp_ref, pre_ref, vel_ref):
    count, ny, nz = l_ref.shape[1], l_ref.shape[2], l_ref.shape[3]
    high, low = split(load_modes(m_ref, MY * count))
    wave = dot_tn(jnp.concatenate([high, high, low], axis=0), zi_ref[...])
    turned = jnp.swapaxes(wave.reshape(MY, count, 2 * nz), 0, 1)
    yi = yi_ref[...]
    for o in range(0, count, 2):
        pair = [
            jnp.concatenate([turned[i, :, :nz], turned[i, :, nz:]], axis=0) for i in (o, o + 1)
        ]
        both = dot(yi, jnp.concatenate(pair, axis=1).astype(bf16))
        pre_ref[0, o] = l_ref[0, o] + both[:, :nz] * scale
        pre_ref[0, o + 1] = l_ref[0, o + 1] + both[:, nz:] * scale

    for y0 in range(0, ny, 2 * ROWS):
        x = tile_pair(pre_ref, y0)
        t = jnp.tanh(x * (ROOT + (0.044715 * ROOT) * (x * x)))
        half = 0.5 * x
        hidden = (half + half * t).astype(bf16)
        put_pair(vel_ref, y0, dot(kp_ref[...], hidden))


def backward_body(
    f_ref, pre_ref, gv_ref, ty_ref, zt_ref, kpt_ref, out_ref, gw_ref, gq_ref, gp_ref, first=0
):
    count, ny, nz = f_ref.shape[1], f_ref.shape[2], f_ref.shape[3]

    @pl.when(pl.program_id(0) == first)
    def _():
        gw_ref[...] = jnp.zeros_like(gw_ref)
        gq_ref[...] = jnp.zeros_like(gq_ref)

    hiddens, grads, fields, slopes = [], [], [], []
    for y0 in range(0, ny, 2 * ROWS):
        gv = tile_pair(gv_ref, y0)
        x = tile_pair(pre_ref, y0)
        cubic = (0.044715 * ROOT) * (x * x)
        t = jnp.tanh(x * (ROOT + cubic))
        cdf = 0.5 + 0.5 * t
        hidden = (x * cdf).astype(bf16)
        slope = cdf + (x * (ROOT + 3.0 * cubic)) * (0.5 - 0.5 * (t * t))
        gp = (dot(kpt_ref[...], gv) * slope).astype(bf16)
        put_pair(gp_ref, y0, gp)
        hiddens.append(hidden)
        grads.append(gp)
        slopes.append(gv)
        fields.append(tile_pair(f_ref, y0))
    gw_ref[...] += dot_nt(jnp.concatenate(fields, axis=1), jnp.concatenate(grads, axis=1))
    gq_ref[...] += dot_nt(jnp.concatenate(hiddens, axis=1), jnp.concatenate(slopes, axis=1))

    store_modes(out_ref, plane_modes(lambda c: gp_ref[0, c], count, ty_ref[...], zt_ref[...]))


def fold(total, columns):
    rows, cols = total.shape
    row = lax.broadcasted_iota(jnp.int32, total.shape, 0) % ROWS
    col = lax.broadcasted_iota(jnp.int32, total.shape, 1) % ROWS
    kept = jnp.where(row == col, total, 0.0).reshape(rows // ROWS, ROWS, cols)
    lane = lax.broadcasted_iota(jnp.int32, (cols, 128), 1)
    block = lax.broadcasted_iota(jnp.int32, (cols, 128), 0) // ROWS
    gather = jnp.where(lane == block + columns, 1.0, 0.0)
    return jnp.dot(jnp.sum(kept, axis=1), gather, precision=precise, preferred_element_type=f32)


def gather_parts(all_ref, zs, zr, xs, xr):
    _, z, x = place()
    zn, rows = all_ref.shape[1], all_ref.shape[2]
    step = rows // PIECES

    def along(p, j):
        part = pl.ds(p * step, step)
        return pltpu.make_async_remote_copy(
            all_ref.at[x, z, part],
            all_ref.at[x, z, part],
            zs.at[p, j - 1],
            zr.at[p, j - 1],
            device_id={"gx": lax.rem(z + j, zn) * 2 + x},
            device_id_type=MESH,
        )

    def across(p, j):
        part = pl.ds(p * step, step)
        t = lax.rem(z - j + zn, zn)
        return pltpu.make_async_remote_copy(
            all_ref.at[x, t, part],
            all_ref.at[x, t, part],
            xs.at[p, j],
            xr.at[p, j],
            device_id={"gx": z * 2 + 1 - x},
            device_id_type=MESH,
        )

    return along, across


def step_body(
    scale, xl, rep,
    f_ref, s_ref, t_ref, mult_ref, kw_ref, xb_ref, zi_ref, yi_ref, kp_ref,
    ty_ref, zt_ref, kpt_ref, xt_ref,
    e_ref, out_ref, sums_ref,
    pre_ref, vel_ref, gv_ref, gp_ref, slab_ref, all_ref, gw_ref, gq_ref, loss_ref,
    edge_ref, halo_ref, zs, zr, xs, xr, us, ur, ps, pr,
    pack_ref, ebuf, es, er, *scatter
):
    i = pl.program_id(0)
    me, z, x = place()
    gx = lax.axis_size("gx")
    zn = gx // 2
    along, across = gather_parts(all_ref, zs, zr, xs, xr)
    right = {"gx": lax.rem(me + 1, gx)}
    left = {"gx": lax.rem(me + gx - 1, gx)}

    def halo(k, sems):
        return pltpu.make_async_remote_copy(
            edge_ref.at[k],
            halo_ref.at[k],
            sems[0].at[k % 2],
            sems[1].at[k % 2],
            device_id=left if k % 2 == 0 else right,
            device_id_type=MESH,
        )

    def penalty(p, before, after):
        u = vel_ref[p, 1], vel_ref[p, 2]
        rows, lanes = u[0].shape
        slope = (after - before) * 0.5
        slope = slope + (pltpu.roll(u[0], rows - 1, 0) - pltpu.roll(u[0], 1, 0)) * 0.5
        slope = slope + (pltpu.roll(u[1], lanes - 1, 1) - pltpu.roll(u[1], 1, 1)) * 0.5
        lam = mult_ref[p].astype(f32) / 64.0
        e_ref[p] = lam + penalty_weight * slope
        add_loss((lam + (0.5 * penalty_weight) * slope) * slope)

    def add_loss(value):
        rows, lanes = value.shape
        loss_ref[...] = loss_ref[...] + jnp.sum(value.reshape(rows // 8, 8, lanes), axis=0)

    @pl.when(i == 0)
    def _():
        all_ref[x, z] = s_ref[...]
        loss_ref[...] = jnp.zeros_like(loss_ref)
        greet(True)
        for p in range(PIECES):
            for j in (2, 1, 3):
                along(p, j).start()
            across(p, 0).start()

    for p in range(PIECES):

        @pl.when(i == ((p + 1) * xl) // PIECES - 1)
        def _(p=p):
            for j in range(1, zn):
                along(p, j).wait_recv()
                across(p, j).start()

    @pl.when(i < xl)
    def _():
        plane_ref = pre_ref.at[pl.ds(i, 1)]
        for y0 in range(0, f_ref.shape[2], 2 * ROWS):
            put_pair(plane_ref, y0, dot(kw_ref[...], tile_pair(f_ref, y0)))

    @pl.when(i == xl)
    def _():
        for p in range(PIECES):
            for j in range(zn):
                across(p, j).wait()
            for j in range(1, zn):
                along(p, j).wait_send()
        x_spread(all_ref, xb_ref, slab_ref)

    @pl.when((i >= xl) & (i < 2 * xl))
    def _():
        m = i - xl
        odd = lax.rem(m, 2)
        p = odd * (xl - 1 - m // 2) + (1 - odd) * (m // 2)
        plane_ref = pre_ref.at[pl.ds(p, 1)]
        modes_ref = slab_ref.at[:, pl.ds(p, 1)]
        middle_body(
            scale, plane_ref, modes_ref, zi_ref, yi_ref, kp_ref, plane_ref,
            vel_ref.at[pl.ds(p, 1)],
        )

    @pl.when(i == xl + 1)
    def _():
        edge_ref[0] = vel_ref[0, 0]
        edge_ref[1] = vel_ref[xl - 1, 0]
        for k in (0, 1):
            halo(k, (us, ur)).start()

    @pl.when(i == xl + xl // 2)
    def _():
        for k in (0, 1):
            halo(k, (us, ur)).wait()
        penalty(0, halo_ref[1], vel_ref[1, 0])
        penalty(xl - 1, vel_ref[xl - 2, 0], halo_ref[0])
        edge_ref[2] = e_ref[0]
        edge_ref[3] = e_ref[xl - 1]
        for k in (2, 3):
            halo(k, (ps, pr)).start()

    @pl.when(i == 2 * xl - 1)
    def _():
        def one(p, carry):
            penalty(p, vel_ref[p - 1, 0], vel_ref[p + 1, 0])
            return carry

        lax.fori_loop(1, xl - 1, one, 0)
        for k in (2, 3):
            halo(k, (ps, pr)).wait()

    @pl.when(i >= 2 * xl)
    def _():
        p = i - 2 * xl
        e = e_ref[p]
        rows, lanes = e.shape
        before = lax.select(
            jnp.broadcast_to(p == 0, e.shape), halo_ref[3], e_ref[lax.rem(p + xl - 1, xl)]
        )
        after = lax.select(
            jnp.broadcast_to(p == xl - 1, e.shape), halo_ref[2], e_ref[lax.rem(p + 1, xl)]
        )
        slopes = (
            (after - before) * 0.5,
            (pltpu.roll(e, rows - 1, 0) - pltpu.roll(e, 1, 0)) * 0.5,
            (pltpu.roll(e, lanes - 1, 1) - pltpu.roll(e, 1, 1)) * 0.5,
        )
        for j in range(3):
            misfit = vel_ref[p, j] - t_ref[0, j].astype(f32)
            add_loss(misfit * misfit)
            gv_ref[0, j] = ((2.0 * misfit - slopes[j]) / rep).astype(bf16)
        backward_body(
            f_ref, pre_ref.at[pl.ds(p, 1)], gv_ref, ty_ref, zt_ref, kpt_ref,
            slab_ref.at[:, pl.ds(p, 1)], gw_ref, gq_ref, gp_ref, first=2 * xl,
        )

    @pl.when(i == pl.num_programs(0) - 1)
    def _():
        x_sum(slab_ref, xt_ref, scatter[0])
        count = f_ref.shape[1]
        lane = lax.broadcasted_iota(jnp.int32, (count, 128), 1)
        pack_ref[...] = (
            fold(gw_ref[...], 0)
            + fold(gq_ref[...], count)
            + jnp.where(lane == count + 3, jnp.sum(loss_ref[...]), 0.0)
        )
        scatter_sum(scatter[0], out_ref, *scatter[1:], extra=(pack_ref, ebuf, es, er))
        sums_ref[...] = pack_ref[...]


def whole(shape):
    return pl.BlockSpec(shape, lambda i: (0,) * len(shape))


def plane(shape):
    return pl.BlockSpec((1,) + tuple(shape), lambda i: (i,) + (0,) * len(shape))


params = pltpu.CompilerParams(
    dimension_semantics=("arbitrary",), vmem_limit_bytes=56 * 1024 * 1024
)


def extended(value, axis_name):
    count = lax.axis_size(axis_name)
    up = [(i, (i + 1) % count) for i in range(count)]
    down = [(j, i) for i, j in up]
    before = lax.ppermute(value[-1:], axis_name, up)
    after = lax.ppermute(value[:1], axis_name, down)
    return jnp.concatenate([before, value, after], axis=0)


def central(values, axis):
    return (jnp.roll(values, -1, axis) - jnp.roll(values, 1, axis)) * 0.5


def local(fields, targets, multipliers, local_weight, proj_weight, spectral_weight):
    gx = lax.axis_size("gx")
    rep = lax.axis_size("rep")
    _, xl, C, NY, NZ = fields.shape
    NX = xl * gx
    PL = MY * MZ // gx
    scale = 1.0 / math.sqrt(NX * NY * NZ)
    fields, targets, multipliers = fields[0], targets[0], multipliers[0]

    cos_y, sin_y = fourier_tables(NY, MY)
    ty = jnp.asarray(np.concatenate([cos_y.T, -sin_y.T], 0).astype(ml_dtypes.bfloat16))
    yi = jnp.asarray(np.concatenate([cos_y, -sin_y], 1).astype(ml_dtypes.bfloat16))
    cos_z, sin_z = fourier_tables(NZ, MZ)
    zt = np.concatenate(
        [np.concatenate([cos_z.T, sin_z.T], 1), np.concatenate([-sin_z.T, cos_z.T], 1)], 0
    )
    direct = gx == 8 and MY % gx == 0 and 128 % (MY // gx * C) == 0
    KY = MY // gx if direct else 0
    PK = 128 // (KY * C) if direct else 1
    HZ = MZ // PK
    order = np.arange(2 * MZ).reshape(2, HZ, PK).transpose(2, 0, 1).reshape(-1)
    zt = zt[order]
    zi_high, zi_low = halves(zt)
    zt = jnp.asarray(np.concatenate([zi_high, zi_low], 0))
    zi = jnp.asarray(np.concatenate([zi_high, zi_low, zi_high], 0))
    cos_x, sin_x = fourier_tables(NX, MX)
    xt = np.stack(
        [np.stack([cos_x.T, sin_x.T], 1), np.stack([-sin_x.T, cos_x.T], 1)], 1
    )
    xt = xt.reshape(MX, 2, 2, gx, xl).transpose((0, 1, 3, 4, 2) if direct else (0, 1, 3, 2, 4))
    xt = xt.reshape(2 * MX, 2 * NX)
    x_forward = jnp.asarray(xt * np.float32(scale))
    x_back = jnp.asarray(np.ascontiguousarray(xt.T))

    def spread(weight):
        rows, columns = weight.shape
        left = jnp.asarray(np.kron(np.eye(rows), np.ones((ROWS, 1))), dtype=bf16)
        right = jnp.asarray(np.kron(np.eye(columns), np.ones((1, ROWS))), dtype=bf16)
        diagonal = jnp.asarray(np.kron(np.ones((rows, columns)), np.eye(ROWS)), dtype=bf16)
        return dot(dot(left, weight).astype(bf16), right).astype(bf16) * diagonal

    kw = spread(local_weight.T)
    kp = spread(proj_weight.T)
    kpt = spread(proj_weight)

    field_spec = plane((C, NY, NZ))
    modes_shape = jax.ShapeDtypeStruct((xl, 2 * MZ, MY * C), f32)
    modes_spec = plane((2 * MZ, MY * C))
    vel_spec = plane((3, NY, NZ))

    def to_owner(slab):
        slab = slab.reshape(xl, 2, MZ, MY, C).transpose(3, 2, 1, 0, 4)
        slab = slab.reshape(gx, PL, 2, xl, C).transpose(0, 2, 3, 1, 4)
        slab = slab.reshape(gx, 2 * xl, PL * C)
        slab = lax.all_to_all(slab, "gx", split_axis=0, concat_axis=0, tiled=True)
        out = jnp.dot(x_forward, slab.reshape(2 * NX, PL * C), precision=precise)
        return out.reshape(MX, 2, PL, C)

    def to_planes(modes):
        out = jnp.dot(x_back, modes.reshape(2 * MX, PL * C), precision=precise)
        out = out.reshape(gx, 2 * xl, PL * C)
        out = lax.all_to_all(out, "gx", split_axis=0, concat_axis=0, tiled=True)
        out = out.reshape(gx, 2, xl, PL, C).transpose(0, 3, 1, 2, 4)
        out = out.reshape(MY, MZ, 2, xl, C).transpose(3, 2, 1, 0, 4)
        return out.reshape(xl, 2 * MZ, MY * C)

    def both_samples(modes):
        part = modes.reshape(rep, MX // rep, 2, PL, C)
        return lax.all_to_all(part, "rep", split_axis=0, concat_axis=0, tiled=True)

    ZN = gx // 2
    QR = HZ * 2 * MX
    slab_scratch = pltpu.VMEM((gx, xl, 2, HZ, 128), f32)
    dma = pltpu.SemaphoreType.DMA

    def comm(number):
        return pltpu.CompilerParams(
            dimension_semantics=("arbitrary",),
            vmem_limit_bytes=60 * 1024 * 1024,
            collective_id=number,
            has_side_effects=True,
        )

    def chunk_modes(chunk):
        out = chunk.reshape(HZ, MX, 2, PK, KY, C).transpose(1, 2, 4, 0, 3, 5)
        return out.reshape(MX, 2, PL, C)

    if direct:
        me = lax.axis_index("gx")
        x_own = lax.dynamic_index_in_dim(x_forward.reshape(2 * MX, gx, 2 * xl), me, 1, False)
        x_out = lax.dynamic_index_in_dim(x_back.reshape(gx, 2 * xl, 2 * MX), me, 0, False)
        slab = pl.pallas_call(
            forward_sum_body,
            grid=(xl,),
            out_shape=jax.ShapeDtypeStruct((QR, 128), f32),
            in_specs=[field_spec, whole(ty.shape), whole(zt.shape), whole(x_own.shape)],
            out_specs=whole((QR, 128)),
            scratch_shapes=[slab_scratch] + scatter_scratch(ZN, QR),
            compiler_params=comm(1),
        )(fields, ty, zt, x_own)
    else:
        slab = pl.pallas_call(
            forward_body,
            grid=(xl,),
            out_shape=modes_shape,
            in_specs=[field_spec, whole(ty.shape), whole(zt.shape)],
            out_specs=modes_spec,
            compiler_params=params,
        )(fields, ty, zt)
        mapped = pl.pallas_call(
            local_body,
            grid=(xl,),
            out_shape=jax.ShapeDtypeStruct((xl, C, NY, NZ), f32),
            in_specs=[field_spec, whole(kw.shape)],
            out_specs=field_spec,
            compiler_params=pltpu.CompilerParams(vmem_limit_bytes=20 * 1024 * 1024),
        )(fields, kw)
    weights = spectral_weight
    weights = weights.transpose(2, 3, 4, 0, 1).reshape(1, 2, C, C, MX // rep * PL)
    weights = lax.all_gather(weights, "rep", axis=0, tiled=True)
    spectrum = chunk_modes(slab) if direct else to_owner(slab)
    KX = MX // rep
    turned = spectrum.reshape(rep, KX, 2, PL, C).transpose(0, 2, 4, 1, 3)
    turned = turned.reshape(rep, 2, 1, C, KX * PL)
    w_re, w_im = weights[:, 0].astype(f32), weights[:, 1].astype(f32)
    s_re, s_im = turned[:, 0], turned[:, 1]
    product = jnp.stack(
        [jnp.sum(w_re * s_re - w_im * s_im, axis=2), jnp.sum(w_re * s_im + w_im * s_re, axis=2)],
        axis=1,
    )
    product = product.reshape(rep, 2, C, KX, PL).transpose(0, 3, 1, 4, 2)
    product = product.reshape(MX, 2, PL, C)
    spectra = both_samples(spectrum)
    middle_shape = (
        jax.ShapeDtypeStruct((xl, C, NY, NZ), f32),
        jax.ShapeDtypeStruct((xl, 3, NY, NZ), f32),
    )
    wide = C * ROWS
    if direct:
        part = product.reshape(MX, 2, KY, HZ, PK, C).transpose(3, 0, 1, 4, 2, 5)
        part = part.reshape(QR, 128)
        tables = [kw, x_out, zi, yi, kp, ty, zt, kpt, x_own]

        def once(shape):
            return pl.BlockSpec(
                shape, lambda i: (0,) * len(shape), pipeline_mode=pl.Buffered(1)
            )

        penalty, chunk, sums = pl.pallas_call(
            functools.partial(step_body, scale, xl, rep),
            grid=(3 * xl,),
            out_shape=(
                jax.ShapeDtypeStruct((xl, NY, NZ), f32),
                jax.ShapeDtypeStruct((QR, 128), f32),
                jax.ShapeDtypeStruct((C, 128), f32),
            ),
            in_specs=[
                pl.BlockSpec(
                    (1, C, NY, NZ),
                    lambda i: ((i % xl) * ((i // xl + 1) % 2), 0, 0, 0),
                ),
                once((QR, 128)),
                pl.BlockSpec((1, 3, NY, NZ), lambda i: ((i % xl) * (i // (2 * xl)), 0, 0, 0)),
                once((xl, NY, NZ)),
            ]
            + [once(t.shape) for t in tables],
            out_specs=(whole((xl, NY, NZ)), whole((QR, 128)), whole((C, 128))),
            scratch_shapes=[
                pltpu.VMEM((xl, C, NY, NZ), f32),
                pltpu.VMEM((xl, 3, NY, NZ), f32),
                pltpu.VMEM((1, 3, NY, NZ), bf16),
                pltpu.VMEM((1, C, NY, NZ), bf16),
                slab_scratch,
                pltpu.VMEM((2, ZN, QR, 128), f32),
                pltpu.VMEM((wide, wide), f32),
                pltpu.VMEM((wide, 3 * ROWS), f32),
                pltpu.VMEM((8, NZ), f32),
                pltpu.VMEM((4, NY, NZ), f32),
                pltpu.VMEM((4, NY, NZ), f32),
            ]
            + [dma((PIECES, ZN - 1))] * 2
            + [dma((PIECES, ZN))] * 2
            + [dma((2,))] * 4
            + [pltpu.VMEM((C, 128), f32), pltpu.VMEM((ZN, C, 128), f32), dma((ZN,)), dma((ZN,))]
            + scatter_scratch(ZN, QR),
            compiler_params=comm(2),
        )(fields, part, targets, multipliers, *tables)
        grads = chunk_modes(chunk)
        both = jnp.concatenate(
            [grads.reshape(rep, -1), jnp.broadcast_to(sums.reshape(1, -1), (rep, sums.size))],
            axis=1,
        )
        both = lax.all_to_all(both, "rep", split_axis=0, concat_axis=0, tiled=True)
        size = grads.size // rep
        grads = both[:, :size].reshape(rep, MX // rep, 2, PL, C)
        sums = jnp.sum(both[:, size:], axis=0).reshape(C, 128)
        grad_w, grad_q, loss = sums[:, :C], sums[:, C : C + 3], sums[0, C + 3 : C + 4]
    else:
        wave = to_planes(product)
        pre, velocity = pl.pallas_call(
            functools.partial(middle_body, scale),
            grid=(xl,),
            out_shape=middle_shape,
            in_specs=[field_spec, modes_spec, whole(zi.shape), whole(yi.shape), whole(kp.shape)],
            out_specs=(field_spec, vel_spec),
            compiler_params=params,
        )(mapped, wave, zi, yi, kp)
        padded = extended(velocity[:, 0].astype(bf16), "gx").astype(f32)
        slope_x = (padded[2:] - padded[:-2]) * 0.5
        divergence = slope_x + central(velocity[:, 1], 1) + central(velocity[:, 2], 2)
        lam = multipliers.astype(f32) / 64.0
        penalty = lam + penalty_weight * divergence
        misfit = velocity - targets.astype(f32)
        loss_sum = (
            jnp.sum(misfit * misfit)
            + jnp.sum(lam * divergence)
            + 0.5 * penalty_weight * jnp.sum(divergence * divergence)
        )
        padded = extended(penalty.astype(bf16), "gx").astype(f32)
        pen_x = (padded[2:] - padded[:-2]) * 0.5
        slopes = jnp.stack([pen_x, central(penalty, 1), central(penalty, 2)], axis=1)
        grad_vel = ((2.0 * misfit - slopes) / rep).astype(bf16)
        grad_slab, gw, gq = pl.pallas_call(
            backward_body,
            grid=(xl,),
            out_shape=(
                modes_shape,
                jax.ShapeDtypeStruct((wide, wide), f32),
                jax.ShapeDtypeStruct((wide, 3 * ROWS), f32),
            ),
            in_specs=[field_spec, field_spec, vel_spec]
            + [whole(ty.shape), whole(zt.shape), whole(kpt.shape)],
            out_specs=(modes_spec, whole((wide, wide)), whole((wide, 3 * ROWS))),
            scratch_shapes=[pltpu.VMEM((1, C, NY, NZ), bf16)],
            compiler_params=params,
        )(fields, pre, grad_vel, ty, zt, kpt)
        gather = jnp.asarray(np.kron(np.eye(C), np.ones((1, ROWS))).astype(np.float32))
        gather_q = jnp.asarray(np.kron(np.eye(3), np.ones((ROWS, 1))).astype(np.float32))
        mask = jnp.asarray(np.kron(np.ones((C, C)), np.eye(ROWS)).astype(np.float32))
        mask_q = jnp.asarray(np.kron(np.ones((C, 3)), np.eye(ROWS)).astype(np.float32))
        grad_w = jnp.dot(gather, gw * mask, precision=precise)
        grad_w = jnp.dot(grad_w, gather.T, precision=precise)
        grad_q = jnp.dot(gather, gq * mask_q, precision=precise)
        grad_q = jnp.dot(grad_q, gather_q, precision=precise)
        grads = both_samples(to_owner(grad_slab))
        packed = jnp.concatenate([grad_w.reshape(-1), grad_q.reshape(-1), loss_sum.reshape(1)])
        packed = lax.psum(packed, ("gx", "rep"))
        grad_w = packed[: C * C].reshape(C, C)
        grad_q = packed[C * C : C * C + 3 * C].reshape(C, 3)
        loss = packed[-1:]
    loss = loss / (rep * NX * NY * NZ)

    g_re, g_im = grads[:, :, 0], grads[:, :, 1]
    across = jnp.stack([jnp.stack([g_re, g_im], 3), jnp.stack([g_im, -g_re], 3)], 1)
    terms = [
        across[b, t][..., None] * spectra[b, :, t][:, :, None, None, :]
        for b in range(rep)
        for t in range(2)
    ]
    grad_r = sum(terms[1:], terms[0])
    return (penalty[None], grad_r, grad_w * scale, grad_q * scale, loss)


def solution(mesh):
    in_specs = (
        P(("grp", "rep"), "gx", None, None, None),
        P(("grp", "rep"), "gx", None, None, None),
        P(("grp", "rep"), "gx", None, None),
        P(),
        P(),
        P("rep", "gx", None, None, None),
    )
    out_specs = (
        P(("grp", "rep"), "gx", None, None),
        P(("grp", "rep"), "gx", None, None, None),
        P("grp", None),
        P("grp", None),
        P("grp"),
    )
    return jax.shard_map(local, mesh=mesh, in_specs=in_specs, out_specs=out_specs, check_vma=False)
```

```python
import functools
import math

import jax
import jax.numpy as jnp
import ml_dtypes
import numpy as np
from jax import lax
from jax.experimental import pallas as pl
from jax.experimental.pallas import tpu as pltpu
from jax.sharding import PartitionSpec as P

MX = 16
MY = 16
MZ = 16
ROWS = 16

penalty_weight = 0.5
precise = lax.Precision.HIGHEST
bf16 = jnp.bfloat16
f32 = jnp.float32
ROOT = math.sqrt(2.0 / math.pi)


def fourier_tables(length, count):
    position = np.arange(count)
    modes = np.where(position < count // 2, position, position - count)
    phase = np.mod(np.arange(length)[:, None] * modes[None, :], length)
    angle = phase.astype(np.float32) * np.float32(2.0 * math.pi / length)
    return np.cos(angle), np.sin(angle)


def halves(table):
    high = table.astype(ml_dtypes.bfloat16)
    low = (table - high.astype(np.float32)).astype(ml_dtypes.bfloat16)
    return high, low


def split(value):
    high = value.astype(bf16)
    return high, (value - high.astype(f32)).astype(bf16)


def dot(a, b):
    return jnp.dot(a, b, preferred_element_type=f32)


def dot_nt(a, b):
    return lax.dot_general(a, b, (((1,), (1,)), ((), ())), preferred_element_type=f32)


def dot_tn(a, b):
    return lax.dot_general(a, b, (((0,), (0,)), ((), ())), preferred_element_type=f32)


def plane_modes(load, count, ty, zt):
    parts = []
    for c in range(0, count, 2):
        pair = dot(ty, jnp.concatenate([load(c), load(c + 1)], axis=1))
        nz = pair.shape[1] // 2
        parts += [pair[:, :nz], pair[:, nz:]]
    turned = jnp.swapaxes(jnp.stack(parts, axis=0), 0, 1)
    real = turned[:MY].reshape(MY * count, nz)
    imag = turned[MY:].reshape(MY * count, nz)
    high, low = split(jnp.concatenate([real, imag], axis=1))
    both = dot_nt(zt, high)
    n = 2 * MZ
    return both[:n] + both[n:] + dot_nt(zt[:n], low)


def store_modes(out_ref, modes):
    if len(out_ref.shape) == 3:
        out_ref[0] = modes
        return
    owners, _, _, high, lanes = out_ref.shape
    width = modes.shape[1] // owners
    rows = 2 * high
    for d in range(owners):
        parts = [
            modes[j * rows : (j + 1) * rows, d * width : (d + 1) * width]
            for j in range(lanes // width)
        ]
        out_ref[d, 0] = jnp.concatenate(parts, axis=1).reshape(2, high, lanes)


def load_modes(m_ref, columns):
    if len(m_ref.shape) == 3:
        return m_ref[0]
    owners, _, _, high, lanes = m_ref.shape
    width = columns // owners
    blocks = [m_ref[d, 0].reshape(2 * high, lanes) for d in range(owners)]
    rows = [
        jnp.concatenate([block[:, j * width : (j + 1) * width] for block in blocks], axis=1)
        for j in range(lanes // width)
    ]
    return jnp.concatenate(rows, axis=0)


def forward_body(f_ref, ty_ref, zt_ref, out_ref):
    count = f_ref.shape[1]
    store_modes(out_ref, plane_modes(lambda c: f_ref[0, c], count, ty_ref[...], zt_ref[...]))


MESH = pl.DeviceIdType.MESH
PIECES = 4


def place():
    me = lax.axis_index("gx")
    return me, me // 2, lax.rem(me, 2)


def pair():
    r = lax.axis_index("rep")
    return r * lax.axis_size("gx") + lax.axis_index("gx"), {"rep": 1 - r}


def greet(ring=False, core=False):
    _, z, x = place()
    zn = lax.axis_size("gx") // 2
    barrier = pltpu.get_barrier_semaphore()
    pl.semaphore_signal(barrier, inc=1, device_id={"gx": z * 2 + 1 - x}, device_id_type=MESH)
    for j in range(1, zn):
        t = lax.rem(z + j, zn)
        pl.semaphore_signal(barrier, inc=1, device_id={"gx": t * 2 + x}, device_id_type=MESH)
    if ring:
        me = z * 2 + x
        t = lax.rem(me + 2 * x - 1 + 2 * zn, 2 * zn)
        pl.semaphore_signal(barrier, inc=1, device_id={"gx": t}, device_id_type=MESH)
    if core:
        pl.semaphore_signal(barrier, inc=1, device_id=pair()[1], device_id_type=MESH)
    pl.semaphore_wait(barrier, zn + (1 if ring else 0) + (1 if core else 0))


def send(src, dst, sems, where):
    copy = pltpu.make_async_remote_copy(
        src, dst, sems[0], sems[1], device_id=where, device_id_type=MESH
    )
    copy.start()
    return copy


def scatter_sum(a_ref, o_ref, xbuf, sbuf, zbuf, xs, xr, zs, zr, extra=None):
    _, z, x = place()
    zn, rows = a_ref.shape[1], a_ref.shape[2]
    step = rows // PIECES
    to_x = {"gx": z * 2 + 1 - x}
    first, second = [], []
    if extra is not None:
        e_ref, ebuf, es, er = extra
        swap = send(e_ref, ebuf.at[0], (es.at[0], er.at[0]), to_x)
    for p in range(PIECES):
        part = pl.ds(p * step, step)
        first.append(send(a_ref.at[1 - x, :, part], xbuf.at[p], (xs.at[p], xr.at[p]), to_x))
    if extra is not None:
        swap.wait()
        e_ref[...] = e_ref[...] + ebuf[0]
        spread = [
            send(e_ref, ebuf.at[j], (es.at[j], er.at[j]), {"gx": lax.rem(z + j, zn) * 2 + x})
            for j in range(1, zn)
        ]
    for p in range(PIECES):
        part = pl.ds(p * step, step)
        first[p].wait_recv()
        for j in (2, 1, 3):
            t = lax.rem(z + j, zn)
            sbuf[p, j - 1] = a_ref[x, t, part] + xbuf[p, t]
            copy = send(
                sbuf.at[p, j - 1],
                zbuf.at[p, j - 1],
                (zs.at[p, j - 1], zr.at[p, j - 1]),
                {"gx": t * 2 + x},
            )
            second.append((p, copy))
        o_ref[part] = a_ref[x, z, part] + xbuf[p, z]
    for p in range(PIECES):
        part = pl.ds(p * step, step)
        for q, copy in second:
            if q == p:
                copy.wait_recv()
        o_ref[part] = o_ref[part] + ((zbuf[p, 0] + zbuf[p, 1]) + zbuf[p, 2])
    for copy in first + [copy for _, copy in second]:
        copy.wait_send()
    if extra is not None:
        for copy in spread:
            copy.wait()
        e_ref[...] = (e_ref[...] + ebuf[1]) + (ebuf[2] + ebuf[3])


def scatter_scratch(zn, rows):
    step = rows // PIECES
    dma = pltpu.SemaphoreType.DMA
    return [
        pltpu.VMEM((2, zn, rows, 128), f32),
        pltpu.VMEM((PIECES, zn, step, 128), f32),
        pltpu.VMEM((PIECES, zn - 1, step, 128), f32),
        pltpu.VMEM((PIECES, zn - 1, step, 128), f32),
        dma((PIECES,)),
        dma((PIECES,)),
        dma((PIECES, zn - 1)),
        dma((PIECES, zn - 1)),
    ]


def x_sum(slab_ref, table_ref, a_ref):
    owners, xl, _, high, lanes = slab_ref.shape
    rows = table_ref.shape[0]
    for d in range(owners):
        turned = jnp.swapaxes(slab_ref[d].reshape(2 * xl, high, lanes), 0, 1)
        for k in range(high):
            a_ref[d % 2, d // 2, k * rows : (k + 1) * rows] = jnp.dot(
                table_ref[...], turned[k], precision=precise, preferred_element_type=f32
            )


def x_spread(all_ref, table_ref, slab_ref):
    owners, xl, _, high, lanes = slab_ref.shape
    rows = table_ref.shape[1]
    for d in range(owners):
        parts = [
            jnp.dot(
                table_ref[...],
                all_ref[d % 2, d // 2, k * rows : (k + 1) * rows],
                precision=precise,
                preferred_element_type=f32,
            )
            for k in range(high)
        ]
        turned = jnp.swapaxes(jnp.stack(parts, axis=0), 0, 1)
        slab_ref[d] = turned.reshape(xl, 2, high, lanes)


def spread_weight(weight, turned):
    rows, cols = weight.shape[::-1] if turned else weight.shape

    def match(shape, low, high):
        a = lax.broadcasted_iota(jnp.int32, shape, 0)
        b = lax.broadcasted_iota(jnp.int32, shape, 1)
        return low(a) == high(b)

    tall = match((rows * ROWS, rows), lambda a: a // ROWS, lambda b: b)
    wide = match((cols, cols * ROWS), lambda a: a, lambda b: b // ROWS)
    tall = jnp.where(tall, 1.0, 0.0).astype(bf16)
    wide = jnp.where(wide, 1.0, 0.0).astype(bf16)
    half = (dot_nt if turned else dot)(tall, weight).astype(bf16)
    diagonal = match((rows * ROWS, cols * ROWS), lambda a: a % ROWS, lambda b: b % ROWS)
    return jnp.where(diagonal, dot(half, wide), 0.0).astype(bf16)


def multiply(chunk_ref, weights, in_ref, res_ref, out_ref):
    steps, high, lanes = in_ref.shape
    KX, PL, _, _, C = weights[0].shape
    KY, PK = PL // MZ, MZ // high
    in_ref[...] = jnp.swapaxes(chunk_ref[...].reshape(high, steps, lanes), 0, 1)
    row = lax.broadcasted_iota(jnp.int32, (high, lanes), 0)
    lane = lax.broadcasted_iota(jnp.int32, (high, lanes), 1)
    low = (lane // C) % 2 == 0

    for half, w_ref in enumerate(weights):

        def one(k, carry, half=half, w_ref=w_ref):
            at = 2 * (half * KX + k)
            rest = in_ref[pl.ds(at, 2)]
            pieces = []
            for _ in range(3):
                pieces.append(rest.astype(bf16).astype(f32))
                rest = rest - pieces[-1]
            results = []
            for ky in range(KY):
                rows = [
                    piece[ri][:, (pk * KY + ky) * C : (pk * KY + ky + 1) * C]
                    for piece in pieces
                    for ri in range(2)
                    for pk in range(PK)
                ]
                w = w_ref[k, ky * MZ : (ky + 1) * MZ].reshape(MZ * 2 * C, C)
                terms = dot_nt(jnp.concatenate(rows, axis=0).astype(bf16), w)
                terms = terms.reshape(3, 2, PK, high, MZ * 2 * C)
                terms = (terms[2] + terms[1]) + terms[0]
                kept = []
                for ri in range(2):
                    value = None
                    for h in range(high):
                        own = slice(h * lanes, (h + 1) * lanes)
                        here = jnp.where(
                            lane < 2 * C, terms[ri, 0][:, own], terms[ri, 1][:, own]
                        )
                        value = here if value is None else jnp.where(row == h, here, value)
                    kept.append(value)
                real, imag = kept
                imag = jnp.where(low, -pltpu.roll(imag, lanes - C, 1), pltpu.roll(imag, C, 1))
                results.append(real + imag)
            one_, two = results
            res_ref[at] = jnp.where(low, one_, pltpu.roll(two, C, 1))
            res_ref[at + 1] = jnp.where(low, pltpu.roll(one_, lanes - C, 1), two)
            return carry

        lax.fori_loop(0, KX, one, 0)
    out_ref[...] = jnp.swapaxes(res_ref[...], 0, 1).reshape(out_ref.shape)


def forward_sum_body(
    f_ref, ty_ref, zt_ref, xt_ref, w_ref,
    out_ref, prod_ref,
    slab_ref, wown_ref, woth_ref, in_ref, res_ref, own_sem, ws, wr, *scatter
):
    i = pl.program_id(0)
    count = f_ref.shape[1]
    table, core = pair()
    fetch = pltpu.make_async_copy(w_ref, wown_ref, own_sem)
    swap = pltpu.make_async_remote_copy(
        w_ref, woth_ref, ws, wr, device_id=core, device_id_type=MESH
    )

    @pl.when(i == 0)
    def _():
        greet(core=True)
        fetch.start()
        swap.start()

    store_modes(
        slab_ref.at[:, pl.ds(i, 1)],
        plane_modes(lambda c: f_ref[0, c], count, ty_ref[...], zt_ref[...]),
    )

    @pl.when(i == pl.num_programs(0) - 1)
    def _():
        x_sum(slab_ref, xt_ref.at[table], scatter[0])
        scatter_sum(scatter[0], out_ref, *scatter[1:])
        fetch.wait()
        swap.wait()
        multiply(out_ref, (wown_ref, woth_ref), in_ref, res_ref, prod_ref)


def grad_body(
    scale, cells, s_ref, g_ref, sums_ref,
    out_ref, gw_ref, gq_ref, loss_ref,
    buf_ref, got_ref, other_ref, ss, rs
):
    i = pl.program_id(0)
    _, PL, _, C, _ = out_ref.shape
    half, high, lanes = buf_ref.shape[2:]
    KY, PK = PL // MZ, MZ // high
    _, core = pair()

    @pl.when(i == 0)
    def _():
        barrier = pltpu.get_barrier_semaphore()
        pl.semaphore_signal(barrier, inc=1, device_id=core, device_id_type=MESH)
        for n, ref in enumerate((s_ref, g_ref)):
            turned = jnp.swapaxes(ref[...].reshape(high, 2 * half, lanes), 0, 1)
            buf_ref[n, 0] = turned[:half]
            buf_ref[n, 1] = turned[half:]
        pl.semaphore_wait(barrier, 1)
        copies = [
            send(buf_ref.at[n, 1], got_ref.at[n], (ss.at[n], rs.at[n]), core) for n in range(2)
        ] + [send(sums_ref, other_ref, (ss.at[2], rs.at[2]), core)]
        for copy in copies:
            copy.wait()
        total = sums_ref[...] + other_ref[...]
        gw_ref[...] = total[:, :C] * scale
        gq_ref[...] = total[:, C : C + 3] * scale
        loss_ref[...] = total[:1, C + 3 : C + 4] * (1.0 / cells)

    def both(n):
        at = pl.ds(2 * i, 2)
        value = jnp.stack([buf_ref[n, 0, at], got_ref[n, at]], axis=0)
        return value.reshape(4 * high, lanes)

    field = both(0)
    turned = both(1).T
    for pk in range(PK):
        for ky in range(KY):
            at = (pk * KY + ky) * C
            for h in range(high):
                f = [field[t * high + h : t * high + h + 1, at : at + C] for t in range(4)]
                g = [turned[at : at + C, t * high + h : t * high + h + 1] for t in range(4)]
                p = ky * MZ + h * PK + pk
                out_ref[0, p, 0] = (g[0] * f[0] + g[1] * f[1]) + (g[2] * f[2] + g[3] * f[3])
                out_ref[0, p, 1] = (g[1] * f[0] - g[0] * f[1]) + (g[3] * f[2] - g[2] * f[3])


def tile_pair(ref, y0):
    count, nz = ref.shape[1], ref.shape[3]
    one = ref[0, :, pl.ds(y0, ROWS), :].reshape(count * ROWS, nz)
    two = ref[0, :, pl.ds(y0 + ROWS, ROWS), :].reshape(count * ROWS, nz)
    return jnp.concatenate([one, two], axis=1)


def put_pair(ref, y0, value):
    count, nz = ref.shape[1], ref.shape[3]
    ref[0, :, pl.ds(y0, ROWS), :] = value[:, :nz].reshape(count, ROWS, nz)
    ref[0, :, pl.ds(y0 + ROWS, ROWS), :] = value[:, nz:].reshape(count, ROWS, nz)


def local_body(f_ref, kw_ref, out_ref):
    for y0 in range(0, f_ref.shape[2], 2 * ROWS):
        put_pair(out_ref, y0, dot(kw_ref[...], tile_pair(f_ref, y0)))


def middle_body(scale, l_ref, m_ref, zi_ref, yi_ref, kp_ref, pre_ref, vel_ref):
    count, ny, nz = l_ref.shape[1], l_ref.shape[2], l_ref.shape[3]
    high, low = split(load_modes(m_ref, MY * count))
    wave = dot_tn(jnp.concatenate([high, high, low], axis=0), zi_ref[...])
    turned = jnp.swapaxes(wave.reshape(MY, count, 2 * nz), 0, 1)
    yi = yi_ref[...]
    for o in range(0, count, 2):
        pair = [
            jnp.concatenate([turned[i, :, :nz], turned[i, :, nz:]], axis=0) for i in (o, o + 1)
        ]
        both = dot(yi, jnp.concatenate(pair, axis=1).astype(bf16))
        pre_ref[0, o] = l_ref[0, o] + both[:, :nz] * scale
        pre_ref[0, o + 1] = l_ref[0, o + 1] + both[:, nz:] * scale

    for y0 in range(0, ny, 2 * ROWS):
        x = tile_pair(pre_ref, y0)
        t = jnp.tanh(x * (ROOT + (0.044715 * ROOT) * (x * x)))
        half = 0.5 * x
        hidden = (half + half * t).astype(bf16)
        put_pair(vel_ref, y0, dot(kp_ref[...], hidden))


def backward_body(
    f_ref, pre_ref, gv_ref, ty_ref, zt_ref, kpt_ref, out_ref, gw_ref, gq_ref, gp_ref, first=0
):
    count, ny, nz = f_ref.shape[1], f_ref.shape[2], f_ref.shape[3]

    @pl.when(pl.program_id(0) == first)
    def _():
        gw_ref[...] = jnp.zeros_like(gw_ref)
        gq_ref[...] = jnp.zeros_like(gq_ref)

    hiddens, grads, fields, slopes = [], [], [], []
    for y0 in range(0, ny, 2 * ROWS):
        gv = tile_pair(gv_ref, y0)
        x = tile_pair(pre_ref, y0)
        cubic = (0.044715 * ROOT) * (x * x)
        t = jnp.tanh(x * (ROOT + cubic))
        cdf = 0.5 + 0.5 * t
        hidden = (x * cdf).astype(bf16)
        slope = cdf + (x * (ROOT + 3.0 * cubic)) * (0.5 - 0.5 * (t * t))
        gp = (dot(kpt_ref[...], gv) * slope).astype(bf16)
        put_pair(gp_ref, y0, gp)
        hiddens.append(hidden)
        grads.append(gp)
        slopes.append(gv)
        fields.append(tile_pair(f_ref, y0))
    gw_ref[...] += dot_nt(jnp.concatenate(fields, axis=1), jnp.concatenate(grads, axis=1))
    gq_ref[...] += dot_nt(jnp.concatenate(hiddens, axis=1), jnp.concatenate(slopes, axis=1))

    store_modes(out_ref, plane_modes(lambda c: gp_ref[0, c], count, ty_ref[...], zt_ref[...]))


def fold(total, columns):
    rows, cols = total.shape
    row = lax.broadcasted_iota(jnp.int32, total.shape, 0) % ROWS
    col = lax.broadcasted_iota(jnp.int32, total.shape, 1) % ROWS
    kept = jnp.where(row == col, total, 0.0).reshape(rows // ROWS, ROWS, cols)
    lane = lax.broadcasted_iota(jnp.int32, (cols, 128), 1)
    block = lax.broadcasted_iota(jnp.int32, (cols, 128), 0) // ROWS
    gather = jnp.where(lane == block + columns, 1.0, 0.0)
    return jnp.dot(jnp.sum(kept, axis=1), gather, precision=precise, preferred_element_type=f32)


def gather_parts(all_ref, zs, zr, xs, xr):
    _, z, x = place()
    zn, rows = all_ref.shape[1], all_ref.shape[2]
    step = rows // PIECES

    def along(p, j):
        part = pl.ds(p * step, step)
        return pltpu.make_async_remote_copy(
            all_ref.at[x, z, part],
            all_ref.at[x, z, part],
            zs.at[p, j - 1],
            zr.at[p, j - 1],
            device_id={"gx": lax.rem(z + j, zn) * 2 + x},
            device_id_type=MESH,
        )

    def across(p, j):
        part = pl.ds(p * step, step)
        t = lax.rem(z - j + zn, zn)
        return pltpu.make_async_remote_copy(
            all_ref.at[x, t, part],
            all_ref.at[x, t, part],
            xs.at[p, j],
            xr.at[p, j],
            device_id={"gx": z * 2 + 1 - x},
            device_id_type=MESH,
        )

    return along, across


def step_body(
    scale, xl, rep,
    f_ref, s_ref, t_ref, mult_ref, lw_ref, pw_ref, xb_ref, zi_ref, yi_ref,
    ty_ref, zt_ref, xt_ref,
    e_ref, out_ref, sums_ref,
    kw_ref, kp_ref, kpt_ref,
    pre_ref, vel_ref, gv_ref, gp_ref, slab_ref, all_ref, gw_ref, gq_ref, loss_ref,
    edge_ref, halo_ref, zs, zr, xs, xr, us, ur, ps, pr,
    pack_ref, ebuf, es, er, *scatter
):
    i = pl.program_id(0)
    me, z, x = place()
    table, _ = pair()
    gx = lax.axis_size("gx")
    zn = gx // 2
    along, across = gather_parts(all_ref, zs, zr, xs, xr)
    right = {"gx": lax.rem(me + 1, gx)}
    left = {"gx": lax.rem(me + gx - 1, gx)}

    def halo(k, sems):
        return pltpu.make_async_remote_copy(
            edge_ref.at[k],
            halo_ref.at[k],
            sems[0].at[k % 2],
            sems[1].at[k % 2],
            device_id=left if k % 2 == 0 else right,
            device_id_type=MESH,
        )

    def penalty(p, before, after):
        u = vel_ref[p, 1], vel_ref[p, 2]
        rows, lanes = u[0].shape
        slope = (after - before) * 0.5
        slope = slope + (pltpu.roll(u[0], rows - 1, 0) - pltpu.roll(u[0], 1, 0)) * 0.5
        slope = slope + (pltpu.roll(u[1], lanes - 1, 1) - pltpu.roll(u[1], 1, 1)) * 0.5
        lam = mult_ref[p].astype(f32) / 64.0
        e_ref[p] = lam + penalty_weight * slope
        add_loss((lam + (0.5 * penalty_weight) * slope) * slope)

    def add_loss(value):
        rows, lanes = value.shape
        loss_ref[...] = loss_ref[...] + jnp.sum(value.reshape(rows // 8, 8, lanes), axis=0)

    @pl.when(i == 0)
    def _():
        all_ref[x, z] = s_ref[...]
        loss_ref[...] = jnp.zeros_like(loss_ref)
        greet(True)
        for p in range(PIECES):
            for j in (2, 1, 3):
                along(p, j).start()
            across(p, 0).start()
        kw_ref[...] = spread_weight(lw_ref[...], True)
        kp_ref[...] = spread_weight(pw_ref[...], True)
        kpt_ref[...] = spread_weight(pw_ref[...], False)

    for p in range(PIECES):

        @pl.when(i == ((p + 1) * xl) // PIECES - 1)
        def _(p=p):
            for j in range(1, zn):
                along(p, j).wait_recv()
                across(p, j).start()

    @pl.when(i < xl)
    def _():
        plane_ref = pre_ref.at[pl.ds(i, 1)]
        for y0 in range(0, f_ref.shape[2], 2 * ROWS):
            put_pair(plane_ref, y0, dot(kw_ref[...], tile_pair(f_ref, y0)))

    @pl.when(i == xl)
    def _():
        for p in range(PIECES):
            for j in range(zn):
                across(p, j).wait()
            for j in range(1, zn):
                along(p, j).wait_send()
        x_spread(all_ref, xb_ref.at[table], slab_ref)

    @pl.when((i >= xl) & (i < 2 * xl))
    def _():
        m = i - xl
        odd = lax.rem(m, 2)
        p = odd * (xl - 1 - m // 2) + (1 - odd) * (m // 2)
        plane_ref = pre_ref.at[pl.ds(p, 1)]
        modes_ref = slab_ref.at[:, pl.ds(p, 1)]
        middle_body(
            scale, plane_ref, modes_ref, zi_ref, yi_ref, kp_ref, plane_ref,
            vel_ref.at[pl.ds(p, 1)],
        )

    @pl.when(i == xl + 1)
    def _():
        edge_ref[0] = vel_ref[0, 0]
        edge_ref[1] = vel_ref[xl - 1, 0]
        for k in (0, 1):
            halo(k, (us, ur)).start()

    @pl.when(i == xl + xl // 2)
    def _():
        for k in (0, 1):
            halo(k, (us, ur)).wait()
        penalty(0, halo_ref[1], vel_ref[1, 0])
        penalty(xl - 1, vel_ref[xl - 2, 0], halo_ref[0])
        edge_ref[2] = e_ref[0]
        edge_ref[3] = e_ref[xl - 1]
        for k in (2, 3):
            halo(k, (ps, pr)).start()

    @pl.when(i == 2 * xl - 1)
    def _():
        def one(p, carry):
            penalty(p, vel_ref[p - 1, 0], vel_ref[p + 1, 0])
            return carry

        lax.fori_loop(1, xl - 1, one, 0)
        for k in (2, 3):
            halo(k, (ps, pr)).wait()

    @pl.when(i >= 2 * xl)
    def _():
        p = i - 2 * xl
        e = e_ref[p]
        rows, lanes = e.shape
        before = lax.select(
            jnp.broadcast_to(p == 0, e.shape), halo_ref[3], e_ref[lax.rem(p + xl - 1, xl)]
        )
        after = lax.select(
            jnp.broadcast_to(p == xl - 1, e.shape), halo_ref[2], e_ref[lax.rem(p + 1, xl)]
        )
        slopes = (
            (after - before) * 0.5,
            (pltpu.roll(e, rows - 1, 0) - pltpu.roll(e, 1, 0)) * 0.5,
            (pltpu.roll(e, lanes - 1, 1) - pltpu.roll(e, 1, 1)) * 0.5,
        )
        for j in range(3):
            misfit = vel_ref[p, j] - t_ref[0, j].astype(f32)
            add_loss(misfit * misfit)
            gv_ref[0, j] = ((2.0 * misfit - slopes[j]) / rep).astype(bf16)
        backward_body(
            f_ref, pre_ref.at[pl.ds(p, 1)], gv_ref, ty_ref, zt_ref, kpt_ref,
            slab_ref.at[:, pl.ds(p, 1)], gw_ref, gq_ref, gp_ref, first=2 * xl,
        )

    @pl.when(i == pl.num_programs(0) - 1)
    def _():
        x_sum(slab_ref, xt_ref.at[table], scatter[0])
        count = f_ref.shape[1]
        lane = lax.broadcasted_iota(jnp.int32, (count, 128), 1)
        pack_ref[...] = (
            fold(gw_ref[...], 0)
            + fold(gq_ref[...], count)
            + jnp.where(lane == count + 3, jnp.sum(loss_ref[...]), 0.0)
        )
        scatter_sum(scatter[0], out_ref, *scatter[1:], extra=(pack_ref, ebuf, es, er))
        sums_ref[...] = pack_ref[...]


def whole(shape):
    return pl.BlockSpec(shape, lambda i: (0,) * len(shape))


def plane(shape):
    return pl.BlockSpec((1,) + tuple(shape), lambda i: (i,) + (0,) * len(shape))


params = pltpu.CompilerParams(
    dimension_semantics=("arbitrary",), vmem_limit_bytes=56 * 1024 * 1024
)


def extended(value, axis_name):
    count = lax.axis_size(axis_name)
    up = [(i, (i + 1) % count) for i in range(count)]
    down = [(j, i) for i, j in up]
    before = lax.ppermute(value[-1:], axis_name, up)
    after = lax.ppermute(value[:1], axis_name, down)
    return jnp.concatenate([before, value, after], axis=0)


def central(values, axis):
    return (jnp.roll(values, -1, axis) - jnp.roll(values, 1, axis)) * 0.5


def local(fields, targets, multipliers, local_weight, proj_weight, spectral_weight):
    gx = lax.axis_size("gx")
    rep = lax.axis_size("rep")
    _, xl, C, NY, NZ = fields.shape
    NX = xl * gx
    PL = MY * MZ // gx
    scale = 1.0 / math.sqrt(NX * NY * NZ)
    fields, targets, multipliers = fields[0], targets[0], multipliers[0]

    cos_y, sin_y = fourier_tables(NY, MY)
    ty = jnp.asarray(np.concatenate([cos_y.T, -sin_y.T], 0).astype(ml_dtypes.bfloat16))
    yi = jnp.asarray(np.concatenate([cos_y, -sin_y], 1).astype(ml_dtypes.bfloat16))
    cos_z, sin_z = fourier_tables(NZ, MZ)
    zt = np.concatenate(
        [np.concatenate([cos_z.T, sin_z.T], 1), np.concatenate([-sin_z.T, cos_z.T], 1)], 0
    )
    direct = gx == 8 and rep == 2 and C == 32
    KY = MY // gx if direct else 0
    PK = 128 // (KY * C) if direct else 1
    HZ = MZ // PK
    order = np.arange(2 * MZ).reshape(2, HZ, PK).transpose(2, 0, 1).reshape(-1)
    zt = zt[order]
    zi_high, zi_low = halves(zt)
    zt = jnp.asarray(np.concatenate([zi_high, zi_low], 0))
    zi = jnp.asarray(np.concatenate([zi_high, zi_low, zi_high], 0))
    cos_x, sin_x = fourier_tables(NX, MX)
    xt = np.stack(
        [np.stack([cos_x.T, sin_x.T], 1), np.stack([-sin_x.T, cos_x.T], 1)], 1
    )
    xt = xt.reshape(MX, 2, 2, gx, xl).transpose((0, 1, 3, 4, 2) if direct else (0, 1, 3, 2, 4))
    xt = xt.reshape(2 * MX, 2 * NX)
    x_forward = jnp.asarray(xt * np.float32(scale))
    x_back = jnp.asarray(np.ascontiguousarray(xt.T))

    def spread(weight):
        rows, columns = weight.shape
        left = jnp.asarray(np.kron(np.eye(rows), np.ones((ROWS, 1))), dtype=bf16)
        right = jnp.asarray(np.kron(np.eye(columns), np.ones((1, ROWS))), dtype=bf16)
        diagonal = jnp.asarray(np.kron(np.ones((rows, columns)), np.eye(ROWS)), dtype=bf16)
        return dot(dot(left, weight).astype(bf16), right).astype(bf16) * diagonal

    kw = spread(local_weight.T)
    kp = spread(proj_weight.T)
    kpt = spread(proj_weight)

    field_spec = plane((C, NY, NZ))
    modes_shape = jax.ShapeDtypeStruct((xl, 2 * MZ, MY * C), f32)
    modes_spec = plane((2 * MZ, MY * C))
    vel_spec = plane((3, NY, NZ))

    def to_owner(slab):
        slab = slab.reshape(xl, 2, MZ, MY, C).transpose(3, 2, 1, 0, 4)
        slab = slab.reshape(gx, PL, 2, xl, C).transpose(0, 2, 3, 1, 4)
        slab = slab.reshape(gx, 2 * xl, PL * C)
        slab = lax.all_to_all(slab, "gx", split_axis=0, concat_axis=0, tiled=True)
        out = jnp.dot(x_forward, slab.reshape(2 * NX, PL * C), precision=precise)
        return out.reshape(MX, 2, PL, C)

    def to_planes(modes):
        out = jnp.dot(x_back, modes.reshape(2 * MX, PL * C), precision=precise)
        out = out.reshape(gx, 2 * xl, PL * C)
        out = lax.all_to_all(out, "gx", split_axis=0, concat_axis=0, tiled=True)
        out = out.reshape(gx, 2, xl, PL, C).transpose(0, 3, 1, 2, 4)
        out = out.reshape(MY, MZ, 2, xl, C).transpose(3, 2, 1, 0, 4)
        return out.reshape(xl, 2 * MZ, MY * C)

    def both_samples(modes):
        part = modes.reshape(rep, MX // rep, 2, PL, C)
        return lax.all_to_all(part, "rep", split_axis=0, concat_axis=0, tiled=True)

    ZN = gx // 2
    QR = HZ * 2 * MX
    slab_scratch = pltpu.VMEM((gx, xl, 2, HZ, 128), f32)
    dma = pltpu.SemaphoreType.DMA

    def comm(number):
        return pltpu.CompilerParams(
            dimension_semantics=("arbitrary",),
            vmem_limit_bytes=60 * 1024 * 1024,
            collective_id=number,
            has_side_effects=True,
        )

    if direct:
        parts = xt.reshape(rep, MX, gx, 2 * xl)
        parts = np.stack([np.concatenate([parts[r], parts[1 - r]], 0) for r in range(rep)])
        parts = parts.transpose(0, 2, 1, 3).reshape(rep * gx, 2 * MX, 2 * xl)
        x_own = jnp.asarray(parts * np.float32(scale))
        x_out = jnp.asarray(np.ascontiguousarray(parts.transpose(0, 2, 1)))
        chunk_shape = jax.ShapeDtypeStruct((QR, 128), f32)
        weight_scratch = pltpu.VMEM(spectral_weight.shape, bf16)
        row_scratch = pltpu.VMEM((2 * MX, HZ, 128), f32)
        spectrum, part = pl.pallas_call(
            forward_sum_body,
            grid=(xl,),
            out_shape=(chunk_shape, chunk_shape),
            in_specs=[field_spec, whole(ty.shape), whole(zt.shape), whole(x_own.shape)]
            + [pl.BlockSpec(memory_space=pl.ANY)],
            out_specs=(whole((QR, 128)), whole((QR, 128))),
            scratch_shapes=[slab_scratch, weight_scratch, weight_scratch]
            + [row_scratch, row_scratch, dma, dma, dma]
            + scatter_scratch(ZN, QR),
            compiler_params=comm(1),
        )(fields, ty, zt, x_own, spectral_weight)
    else:
        slab = pl.pallas_call(
            forward_body,
            grid=(xl,),
            out_shape=modes_shape,
            in_specs=[field_spec, whole(ty.shape), whole(zt.shape)],
            out_specs=modes_spec,
            compiler_params=params,
        )(fields, ty, zt)
        mapped = pl.pallas_call(
            local_body,
            grid=(xl,),
            out_shape=jax.ShapeDtypeStruct((xl, C, NY, NZ), f32),
            in_specs=[field_spec, whole(kw.shape)],
            out_specs=field_spec,
            compiler_params=pltpu.CompilerParams(vmem_limit_bytes=20 * 1024 * 1024),
        )(fields, kw)
    middle_shape = (
        jax.ShapeDtypeStruct((xl, C, NY, NZ), f32),
        jax.ShapeDtypeStruct((xl, 3, NY, NZ), f32),
    )
    wide = C * ROWS
    if direct:
        tables = [local_weight, proj_weight, x_out, zi, yi, ty, zt, x_own]

        def once(shape):
            return pl.BlockSpec(
                shape, lambda i: (0,) * len(shape), pipeline_mode=pl.Buffered(1)
            )

        penalty, chunk, sums = pl.pallas_call(
            functools.partial(step_body, scale, xl, rep),
            grid=(3 * xl,),
            out_shape=(
                jax.ShapeDtypeStruct((xl, NY, NZ), f32),
                jax.ShapeDtypeStruct((QR, 128), f32),
                jax.ShapeDtypeStruct((C, 128), f32),
            ),
            in_specs=[
                pl.BlockSpec(
                    (1, C, NY, NZ),
                    lambda i: ((i % xl) * ((i // xl + 1) % 2), 0, 0, 0),
                ),
                once((QR, 128)),
                pl.BlockSpec((1, 3, NY, NZ), lambda i: ((i % xl) * (i // (2 * xl)), 0, 0, 0)),
                once((xl, NY, NZ)),
            ]
            + [once(t.shape) for t in tables],
            out_specs=(whole((xl, NY, NZ)), whole((QR, 128)), whole((C, 128))),
            scratch_shapes=[
                pltpu.VMEM((wide, wide), bf16),
                pltpu.VMEM((3 * ROWS, wide), bf16),
                pltpu.VMEM((wide, 3 * ROWS), bf16),
                pltpu.VMEM((xl, C, NY, NZ), f32),
                pltpu.VMEM((xl, 3, NY, NZ), f32),
                pltpu.VMEM((1, 3, NY, NZ), bf16),
                pltpu.VMEM((1, C, NY, NZ), bf16),
                slab_scratch,
                pltpu.VMEM((2, ZN, QR, 128), f32),
                pltpu.VMEM((wide, wide), f32),
                pltpu.VMEM((wide, 3 * ROWS), f32),
                pltpu.VMEM((8, NZ), f32),
                pltpu.VMEM((4, NY, NZ), f32),
                pltpu.VMEM((4, NY, NZ), f32),
            ]
            + [dma((PIECES, ZN - 1))] * 2
            + [dma((PIECES, ZN))] * 2
            + [dma((2,))] * 4
            + [pltpu.VMEM((C, 128), f32), pltpu.VMEM((ZN, C, 128), f32), dma((ZN,)), dma((ZN,))]
            + scatter_scratch(ZN, QR),
            compiler_params=comm(2),
        )(fields, part, targets, multipliers, *tables)
        half = (2, MX, HZ, 128)
        grad_r, grad_w, grad_q, loss = pl.pallas_call(
            functools.partial(grad_body, scale, rep * NX * NY * NZ),
            grid=(MX // rep,),
            out_shape=(
                jax.ShapeDtypeStruct(spectral_weight.shape, f32),
                jax.ShapeDtypeStruct((C, C), f32),
                jax.ShapeDtypeStruct((C, 3), f32),
                jax.ShapeDtypeStruct((1, 1), f32),
            ),
            in_specs=[whole((QR, 128)), whole((QR, 128)), whole((C, 128))],
            out_specs=(plane((PL, 2, C, C)), whole((C, C)), whole((C, 3)), whole((1, 1))),
            scratch_shapes=[
                pltpu.VMEM((2,) + half, f32),
                pltpu.VMEM(half, f32),
                pltpu.VMEM((C, 128), f32),
                dma((3,)),
                dma((3,)),
            ],
            compiler_params=comm(3),
        )(spectrum, chunk, sums)
        return (penalty[None], grad_r, grad_w, grad_q, loss[0])
    else:
        weights = spectral_weight
        weights = weights.transpose(2, 3, 4, 0, 1).reshape(1, 2, C, C, MX // rep * PL)
        weights = lax.all_gather(weights, "rep", axis=0, tiled=True)
        spectrum = to_owner(slab)
        KX = MX // rep
        turned = spectrum.reshape(rep, KX, 2, PL, C).transpose(0, 2, 4, 1, 3)
        turned = turned.reshape(rep, 2, 1, C, KX * PL)
        w_re, w_im = weights[:, 0].astype(f32), weights[:, 1].astype(f32)
        s_re, s_im = turned[:, 0], turned[:, 1]
        product = jnp.stack(
            [jnp.sum(w_re * s_re - w_im * s_im, axis=2), jnp.sum(w_re * s_im + w_im * s_re, axis=2)],
            axis=1,
        )
        product = product.reshape(rep, 2, C, KX, PL).transpose(0, 3, 1, 4, 2)
        product = product.reshape(MX, 2, PL, C)
        spectra = both_samples(spectrum)
        wave = to_planes(product)
        pre, velocity = pl.pallas_call(
            functools.partial(middle_body, scale),
            grid=(xl,),
            out_shape=middle_shape,
            in_specs=[field_spec, modes_spec, whole(zi.shape), whole(yi.shape), whole(kp.shape)],
            out_specs=(field_spec, vel_spec),
            compiler_params=params,
        )(mapped, wave, zi, yi, kp)
        padded = extended(velocity[:, 0].astype(bf16), "gx").astype(f32)
        slope_x = (padded[2:] - padded[:-2]) * 0.5
        divergence = slope_x + central(velocity[:, 1], 1) + central(velocity[:, 2], 2)
        lam = multipliers.astype(f32) / 64.0
        penalty = lam + penalty_weight * divergence
        misfit = velocity - targets.astype(f32)
        loss_sum = (
            jnp.sum(misfit * misfit)
            + jnp.sum(lam * divergence)
            + 0.5 * penalty_weight * jnp.sum(divergence * divergence)
        )
        padded = extended(penalty.astype(bf16), "gx").astype(f32)
        pen_x = (padded[2:] - padded[:-2]) * 0.5
        slopes = jnp.stack([pen_x, central(penalty, 1), central(penalty, 2)], axis=1)
        grad_vel = ((2.0 * misfit - slopes) / rep).astype(bf16)
        grad_slab, gw, gq = pl.pallas_call(
            backward_body,
            grid=(xl,),
            out_shape=(
                modes_shape,
                jax.ShapeDtypeStruct((wide, wide), f32),
                jax.ShapeDtypeStruct((wide, 3 * ROWS), f32),
            ),
            in_specs=[field_spec, field_spec, vel_spec]
            + [whole(ty.shape), whole(zt.shape), whole(kpt.shape)],
            out_specs=(modes_spec, whole((wide, wide)), whole((wide, 3 * ROWS))),
            scratch_shapes=[pltpu.VMEM((1, C, NY, NZ), bf16)],
            compiler_params=params,
        )(fields, pre, grad_vel, ty, zt, kpt)
        gather = jnp.asarray(np.kron(np.eye(C), np.ones((1, ROWS))).astype(np.float32))
        gather_q = jnp.asarray(np.kron(np.eye(3), np.ones((ROWS, 1))).astype(np.float32))
        mask = jnp.asarray(np.kron(np.ones((C, C)), np.eye(ROWS)).astype(np.float32))
        mask_q = jnp.asarray(np.kron(np.ones((C, 3)), np.eye(ROWS)).astype(np.float32))
        grad_w = jnp.dot(gather, gw * mask, precision=precise)
        grad_w = jnp.dot(grad_w, gather.T, precision=precise)
        grad_q = jnp.dot(gather, gq * mask_q, precision=precise)
        grad_q = jnp.dot(grad_q, gather_q, precision=precise)
        grads = both_samples(to_owner(grad_slab))
        packed = jnp.concatenate([grad_w.reshape(-1), grad_q.reshape(-1), loss_sum.reshape(1)])
        packed = lax.psum(packed, ("gx", "rep"))
        grad_w = packed[: C * C].reshape(C, C)
        grad_q = packed[C * C : C * C + 3 * C].reshape(C, 3)
        loss = packed[-1:]
    loss = loss / (rep * NX * NY * NZ)

    g_re, g_im = grads[:, :, 0], grads[:, :, 1]
    across = jnp.stack([jnp.stack([g_re, g_im], 3), jnp.stack([g_im, -g_re], 3)], 1)
    terms = [
        across[b, t][..., None] * spectra[b, :, t][:, :, None, None, :]
        for b in range(rep)
        for t in range(2)
    ]
    grad_r = sum(terms[1:], terms[0])
    return (penalty[None], grad_r, grad_w * scale, grad_q * scale, loss)


def solution(mesh):
    in_specs = (
        P(("grp", "rep"), "gx", None, None, None),
        P(("grp", "rep"), "gx", None, None, None),
        P(("grp", "rep"), "gx", None, None),
        P(),
        P(),
        P("rep", "gx", None, None, None),
    )
    out_specs = (
        P(("grp", "rep"), "gx", None, None),
        P(("grp", "rep"), "gx", None, None, None),
        P("grp", None),
        P("grp", None),
        P("grp"),
    )
    return jax.shard_map(local, mesh=mesh, in_specs=in_specs, out_specs=out_specs, check_vma=False)
```

```python
import functools
import math

import jax
import jax.numpy as jnp
import ml_dtypes
import numpy as np
from jax import lax
from jax.experimental import pallas as pl
from jax.experimental.pallas import tpu as pltpu
from jax.sharding import PartitionSpec as P

MX = 16
MY = 16
MZ = 16
ROWS = 16

penalty_weight = 0.5
precise = lax.Precision.HIGHEST
bf16 = jnp.bfloat16
f32 = jnp.float32
ROOT = math.sqrt(2.0 / math.pi)


def fourier_tables(length, count):
    position = np.arange(count)
    modes = np.where(position < count // 2, position, position - count)
    phase = np.mod(np.arange(length)[:, None] * modes[None, :], length)
    angle = phase.astype(np.float32) * np.float32(2.0 * math.pi / length)
    return np.cos(angle), np.sin(angle)


def halves(table):
    high = table.astype(ml_dtypes.bfloat16)
    low = (table - high.astype(np.float32)).astype(ml_dtypes.bfloat16)
    return high, low


def split(value):
    high = value.astype(bf16)
    return high, (value - high.astype(f32)).astype(bf16)


def dot(a, b):
    return jnp.dot(a, b, preferred_element_type=f32)


def dot_nt(a, b):
    return lax.dot_general(a, b, (((1,), (1,)), ((), ())), preferred_element_type=f32)


def dot_tn(a, b):
    return lax.dot_general(a, b, (((0,), (0,)), ((), ())), preferred_element_type=f32)


def plane_modes(load, count, ty, zt):
    parts = []
    for c in range(0, count, 2):
        pair = dot(ty, jnp.concatenate([load(c), load(c + 1)], axis=1))
        nz = pair.shape[1] // 2
        parts += [pair[:, :nz], pair[:, nz:]]
    turned = jnp.swapaxes(jnp.stack(parts, axis=0), 0, 1)
    real = turned[:MY].reshape(MY * count, nz)
    imag = turned[MY:].reshape(MY * count, nz)
    high, low = split(jnp.concatenate([real, imag], axis=1))
    both = dot_nt(zt, high)
    n = 2 * MZ
    return both[:n] + both[n:] + dot_nt(zt[:n], low)


def store_modes(out_ref, modes):
    if len(out_ref.shape) == 3:
        out_ref[0] = modes
        return
    owners, _, _, high, lanes = out_ref.shape
    width = modes.shape[1] // owners
    rows = 2 * high
    for d in range(owners):
        parts = [
            modes[j * rows : (j + 1) * rows, d * width : (d + 1) * width]
            for j in range(lanes // width)
        ]
        out_ref[d, 0] = jnp.concatenate(parts, axis=1).reshape(2, high, lanes)


def load_modes(m_ref, columns):
    if len(m_ref.shape) == 3:
        return m_ref[0]
    owners, _, _, high, lanes = m_ref.shape
    width = columns // owners
    blocks = [m_ref[d, 0].reshape(2 * high, lanes) for d in range(owners)]
    rows = [
        jnp.concatenate([block[:, j * width : (j + 1) * width] for block in blocks], axis=1)
        for j in range(lanes // width)
    ]
    return jnp.concatenate(rows, axis=0)


def forward_body(f_ref, ty_ref, zt_ref, out_ref):
    count = f_ref.shape[1]
    store_modes(out_ref, plane_modes(lambda c: f_ref[0, c], count, ty_ref[...], zt_ref[...]))


MESH = pl.DeviceIdType.MESH
PIECES = 4


def place():
    me = lax.axis_index("gx")
    return me, me // 2, lax.rem(me, 2)


def pair():
    r = lax.axis_index("rep")
    return r * lax.axis_size("gx") + lax.axis_index("gx"), {"rep": 1 - r}


def greet(ring=False, core=False):
    _, z, x = place()
    zn = lax.axis_size("gx") // 2
    barrier = pltpu.get_barrier_semaphore()
    pl.semaphore_signal(barrier, inc=1, device_id={"gx": z * 2 + 1 - x}, device_id_type=MESH)
    for j in range(1, zn):
        t = lax.rem(z + j, zn)
        pl.semaphore_signal(barrier, inc=1, device_id={"gx": t * 2 + x}, device_id_type=MESH)
    if ring:
        me = z * 2 + x
        t = lax.rem(me + 2 * x - 1 + 2 * zn, 2 * zn)
        pl.semaphore_signal(barrier, inc=1, device_id={"gx": t}, device_id_type=MESH)
    if core:
        pl.semaphore_signal(barrier, inc=1, device_id=pair()[1], device_id_type=MESH)
    pl.semaphore_wait(barrier, zn + (1 if ring else 0) + (1 if core else 0))


def send(src, dst, sems, where):
    copy = pltpu.make_async_remote_copy(
        src, dst, sems[0], sems[1], device_id=where, device_id_type=MESH
    )
    copy.start()
    return copy


def scatter_sum(a_ref, o_ref, xbuf, sbuf, zbuf, xs, xr, zs, zr, extra=None):
    _, z, x = place()
    zn, rows = a_ref.shape[1], a_ref.shape[2]
    step = rows // PIECES
    to_x = {"gx": z * 2 + 1 - x}
    first, second = [], []
    if extra is not None:
        e_ref, ebuf, es, er = extra
        swap = send(e_ref, ebuf.at[0], (es.at[0], er.at[0]), to_x)
    for p in range(PIECES):
        part = pl.ds(p * step, step)
        first.append(send(a_ref.at[1 - x, :, part], xbuf.at[p], (xs.at[p], xr.at[p]), to_x))
    if extra is not None:
        swap.wait()
        e_ref[...] = e_ref[...] + ebuf[0]
        spread = [
            send(e_ref, ebuf.at[j], (es.at[j], er.at[j]), {"gx": lax.rem(z + j, zn) * 2 + x})
            for j in range(1, zn)
        ]
    for p in range(PIECES):
        part = pl.ds(p * step, step)
        first[p].wait_recv()
        for j in (2, 1, 3):
            t = lax.rem(z + j, zn)
            sbuf[p, j - 1] = a_ref[x, t, part] + xbuf[p, t]
            copy = send(
                sbuf.at[p, j - 1],
                zbuf.at[p, j - 1],
                (zs.at[p, j - 1], zr.at[p, j - 1]),
                {"gx": t * 2 + x},
            )
            second.append((p, copy))
        o_ref[part] = a_ref[x, z, part] + xbuf[p, z]
    for p in range(PIECES):
        part = pl.ds(p * step, step)
        for q, copy in second:
            if q == p:
                copy.wait_recv()
        o_ref[part] = o_ref[part] + ((zbuf[p, 0] + zbuf[p, 1]) + zbuf[p, 2])
    for copy in first + [copy for _, copy in second]:
        copy.wait_send()
    if extra is not None:
        for copy in spread:
            copy.wait()
        e_ref[...] = (e_ref[...] + ebuf[1]) + (ebuf[2] + ebuf[3])


def scatter_scratch(zn, rows):
    step = rows // PIECES
    dma = pltpu.SemaphoreType.DMA
    return [
        pltpu.VMEM((2, zn, rows, 128), f32),
        pltpu.VMEM((PIECES, zn, step, 128), f32),
        pltpu.VMEM((PIECES, zn - 1, step, 128), f32),
        pltpu.VMEM((PIECES, zn - 1, step, 128), f32),
        dma((PIECES,)),
        dma((PIECES,)),
        dma((PIECES, zn - 1)),
        dma((PIECES, zn - 1)),
    ]


def x_sum(slab_ref, table_ref, a_ref):
    owners, xl, _, high, lanes = slab_ref.shape
    rows = table_ref.shape[0]
    for d in range(owners):
        turned = jnp.swapaxes(slab_ref[d].reshape(2 * xl, high, lanes), 0, 1)
        for k in range(high):
            a_ref[d % 2, d // 2, k * rows : (k + 1) * rows] = jnp.dot(
                table_ref[...], turned[k], precision=precise, preferred_element_type=f32
            )


def x_spread(all_ref, table_ref, slab_ref):
    owners, xl, _, high, lanes = slab_ref.shape
    rows = table_ref.shape[1]
    for d in range(owners):
        parts = [
            jnp.dot(
                table_ref[...],
                all_ref[d % 2, d // 2, k * rows : (k + 1) * rows],
                precision=precise,
                preferred_element_type=f32,
            )
            for k in range(high)
        ]
        turned = jnp.swapaxes(jnp.stack(parts, axis=0), 0, 1)
        slab_ref[d] = turned.reshape(xl, 2, high, lanes)


def spread_weight(weight, turned):
    rows, cols = weight.shape[::-1] if turned else weight.shape

    def match(shape, low, high):
        a = lax.broadcasted_iota(jnp.int32, shape, 0)
        b = lax.broadcasted_iota(jnp.int32, shape, 1)
        return low(a) == high(b)

    tall = match((rows * ROWS, rows), lambda a: a // ROWS, lambda b: b)
    wide = match((cols, cols * ROWS), lambda a: a, lambda b: b // ROWS)
    tall = jnp.where(tall, 1.0, 0.0).astype(bf16)
    wide = jnp.where(wide, 1.0, 0.0).astype(bf16)
    half = (dot_nt if turned else dot)(tall, weight).astype(bf16)
    diagonal = match((rows * ROWS, cols * ROWS), lambda a: a % ROWS, lambda b: b % ROWS)
    return jnp.where(diagonal, dot(half, wide), 0.0).astype(bf16)


def turn(chunk_ref, out_ref):
    steps, high, lanes = out_ref.shape
    out_ref[...] = jnp.swapaxes(chunk_ref[...].reshape(high, steps, lanes), 0, 1)


def multiply(weights, in_ref, res_ref, out_ref):
    steps, high, lanes = in_ref.shape
    KX, PL, _, _, C = weights[0].shape
    KY, PK = PL // MZ, MZ // high
    row = lax.broadcasted_iota(jnp.int32, (high, lanes), 0)
    lane = lax.broadcasted_iota(jnp.int32, (high, lanes), 1)
    low = (lane // C) % 2 == 0

    for half, w_ref in enumerate(weights):

        def one(k, carry, half=half, w_ref=w_ref):
            at = 2 * (half * KX + k)
            rest = in_ref[pl.ds(at, 2)]
            pieces = []
            for _ in range(3):
                pieces.append(rest.astype(bf16).astype(f32))
                rest = rest - pieces[-1]
            results = []
            for ky in range(KY):
                rows = [
                    piece[ri][:, (pk * KY + ky) * C : (pk * KY + ky + 1) * C]
                    for piece in pieces
                    for ri in range(2)
                    for pk in range(PK)
                ]
                w = w_ref[k, ky * MZ : (ky + 1) * MZ].reshape(MZ * 2 * C, C)
                terms = dot_nt(jnp.concatenate(rows, axis=0).astype(bf16), w)
                terms = terms.reshape(3, 2, PK, high, MZ * 2 * C)
                terms = (terms[2] + terms[1]) + terms[0]
                kept = []
                for ri in range(2):
                    value = None
                    for h in range(high):
                        own = slice(h * lanes, (h + 1) * lanes)
                        here = jnp.where(
                            lane < 2 * C, terms[ri, 0][:, own], terms[ri, 1][:, own]
                        )
                        value = here if value is None else jnp.where(row == h, here, value)
                    kept.append(value)
                real, imag = kept
                imag = jnp.where(low, -pltpu.roll(imag, lanes - C, 1), pltpu.roll(imag, C, 1))
                results.append(real + imag)
            one_, two = results
            res_ref[at] = jnp.where(low, one_, pltpu.roll(two, C, 1))
            res_ref[at + 1] = jnp.where(low, pltpu.roll(one_, lanes - C, 1), two)
            return carry

        lax.fori_loop(0, KX, one, 0)
    out_ref[...] = jnp.swapaxes(res_ref[...], 0, 1).reshape(out_ref.shape)


def forward_sum_body(
    f_ref, ty_ref, zt_ref, xt_ref, w_ref,
    both_ref, prod_ref,
    slab_ref, wown_ref, woth_ref, chunk_ref, in_ref, res_ref, got_ref,
    own_sem, ws, wr, ss, sr, *scatter
):
    i = pl.program_id(0)
    count = f_ref.shape[1]
    table, core = pair()
    fetch = pltpu.make_async_copy(w_ref, wown_ref, own_sem)
    swap = pltpu.make_async_remote_copy(
        w_ref, woth_ref, ws, wr, device_id=core, device_id_type=MESH
    )

    @pl.when(i == 0)
    def _():
        greet(core=True)
        fetch.start()
        swap.start()

    store_modes(
        slab_ref.at[:, pl.ds(i, 1)],
        plane_modes(lambda c: f_ref[0, c], count, ty_ref[...], zt_ref[...]),
    )

    @pl.when(i == pl.num_programs(0) - 1)
    def _():
        x_sum(slab_ref, xt_ref.at[table], scatter[0])
        scatter_sum(scatter[0], chunk_ref, *scatter[1:])
        turn(chunk_ref, in_ref)
        half = in_ref.shape[0] // 2
        cross = send(in_ref.at[pl.ds(half, half)], got_ref, (ss, sr), core)
        fetch.wait()
        swap.wait()
        multiply((wown_ref, woth_ref), in_ref, res_ref, prod_ref)
        cross.wait()
        both_ref[0] = in_ref[:half]
        both_ref[1] = got_ref[...]


def grad_body(
    scale, cells, s_ref, g_ref, sums_ref, e_ref,
    out_ref, gw_ref, gq_ref, loss_ref, copy_ref
):
    _, PL, _, C, _ = out_ref.shape
    _, _, high, lanes = s_ref.shape
    KY, PK = PL // MZ, MZ // high
    copy_ref[...] = e_ref[...]

    @pl.when(pl.program_id(0) == 0)
    def _():
        total = sums_ref[...]
        gw_ref[...] = total[:, :C] * scale
        gq_ref[...] = (total[:, C : C + 8] * scale).T[:3]
        loss_ref[...] = total[:1, C + 3 : C + 4] * (1.0 / cells)

    def pieces(ref):
        high_part, low_part = split(ref[...].reshape(4, high, lanes))
        return high_part.astype(f32), low_part.astype(f32)

    f_high, f_low = pieces(s_ref)
    field = jnp.concatenate([f_high, f_low, f_high], axis=0).reshape(12 * high, lanes)
    field = field.astype(bf16)
    g_high, g_low = pieces(g_ref)
    grads = [g_high, g_high, g_low]
    swapped = [jnp.stack([g[1], -g[0], g[3], -g[2]], axis=0) for g in grads]
    turned = [
        jnp.concatenate(g, axis=0).reshape(12 * high, lanes).T for g in (grads, swapped)
    ]
    lane = lax.broadcasted_iota(jnp.int32, (C, 12 * high), 1) % high
    for pk in range(PK):
        for ky in range(KY):
            at = (pk * KY + ky) * C
            rows = [
                jnp.where(lane == h, turned[n][at : at + C], 0.0).astype(bf16)
                for h in range(high)
                for n in range(2)
            ]
            value = dot(jnp.concatenate(rows, axis=0), field[:, at : at + C])
            for h in range(high):
                for n in range(2):
                    row = (2 * h + n) * C
                    out_ref[0, ky * MZ + h * PK + pk, n] = value[row : row + C]


def tile_pair(ref, y0):
    count, nz = ref.shape[1], ref.shape[3]
    one = ref[0, :, pl.ds(y0, ROWS), :].reshape(count * ROWS, nz)
    two = ref[0, :, pl.ds(y0 + ROWS, ROWS), :].reshape(count * ROWS, nz)
    return jnp.concatenate([one, two], axis=1)


def put_pair(ref, y0, value):
    count, nz = ref.shape[1], ref.shape[3]
    ref[0, :, pl.ds(y0, ROWS), :] = value[:, :nz].reshape(count, ROWS, nz)
    ref[0, :, pl.ds(y0 + ROWS, ROWS), :] = value[:, nz:].reshape(count, ROWS, nz)


def local_body(f_ref, kw_ref, out_ref):
    for y0 in range(0, f_ref.shape[2], 2 * ROWS):
        put_pair(out_ref, y0, dot(kw_ref[...], tile_pair(f_ref, y0)))


def middle_body(scale, l_ref, m_ref, zi_ref, yi_ref, kp_ref, pre_ref, vel_ref):
    count, ny, nz = l_ref.shape[1], l_ref.shape[2], l_ref.shape[3]
    high, low = split(load_modes(m_ref, MY * count))
    wave = dot_tn(jnp.concatenate([high, high, low], axis=0), zi_ref[...])
    turned = jnp.swapaxes(wave.reshape(MY, count, 2 * nz), 0, 1)
    yi = yi_ref[...]
    for o in range(0, count, 2):
        pair = [
            jnp.concatenate([turned[i, :, :nz], turned[i, :, nz:]], axis=0) for i in (o, o + 1)
        ]
        both = dot(yi, jnp.concatenate(pair, axis=1).astype(bf16))
        pre_ref[0, o] = l_ref[0, o] + both[:, :nz] * scale
        pre_ref[0, o + 1] = l_ref[0, o + 1] + both[:, nz:] * scale

    for y0 in range(0, ny, 2 * ROWS):
        x = tile_pair(pre_ref, y0)
        t = jnp.tanh(x * (ROOT + (0.044715 * ROOT) * (x * x)))
        half = 0.5 * x
        hidden = (half + half * t).astype(bf16)
        put_pair(vel_ref, y0, dot(kp_ref[...], hidden))


def backward_body(
    f_ref, pre_ref, gv_ref, ty_ref, zt_ref, kpt_ref, out_ref, gw_ref, gq_ref, gp_ref, first=0
):
    count, ny, nz = f_ref.shape[1], f_ref.shape[2], f_ref.shape[3]

    @pl.when(pl.program_id(0) == first)
    def _():
        gw_ref[...] = jnp.zeros_like(gw_ref)
        gq_ref[...] = jnp.zeros_like(gq_ref)

    hiddens, grads, fields, slopes = [], [], [], []
    for y0 in range(0, ny, 2 * ROWS):
        gv = tile_pair(gv_ref, y0)
        x = tile_pair(pre_ref, y0)
        cubic = (0.044715 * ROOT) * (x * x)
        t = jnp.tanh(x * (ROOT + cubic))
        cdf = 0.5 + 0.5 * t
        hidden = (x * cdf).astype(bf16)
        slope = cdf + (x * (ROOT + 3.0 * cubic)) * (0.5 - 0.5 * (t * t))
        gp = (dot(kpt_ref[...], gv) * slope).astype(bf16)
        put_pair(gp_ref, y0, gp)
        hiddens.append(hidden)
        grads.append(gp)
        slopes.append(gv)
        fields.append(tile_pair(f_ref, y0))
    gw_ref[...] += dot_nt(jnp.concatenate(fields, axis=1), jnp.concatenate(grads, axis=1))
    gq_ref[...] += dot_nt(jnp.concatenate(hiddens, axis=1), jnp.concatenate(slopes, axis=1))

    store_modes(out_ref, plane_modes(lambda c: gp_ref[0, c], count, ty_ref[...], zt_ref[...]))


def fold(total, columns):
    rows, cols = total.shape
    row = lax.broadcasted_iota(jnp.int32, total.shape, 0) % ROWS
    col = lax.broadcasted_iota(jnp.int32, total.shape, 1) % ROWS
    kept = jnp.where(row == col, total, 0.0).reshape(rows // ROWS, ROWS, cols)
    lane = lax.broadcasted_iota(jnp.int32, (cols, 128), 1)
    block = lax.broadcasted_iota(jnp.int32, (cols, 128), 0) // ROWS
    gather = jnp.where(lane == block + columns, 1.0, 0.0)
    return jnp.dot(jnp.sum(kept, axis=1), gather, precision=precise, preferred_element_type=f32)


def gather_parts(all_ref, zs, zr, xs, xr):
    _, z, x = place()
    zn, rows = all_ref.shape[1], all_ref.shape[2]
    step = rows // PIECES

    def along(p, j):
        part = pl.ds(p * step, step)
        return pltpu.make_async_remote_copy(
            all_ref.at[x, z, part],
            all_ref.at[x, z, part],
            zs.at[p, j - 1],
            zr.at[p, j - 1],
            device_id={"gx": lax.rem(z + j, zn) * 2 + x},
            device_id_type=MESH,
        )

    def across(p, j):
        part = pl.ds(p * step, step)
        t = lax.rem(z - j + zn, zn)
        return pltpu.make_async_remote_copy(
            all_ref.at[x, t, part],
            all_ref.at[x, t, part],
            xs.at[p, j],
            xr.at[p, j],
            device_id={"gx": z * 2 + 1 - x},
            device_id_type=MESH,
        )

    return along, across


def step_body(
    scale, xl, rep,
    f_ref, s_ref, t_ref, mult_ref, lw_ref, pw_ref, xb_ref, zi_ref, yi_ref,
    ty_ref, zt_ref, xt_ref,
    e_ref, both_ref, sums_ref,
    kw_ref, kp_ref, kpt_ref,
    pre_ref, vel_ref, gv_ref, gp_ref, slab_ref, all_ref, gw_ref, gq_ref, loss_ref,
    edge_ref, halo_ref, zs, zr, xs, xr, us, ur, ps, pr,
    pack_ref, ebuf, es, er, chunk_ref, turned_ref, got_ref, other_ref, cs, cr, *scatter
):
    i = pl.program_id(0)
    me, z, x = place()
    table, core = pair()
    gx = lax.axis_size("gx")
    zn = gx // 2
    along, across = gather_parts(all_ref, zs, zr, xs, xr)
    right = {"gx": lax.rem(me + 1, gx)}
    left = {"gx": lax.rem(me + gx - 1, gx)}

    def halo(k, sems):
        return pltpu.make_async_remote_copy(
            edge_ref.at[k],
            halo_ref.at[k],
            sems[0].at[k % 2],
            sems[1].at[k % 2],
            device_id=left if k % 2 == 0 else right,
            device_id_type=MESH,
        )

    def penalty(p, before, after):
        u = vel_ref[p, 1], vel_ref[p, 2]
        rows, lanes = u[0].shape
        slope = (after - before) * 0.5
        slope = slope + (pltpu.roll(u[0], rows - 1, 0) - pltpu.roll(u[0], 1, 0)) * 0.5
        slope = slope + (pltpu.roll(u[1], lanes - 1, 1) - pltpu.roll(u[1], 1, 1)) * 0.5
        lam = mult_ref[p].astype(f32) / 64.0
        e_ref[p] = lam + penalty_weight * slope
        add_loss((lam + (0.5 * penalty_weight) * slope) * slope)

    def add_loss(value):
        rows, lanes = value.shape
        loss_ref[...] = loss_ref[...] + jnp.sum(value.reshape(rows // 8, 8, lanes), axis=0)

    @pl.when(i == 0)
    def _():
        all_ref[x, z] = s_ref[...]
        loss_ref[...] = jnp.zeros_like(loss_ref)
        greet(True, True)
        for p in range(PIECES):
            for j in (2, 1, 3):
                along(p, j).start()
            across(p, 0).start()
        kw_ref[...] = spread_weight(lw_ref[...], True)
        kp_ref[...] = spread_weight(pw_ref[...], False)
        kpt_ref[...] = spread_weight(pw_ref[...], True)

    for p in range(PIECES):

        @pl.when(i == ((p + 1) * xl) // PIECES - 1)
        def _(p=p):
            for j in range(1, zn):
                along(p, j).wait_recv()
                across(p, j).start()

    @pl.when(i < xl)
    def _():
        plane_ref = pre_ref.at[pl.ds(i, 1)]
        for y0 in range(0, f_ref.shape[2], 2 * ROWS):
            put_pair(plane_ref, y0, dot(kw_ref[...], tile_pair(f_ref, y0)))

    @pl.when(i == xl)
    def _():
        for p in range(PIECES):
            for j in range(zn):
                across(p, j).wait()
            for j in range(1, zn):
                along(p, j).wait_send()
        x_spread(all_ref, xb_ref.at[table], slab_ref)

    @pl.when((i >= xl) & (i < 2 * xl))
    def _():
        m = i - xl
        odd = lax.rem(m, 2)
        p = odd * (xl - 1 - m // 2) + (1 - odd) * (m // 2)
        plane_ref = pre_ref.at[pl.ds(p, 1)]
        modes_ref = slab_ref.at[:, pl.ds(p, 1)]
        middle_body(
            scale, plane_ref, modes_ref, zi_ref, yi_ref, kp_ref, plane_ref,
            vel_ref.at[pl.ds(p, 1)],
        )

    @pl.when(i == xl + 1)
    def _():
        edge_ref[0] = vel_ref[0, 0]
        edge_ref[1] = vel_ref[xl - 1, 0]
        for k in (0, 1):
            halo(k, (us, ur)).start()

    @pl.when(i == xl + xl // 2)
    def _():
        for k in (0, 1):
            halo(k, (us, ur)).wait()
        penalty(0, halo_ref[1], vel_ref[1, 0])
        penalty(xl - 1, vel_ref[xl - 2, 0], halo_ref[0])
        edge_ref[2] = e_ref[0]
        edge_ref[3] = e_ref[xl - 1]
        for k in (2, 3):
            halo(k, (ps, pr)).start()

    @pl.when(i == 2 * xl - 1)
    def _():
        def one(p, carry):
            penalty(p, vel_ref[p - 1, 0], vel_ref[p + 1, 0])
            return carry

        lax.fori_loop(1, xl - 1, one, 0)
        for k in (2, 3):
            halo(k, (ps, pr)).wait()

    @pl.when(i >= 2 * xl)
    def _():
        p = i - 2 * xl
        e = e_ref[p]
        rows, lanes = e.shape
        before = lax.select(
            jnp.broadcast_to(p == 0, e.shape), halo_ref[3], e_ref[lax.rem(p + xl - 1, xl)]
        )
        after = lax.select(
            jnp.broadcast_to(p == xl - 1, e.shape), halo_ref[2], e_ref[lax.rem(p + 1, xl)]
        )
        slopes = (
            (after - before) * 0.5,
            (pltpu.roll(e, rows - 1, 0) - pltpu.roll(e, 1, 0)) * 0.5,
            (pltpu.roll(e, lanes - 1, 1) - pltpu.roll(e, 1, 1)) * 0.5,
        )
        for j in range(3):
            misfit = vel_ref[p, j] - t_ref[0, j].astype(f32)
            add_loss(misfit * misfit)
            gv_ref[0, j] = ((2.0 * misfit - slopes[j]) / rep).astype(bf16)
        backward_body(
            f_ref, pre_ref.at[pl.ds(p, 1)], gv_ref, ty_ref, zt_ref, kpt_ref,
            slab_ref.at[:, pl.ds(p, 1)], gw_ref, gq_ref, gp_ref, first=2 * xl,
        )

    @pl.when(i == pl.num_programs(0) - 1)
    def _():
        x_sum(slab_ref, xt_ref.at[table], scatter[0])
        count = f_ref.shape[1]
        lane = lax.broadcasted_iota(jnp.int32, (count, 128), 1)
        pack_ref[...] = (
            fold(gw_ref[...], 0)
            + fold(gq_ref[...], count)
            + jnp.where(lane == count + 3, jnp.sum(loss_ref[...]), 0.0)
        )
        scatter_sum(scatter[0], chunk_ref, *scatter[1:], extra=(pack_ref, ebuf, es, er))
        turn(chunk_ref, turned_ref)
        half = turned_ref.shape[0] // 2
        copies = [
            send(turned_ref.at[pl.ds(half, half)], got_ref, (cs.at[0], cr.at[0]), core),
            send(pack_ref, other_ref, (cs.at[1], cr.at[1]), core),
        ]
        for copy in copies:
            copy.wait()
        both_ref[0] = turned_ref[:half]
        both_ref[1] = got_ref[...]
        sums_ref[...] = pack_ref[...] + other_ref[...]


def whole(shape):
    return pl.BlockSpec(shape, lambda i: (0,) * len(shape))


def plane(shape):
    return pl.BlockSpec((1,) + tuple(shape), lambda i: (i,) + (0,) * len(shape))


params = pltpu.CompilerParams(
    dimension_semantics=("arbitrary",), vmem_limit_bytes=56 * 1024 * 1024
)


def extended(value, axis_name):
    count = lax.axis_size(axis_name)
    up = [(i, (i + 1) % count) for i in range(count)]
    down = [(j, i) for i, j in up]
    before = lax.ppermute(value[-1:], axis_name, up)
    after = lax.ppermute(value[:1], axis_name, down)
    return jnp.concatenate([before, value, after], axis=0)


def central(values, axis):
    return (jnp.roll(values, -1, axis) - jnp.roll(values, 1, axis)) * 0.5


def local(fields, targets, multipliers, local_weight, proj_weight, spectral_weight):
    gx = lax.axis_size("gx")
    rep = lax.axis_size("rep")
    _, xl, C, NY, NZ = fields.shape
    NX = xl * gx
    PL = MY * MZ // gx
    scale = 1.0 / math.sqrt(NX * NY * NZ)
    fields, targets, multipliers = fields[0], targets[0], multipliers[0]

    cos_y, sin_y = fourier_tables(NY, MY)
    ty = jnp.asarray(np.concatenate([cos_y.T, -sin_y.T], 0).astype(ml_dtypes.bfloat16))
    yi = jnp.asarray(np.concatenate([cos_y, -sin_y], 1).astype(ml_dtypes.bfloat16))
    cos_z, sin_z = fourier_tables(NZ, MZ)
    zt = np.concatenate(
        [np.concatenate([cos_z.T, sin_z.T], 1), np.concatenate([-sin_z.T, cos_z.T], 1)], 0
    )
    direct = gx == 8 and rep == 2 and C == 32
    KY = MY // gx if direct else 0
    PK = 128 // (KY * C) if direct else 1
    HZ = MZ // PK
    order = np.arange(2 * MZ).reshape(2, HZ, PK).transpose(2, 0, 1).reshape(-1)
    zt = zt[order]
    zi_high, zi_low = halves(zt)
    zt = jnp.asarray(np.concatenate([zi_high, zi_low], 0))
    zi = jnp.asarray(np.concatenate([zi_high, zi_low, zi_high], 0))
    cos_x, sin_x = fourier_tables(NX, MX)
    xt = np.stack(
        [np.stack([cos_x.T, sin_x.T], 1), np.stack([-sin_x.T, cos_x.T], 1)], 1
    )
    xt = xt.reshape(MX, 2, 2, gx, xl).transpose((0, 1, 3, 4, 2) if direct else (0, 1, 3, 2, 4))
    xt = xt.reshape(2 * MX, 2 * NX)
    x_forward = jnp.asarray(xt * np.float32(scale))
    x_back = jnp.asarray(np.ascontiguousarray(xt.T))

    def spread(weight):
        rows, columns = weight.shape
        left = jnp.asarray(np.kron(np.eye(rows), np.ones((ROWS, 1))), dtype=bf16)
        right = jnp.asarray(np.kron(np.eye(columns), np.ones((1, ROWS))), dtype=bf16)
        diagonal = jnp.asarray(np.kron(np.ones((rows, columns)), np.eye(ROWS)), dtype=bf16)
        return dot(dot(left, weight).astype(bf16), right).astype(bf16) * diagonal

    kw = spread(local_weight.T)
    kp = spread(proj_weight.T)
    kpt = spread(proj_weight)

    field_spec = plane((C, NY, NZ))
    modes_shape = jax.ShapeDtypeStruct((xl, 2 * MZ, MY * C), f32)
    modes_spec = plane((2 * MZ, MY * C))
    vel_spec = plane((3, NY, NZ))

    def to_owner(slab):
        slab = slab.reshape(xl, 2, MZ, MY, C).transpose(3, 2, 1, 0, 4)
        slab = slab.reshape(gx, PL, 2, xl, C).transpose(0, 2, 3, 1, 4)
        slab = slab.reshape(gx, 2 * xl, PL * C)
        slab = lax.all_to_all(slab, "gx", split_axis=0, concat_axis=0, tiled=True)
        out = jnp.dot(x_forward, slab.reshape(2 * NX, PL * C), precision=precise)
        return out.reshape(MX, 2, PL, C)

    def to_planes(modes):
        out = jnp.dot(x_back, modes.reshape(2 * MX, PL * C), precision=precise)
        out = out.reshape(gx, 2 * xl, PL * C)
        out = lax.all_to_all(out, "gx", split_axis=0, concat_axis=0, tiled=True)
        out = out.reshape(gx, 2, xl, PL, C).transpose(0, 3, 1, 2, 4)
        out = out.reshape(MY, MZ, 2, xl, C).transpose(3, 2, 1, 0, 4)
        return out.reshape(xl, 2 * MZ, MY * C)

    def both_samples(modes):
        part = modes.reshape(rep, MX // rep, 2, PL, C)
        return lax.all_to_all(part, "rep", split_axis=0, concat_axis=0, tiled=True)

    ZN = gx // 2
    QR = HZ * 2 * MX
    slab_scratch = pltpu.VMEM((gx, xl, 2, HZ, 128), f32)
    dma = pltpu.SemaphoreType.DMA

    def comm(number):
        return pltpu.CompilerParams(
            dimension_semantics=("arbitrary",),
            vmem_limit_bytes=60 * 1024 * 1024,
            collective_id=number,
            has_side_effects=True,
        )

    if direct:
        parts = xt.reshape(rep, MX, gx, 2 * xl)
        parts = np.stack([np.concatenate([parts[r], parts[1 - r]], 0) for r in range(rep)])
        parts = parts.transpose(0, 2, 1, 3).reshape(rep * gx, 2 * MX, 2 * xl)
        x_own = jnp.asarray(parts * np.float32(scale))
        x_out = jnp.asarray(np.ascontiguousarray(parts.transpose(0, 2, 1)))
        chunk_shape = jax.ShapeDtypeStruct((QR, 128), f32)
        weight_scratch = pltpu.VMEM(spectral_weight.shape, bf16)
        row_scratch = pltpu.VMEM((2 * MX, HZ, 128), f32)
        both_shape = jax.ShapeDtypeStruct((2, MX, HZ, 128), f32)
        half_scratch = pltpu.VMEM((MX, HZ, 128), f32)
        spectrum, part = pl.pallas_call(
            forward_sum_body,
            grid=(xl,),
            out_shape=(both_shape, chunk_shape),
            in_specs=[field_spec, whole(ty.shape), whole(zt.shape), whole(x_own.shape)]
            + [pl.BlockSpec(memory_space=pl.ANY)],
            out_specs=(whole(both_shape.shape), whole((QR, 128))),
            scratch_shapes=[slab_scratch, weight_scratch, weight_scratch]
            + [pltpu.VMEM((QR, 128), f32), row_scratch, row_scratch, half_scratch]
            + [dma] * 5
            + scatter_scratch(ZN, QR),
            compiler_params=comm(1),
        )(fields, ty, zt, x_own, spectral_weight)
    else:
        slab = pl.pallas_call(
            forward_body,
            grid=(xl,),
            out_shape=modes_shape,
            in_specs=[field_spec, whole(ty.shape), whole(zt.shape)],
            out_specs=modes_spec,
            compiler_params=params,
        )(fields, ty, zt)
        mapped = pl.pallas_call(
            local_body,
            grid=(xl,),
            out_shape=jax.ShapeDtypeStruct((xl, C, NY, NZ), f32),
            in_specs=[field_spec, whole(kw.shape)],
            out_specs=field_spec,
            compiler_params=pltpu.CompilerParams(vmem_limit_bytes=20 * 1024 * 1024),
        )(fields, kw)
    middle_shape = (
        jax.ShapeDtypeStruct((xl, C, NY, NZ), f32),
        jax.ShapeDtypeStruct((xl, 3, NY, NZ), f32),
    )
    wide = C * ROWS
    if direct:
        tables = [local_weight, proj_weight.T, x_out, zi, yi, ty, zt, x_own]

        def once(shape):
            return pl.BlockSpec(
                shape, lambda i: (0,) * len(shape), pipeline_mode=pl.Buffered(1)
            )

        penalty, chunk, sums = pl.pallas_call(
            functools.partial(step_body, scale, xl, rep),
            grid=(3 * xl,),
            out_shape=(
                jax.ShapeDtypeStruct((xl, NY, NZ), f32),
                both_shape,
                jax.ShapeDtypeStruct((C, 128), f32),
            ),
            in_specs=[
                pl.BlockSpec(
                    (1, C, NY, NZ),
                    lambda i: ((i % xl) * ((i // xl + 1) % 2), 0, 0, 0),
                ),
                once((QR, 128)),
                pl.BlockSpec((1, 3, NY, NZ), lambda i: ((i % xl) * (i // (2 * xl)), 0, 0, 0)),
                once((xl, NY, NZ)),
            ]
            + [once(t.shape) for t in tables],
            out_specs=(whole((xl, NY, NZ)), whole(both_shape.shape), whole((C, 128))),
            scratch_shapes=[
                pltpu.VMEM((wide, wide), bf16),
                pltpu.VMEM((3 * ROWS, wide), bf16),
                pltpu.VMEM((wide, 3 * ROWS), bf16),
                pltpu.VMEM((xl, C, NY, NZ), f32),
                pltpu.VMEM((xl, 3, NY, NZ), f32),
                pltpu.VMEM((1, 3, NY, NZ), bf16),
                pltpu.VMEM((1, C, NY, NZ), bf16),
                slab_scratch,
                pltpu.VMEM((2, ZN, QR, 128), f32),
                pltpu.VMEM((wide, wide), f32),
                pltpu.VMEM((wide, 3 * ROWS), f32),
                pltpu.VMEM((8, NZ), f32),
                pltpu.VMEM((4, NY, NZ), f32),
                pltpu.VMEM((4, NY, NZ), f32),
            ]
            + [dma((PIECES, ZN - 1))] * 2
            + [dma((PIECES, ZN))] * 2
            + [dma((2,))] * 4
            + [pltpu.VMEM((C, 128), f32), pltpu.VMEM((ZN, C, 128), f32), dma((ZN,)), dma((ZN,))]
            + [pltpu.VMEM((QR, 128), f32), row_scratch, half_scratch]
            + [pltpu.VMEM((C, 128), f32), dma((2,)), dma((2,))]
            + scatter_scratch(ZN, QR),
            compiler_params=comm(2),
        )(fields, part, targets, multipliers, *tables)
        KX = MX // rep
        modes_of = pl.BlockSpec((2, 2, HZ, 128), lambda i: (0, i, 0, 0))
        planes = pl.BlockSpec((xl // KX, NY, NZ), lambda i: (i, 0, 0))
        grad_r, grad_w, grad_q, loss, penalty = pl.pallas_call(
            functools.partial(grad_body, scale, rep * NX * NY * NZ),
            grid=(KX,),
            out_shape=(
                jax.ShapeDtypeStruct(spectral_weight.shape, f32),
                jax.ShapeDtypeStruct((C, C), f32),
                jax.ShapeDtypeStruct((3, C), f32),
                jax.ShapeDtypeStruct((1, 1), f32),
                jax.ShapeDtypeStruct(penalty.shape, f32),
            ),
            in_specs=[modes_of, modes_of, whole((C, 128)), planes],
            out_specs=(
                plane((PL, 2, C, C)),
                whole((C, C)),
                whole((3, C)),
                whole((1, 1)),
                planes,
            ),
            compiler_params=params,
        )(spectrum, chunk, sums, penalty)
        return (penalty[None], grad_r, grad_w, grad_q.T, loss[0])
    else:
        weights = spectral_weight
        weights = weights.transpose(2, 3, 4, 0, 1).reshape(1, 2, C, C, MX // rep * PL)
        weights = lax.all_gather(weights, "rep", axis=0, tiled=True)
        spectrum = to_owner(slab)
        KX = MX // rep
        turned = spectrum.reshape(rep, KX, 2, PL, C).transpose(0, 2, 4, 1, 3)
        turned = turned.reshape(rep, 2, 1, C, KX * PL)
        w_re, w_im = weights[:, 0].astype(f32), weights[:, 1].astype(f32)
        s_re, s_im = turned[:, 0], turned[:, 1]
        product = jnp.stack(
            [jnp.sum(w_re * s_re - w_im * s_im, axis=2), jnp.sum(w_re * s_im + w_im * s_re, axis=2)],
            axis=1,
        )
        product = product.reshape(rep, 2, C, KX, PL).transpose(0, 3, 1, 4, 2)
        product = product.reshape(MX, 2, PL, C)
        spectra = both_samples(spectrum)
        wave = to_planes(product)
        pre, velocity = pl.pallas_call(
            functools.partial(middle_body, scale),
            grid=(xl,),
            out_shape=middle_shape,
            in_specs=[field_spec, modes_spec, whole(zi.shape), whole(yi.shape), whole(kp.shape)],
            out_specs=(field_spec, vel_spec),
            compiler_params=params,
        )(mapped, wave, zi, yi, kp)
        padded = extended(velocity[:, 0].astype(bf16), "gx").astype(f32)
        slope_x = (padded[2:] - padded[:-2]) * 0.5
        divergence = slope_x + central(velocity[:, 1], 1) + central(velocity[:, 2], 2)
        lam = multipliers.astype(f32) / 64.0
        penalty = lam + penalty_weight * divergence
        misfit = velocity - targets.astype(f32)
        loss_sum = (
            jnp.sum(misfit * misfit)
            + jnp.sum(lam * divergence)
            + 0.5 * penalty_weight * jnp.sum(divergence * divergence)
        )
        padded = extended(penalty.astype(bf16), "gx").astype(f32)
        pen_x = (padded[2:] - padded[:-2]) * 0.5
        slopes = jnp.stack([pen_x, central(penalty, 1), central(penalty, 2)], axis=1)
        grad_vel = ((2.0 * misfit - slopes) / rep).astype(bf16)
        grad_slab, gw, gq = pl.pallas_call(
            backward_body,
            grid=(xl,),
            out_shape=(
                modes_shape,
                jax.ShapeDtypeStruct((wide, wide), f32),
                jax.ShapeDtypeStruct((wide, 3 * ROWS), f32),
            ),
            in_specs=[field_spec, field_spec, vel_spec]
            + [whole(ty.shape), whole(zt.shape), whole(kpt.shape)],
            out_specs=(modes_spec, whole((wide, wide)), whole((wide, 3 * ROWS))),
            scratch_shapes=[pltpu.VMEM((1, C, NY, NZ), bf16)],
            compiler_params=params,
        )(fields, pre, grad_vel, ty, zt, kpt)
        gather = jnp.asarray(np.kron(np.eye(C), np.ones((1, ROWS))).astype(np.float32))
        gather_q = jnp.asarray(np.kron(np.eye(3), np.ones((ROWS, 1))).astype(np.float32))
        mask = jnp.asarray(np.kron(np.ones((C, C)), np.eye(ROWS)).astype(np.float32))
        mask_q = jnp.asarray(np.kron(np.ones((C, 3)), np.eye(ROWS)).astype(np.float32))
        grad_w = jnp.dot(gather, gw * mask, precision=precise)
        grad_w = jnp.dot(grad_w, gather.T, precision=precise)
        grad_q = jnp.dot(gather, gq * mask_q, precision=precise)
        grad_q = jnp.dot(grad_q, gather_q, precision=precise)
        grads = both_samples(to_owner(grad_slab))
        packed = jnp.concatenate([grad_w.reshape(-1), grad_q.reshape(-1), loss_sum.reshape(1)])
        packed = lax.psum(packed, ("gx", "rep"))
        grad_w = packed[: C * C].reshape(C, C)
        grad_q = packed[C * C : C * C + 3 * C].reshape(C, 3)
        loss = packed[-1:]
    loss = loss / (rep * NX * NY * NZ)

    g_re, g_im = grads[:, :, 0], grads[:, :, 1]
    across = jnp.stack([jnp.stack([g_re, g_im], 3), jnp.stack([g_im, -g_re], 3)], 1)
    terms = [
        across[b, t][..., None] * spectra[b, :, t][:, :, None, None, :]
        for b in range(rep)
        for t in range(2)
    ]
    grad_r = sum(terms[1:], terms[0])
    return (penalty[None], grad_r, grad_w * scale, grad_q * scale, loss)


def solution(mesh):
    in_specs = (
        P(("grp", "rep"), "gx", None, None, None),
        P(("grp", "rep"), "gx", None, None, None),
        P(("grp", "rep"), "gx", None, None),
        P(),
        P(),
        P("rep", "gx", None, None, None),
    )
    out_specs = (
        P(("grp", "rep"), "gx", None, None),
        P(("grp", "rep"), "gx", None, None, None),
        P("grp", None),
        P("grp", None),
        P("grp"),
    )
    return jax.shard_map(local, mesh=mesh, in_specs=in_specs, out_specs=out_specs, check_vma=False)
```

```python
import functools
import math

import jax
import jax.numpy as jnp
import ml_dtypes
import numpy as np
from jax import lax
from jax.experimental import pallas as pl
from jax.experimental.pallas import tpu as pltpu
from jax.sharding import PartitionSpec as P

MX = 16
MY = 16
MZ = 16
ROWS = 16

penalty_weight = 0.5
precise = lax.Precision.HIGHEST
bf16 = jnp.bfloat16
f32 = jnp.float32
ROOT = math.sqrt(2.0 / math.pi)


def fourier_tables(length, count):
    position = np.arange(count)
    modes = np.where(position < count // 2, position, position - count)
    phase = np.mod(np.arange(length)[:, None] * modes[None, :], length)
    angle = phase.astype(np.float32) * np.float32(2.0 * math.pi / length)
    return np.cos(angle), np.sin(angle)


def halves(table):
    high = table.astype(ml_dtypes.bfloat16)
    low = (table - high.astype(np.float32)).astype(ml_dtypes.bfloat16)
    return high, low


def split(value):
    high = value.astype(bf16)
    return high, (value - high.astype(f32)).astype(bf16)


def dot(a, b):
    return jnp.dot(a, b, preferred_element_type=f32)


def dot_nt(a, b):
    return lax.dot_general(a, b, (((1,), (1,)), ((), ())), preferred_element_type=f32)


def dot_tn(a, b):
    return lax.dot_general(a, b, (((0,), (0,)), ((), ())), preferred_element_type=f32)


def plane_modes(load, count, ty, zt):
    parts = []
    for c in range(0, count, 2):
        pair = dot(ty, jnp.concatenate([load(c), load(c + 1)], axis=1))
        nz = pair.shape[1] // 2
        parts += [pair[:, :nz], pair[:, nz:]]
    turned = jnp.swapaxes(jnp.stack(parts, axis=0), 0, 1)
    real = turned[:MY].reshape(MY * count, nz)
    imag = turned[MY:].reshape(MY * count, nz)
    high, low = split(jnp.concatenate([real, imag], axis=1))
    both = dot_nt(zt, high)
    n = 2 * MZ
    return both[:n] + both[n:] + dot_nt(zt[:n], low)


def store_modes(out_ref, modes):
    if len(out_ref.shape) == 3:
        out_ref[0] = modes
        return
    owners, _, _, high, lanes = out_ref.shape
    width = modes.shape[1] // owners
    rows = 2 * high
    for d in range(owners):
        parts = [
            modes[j * rows : (j + 1) * rows, d * width : (d + 1) * width]
            for j in range(lanes // width)
        ]
        out_ref[d, 0] = jnp.concatenate(parts, axis=1).reshape(2, high, lanes)


def load_modes(m_ref, columns):
    if len(m_ref.shape) == 3:
        return m_ref[0]
    owners, _, _, high, lanes = m_ref.shape
    width = columns // owners
    blocks = [m_ref[d, 0].reshape(2 * high, lanes) for d in range(owners)]
    rows = [
        jnp.concatenate([block[:, j * width : (j + 1) * width] for block in blocks], axis=1)
        for j in range(lanes // width)
    ]
    return jnp.concatenate(rows, axis=0)


def forward_body(f_ref, ty_ref, zt_ref, out_ref):
    count = f_ref.shape[1]
    store_modes(out_ref, plane_modes(lambda c: f_ref[0, c], count, ty_ref[...], zt_ref[...]))


MESH = pl.DeviceIdType.MESH
PIECES = 4


def place():
    me = lax.axis_index("gx")
    return me, me // 2, lax.rem(me, 2)


def pair():
    r = lax.axis_index("rep")
    return r * lax.axis_size("gx") + lax.axis_index("gx"), {"rep": 1 - r}


def greet(ring=False, core=False):
    _, z, x = place()
    zn = lax.axis_size("gx") // 2
    barrier = pltpu.get_barrier_semaphore()
    pl.semaphore_signal(barrier, inc=1, device_id={"gx": z * 2 + 1 - x}, device_id_type=MESH)
    for j in range(1, zn):
        t = lax.rem(z + j, zn)
        pl.semaphore_signal(barrier, inc=1, device_id={"gx": t * 2 + x}, device_id_type=MESH)
    if ring:
        me = z * 2 + x
        t = lax.rem(me + 2 * x - 1 + 2 * zn, 2 * zn)
        pl.semaphore_signal(barrier, inc=1, device_id={"gx": t}, device_id_type=MESH)
    if core:
        pl.semaphore_signal(barrier, inc=1, device_id=pair()[1], device_id_type=MESH)
    pl.semaphore_wait(barrier, zn + (1 if ring else 0) + (1 if core else 0))


def send(src, dst, sems, where):
    copy = pltpu.make_async_remote_copy(
        src, dst, sems[0], sems[1], device_id=where, device_id_type=MESH
    )
    copy.start()
    return copy


class Scatter:
    def __init__(self, a_ref, o_ref, xbuf, sbuf, zbuf, xs, xr, zs, zr):
        self.refs = a_ref, o_ref, xbuf, sbuf, zbuf
        self.sems = xs, xr, zs, zr
        _, self.z, self.x = place()
        self.zn = a_ref.shape[1]
        self.step = a_ref.shape[2] // PIECES
        self.to_x = {"gx": self.z * 2 + 1 - self.x}

    def part(self, p):
        return pl.ds(p * self.step, self.step)

    def copy(self, src, dst, sems, where):
        return pltpu.make_async_remote_copy(
            src, dst, sems[0], sems[1], device_id=where, device_id_type=MESH
        )

    def across(self, p):
        a_ref, _, xbuf, _, _ = self.refs
        xs, xr, _, _ = self.sems
        return self.copy(
            a_ref.at[1 - self.x, :, self.part(p)], xbuf.at[p], (xs.at[p], xr.at[p]), self.to_x
        )

    def along(self, p, j):
        _, _, _, sbuf, zbuf = self.refs
        _, _, zs, zr = self.sems
        t = lax.rem(self.z + j, self.zn)
        return self.copy(
            sbuf.at[p, j - 1],
            zbuf.at[p, j - 1],
            (zs.at[p, j - 1], zr.at[p, j - 1]),
            {"gx": t * 2 + self.x},
        )

    def start(self):
        for p in range(PIECES):
            self.across(p).start()

    def forward(self, p):
        a_ref, o_ref, xbuf, sbuf, _ = self.refs
        self.across(p).wait_recv()
        for j in (2, 1, 3):
            t = lax.rem(self.z + j, self.zn)
            sbuf[p, j - 1] = a_ref[self.x, t, self.part(p)] + xbuf[p, t]
            self.along(p, j).start()
        o_ref[self.part(p)] = a_ref[self.x, self.z, self.part(p)] + xbuf[p, self.z]

    def finish(self, p):
        _, o_ref, _, _, zbuf = self.refs
        for j in range(1, self.zn):
            self.along(p, j).wait_recv()
        total = (zbuf[p, 0] + zbuf[p, 1]) + zbuf[p, 2]
        o_ref[self.part(p)] = o_ref[self.part(p)] + total

    def settle(self):
        for p in range(PIECES):
            self.across(p).wait_send()
            for j in range(1, self.zn):
                self.along(p, j).wait_send()


def scatter_sum(scatter, e_ref, ebuf, es, er):
    z, x, zn = scatter.z, scatter.x, scatter.zn
    swap = send(e_ref, ebuf.at[0], (es.at[0], er.at[0]), scatter.to_x)
    scatter.start()
    swap.wait()
    e_ref[...] = e_ref[...] + ebuf[0]
    spread = [
        send(e_ref, ebuf.at[j], (es.at[j], er.at[j]), {"gx": lax.rem(z + j, zn) * 2 + x})
        for j in range(1, zn)
    ]
    for p in range(PIECES):
        scatter.forward(p)
    for p in range(PIECES):
        scatter.finish(p)
    scatter.settle()
    for copy in spread:
        copy.wait()
    e_ref[...] = (e_ref[...] + ebuf[1]) + (ebuf[2] + ebuf[3])


def scatter_scratch(zn, rows):
    step = rows // PIECES
    dma = pltpu.SemaphoreType.DMA
    return [
        pltpu.VMEM((2, zn, rows, 128), f32),
        pltpu.VMEM((PIECES, zn, step, 128), f32),
        pltpu.VMEM((PIECES, zn - 1, step, 128), f32),
        pltpu.VMEM((PIECES, zn - 1, step, 128), f32),
        dma((PIECES,)),
        dma((PIECES,)),
        dma((PIECES, zn - 1)),
        dma((PIECES, zn - 1)),
    ]


def x_sum(slab_ref, table_ref, a_ref):
    owners, xl, _, high, lanes = slab_ref.shape
    rows = table_ref.shape[0]
    for d in range(owners):
        turned = jnp.swapaxes(slab_ref[d].reshape(2 * xl, high, lanes), 0, 1)
        for k in range(high):
            a_ref[d % 2, d // 2, k * rows : (k + 1) * rows] = jnp.dot(
                table_ref[...], turned[k], precision=precise, preferred_element_type=f32
            )


def x_spread(all_ref, table_ref, slab_ref):
    owners, xl, _, high, lanes = slab_ref.shape
    rows = table_ref.shape[1]
    for d in range(owners):
        parts = [
            jnp.dot(
                table_ref[...],
                all_ref[d % 2, d // 2, k * rows : (k + 1) * rows],
                precision=precise,
                preferred_element_type=f32,
            )
            for k in range(high)
        ]
        turned = jnp.swapaxes(jnp.stack(parts, axis=0), 0, 1)
        slab_ref[d] = turned.reshape(xl, 2, high, lanes)


def spread_weight(weight, turned):
    rows, cols = weight.shape[::-1] if turned else weight.shape

    def match(shape, low, high):
        a = lax.broadcasted_iota(jnp.int32, shape, 0)
        b = lax.broadcasted_iota(jnp.int32, shape, 1)
        return low(a) == high(b)

    tall = match((rows * ROWS, rows), lambda a: a // ROWS, lambda b: b)
    wide = match((cols, cols * ROWS), lambda a: a, lambda b: b // ROWS)
    tall = jnp.where(tall, 1.0, 0.0).astype(bf16)
    wide = jnp.where(wide, 1.0, 0.0).astype(bf16)
    half = (dot_nt if turned else dot)(tall, weight).astype(bf16)
    diagonal = match((rows * ROWS, cols * ROWS), lambda a: a % ROWS, lambda b: b % ROWS)
    return jnp.where(diagonal, dot(half, wide), 0.0).astype(bf16)


def turn(chunk_ref, out_ref):
    steps, high, lanes = out_ref.shape
    out_ref[...] = jnp.swapaxes(chunk_ref[...].reshape(high, steps, lanes), 0, 1)


def multiply(weights, in_ref, res_ref, first, count):
    steps, high, lanes = in_ref.shape
    KX, PL, _, _, C = weights[0].shape
    KY, PK = PL // MZ, MZ // high
    row = lax.broadcasted_iota(jnp.int32, (high, lanes), 0)
    lane = lax.broadcasted_iota(jnp.int32, (high, lanes), 1)
    low = (lane // C) % 2 == 0

    for half, w_ref in enumerate(weights):

        def one(k, carry, half=half, w_ref=w_ref):
            at = 2 * (half * KX + k)
            rest = in_ref[pl.ds(at, 2)]
            pieces = []
            for _ in range(3):
                pieces.append(rest.astype(bf16).astype(f32))
                rest = rest - pieces[-1]
            results = []
            for ky in range(KY):
                rows = [
                    piece[ri][:, (pk * KY + ky) * C : (pk * KY + ky + 1) * C]
                    for piece in pieces
                    for ri in range(2)
                    for pk in range(PK)
                ]
                base = ky * MZ + first * PK
                w = w_ref[k, base : base + count * PK].reshape(count * PK * 2 * C, C)
                terms = dot_nt(jnp.concatenate(rows, axis=0).astype(bf16), w)
                terms = terms.reshape(3, 2, PK, high, count * lanes)
                terms = (terms[2] + terms[1]) + terms[0]
                kept = []
                for ri in range(2):
                    value = None
                    for h in range(count):
                        own = slice(h * lanes, (h + 1) * lanes)
                        here = jnp.where(
                            lane < 2 * C, terms[ri, 0][:, own], terms[ri, 1][:, own]
                        )
                        value = here if value is None else jnp.where(row == first + h, here, value)
                    kept.append(value)
                real, imag = kept
                imag = jnp.where(low, -pltpu.roll(imag, lanes - C, 1), pltpu.roll(imag, C, 1))
                results.append(real + imag)
            one_, two = results
            real = jnp.where(low, one_, pltpu.roll(two, C, 1))
            imag = jnp.where(low, pltpu.roll(one_, lanes - C, 1), two)
            res_ref[at] = jnp.where(row < first, res_ref[at], real)
            res_ref[at + 1] = jnp.where(row < first, res_ref[at + 1], imag)
            return carry

        lax.fori_loop(0, KX, one, 0)


def forward_sum_body(
    xl,
    f_ref, ty_ref, zt_ref, xt_ref, lw_ref, w_ref,
    both_ref, gathered_ref, out_ref,
    slab_ref, wown_ref, woth_ref, chunk_ref, in_ref, res_ref, got_ref, kw_ref, all_ref,
    own_sem, ws, wr, ss, sr, gzs, gzr, gxs, gxr, *scatter
):
    i = pl.program_id(0)
    count = f_ref.shape[1]
    table, core = pair()
    _, z, x = place()
    zn = lax.axis_size("gx") // 2
    steps, high, _ = in_ref.shape
    fetch = pltpu.make_async_copy(w_ref, wown_ref, own_sem)
    swap = pltpu.make_async_remote_copy(
        w_ref, woth_ref, ws, wr, device_id=core, device_id_type=MESH
    )
    half = steps // 2
    cross = pltpu.make_async_remote_copy(
        in_ref.at[pl.ds(half, half)], got_ref, ss, sr, device_id=core, device_id_type=MESH
    )
    total = Scatter(scatter[0], chunk_ref, *scatter[1:])
    along, across = gather_parts(all_ref, gzs, gzr, gxs, gxr)
    rows = high // PIECES

    def mapped(p):
        total.finish(p)
        for h in range(rows * p, rows * (p + 1)):
            in_ref[:, h, :] = chunk_ref[h * steps : (h + 1) * steps]
        multiply((wown_ref, woth_ref), in_ref, res_ref, rows * p, rows)
        for h in range(rows * p, rows * (p + 1)):
            all_ref[x, z, h * steps : (h + 1) * steps] = res_ref[:, h, :]
        for j in (2, 1, 3):
            along(p, j).start()
        across(p, 0).start()

    def passed(p):
        for j in range(1, zn):
            along(p, j).wait_recv()
            across(p, j).start()

    @pl.when(i == 0)
    def _():
        greet(core=True)
        fetch.start()
        swap.start()
        in_ref[...] = jnp.zeros_like(in_ref)
        res_ref[...] = jnp.zeros_like(res_ref)
        kw_ref[...] = spread_weight(lw_ref[...], True)

    @pl.when(i < xl)
    def _():
        store_modes(
            slab_ref.at[:, pl.ds(i, 1)],
            plane_modes(lambda c: f_ref[0, c], count, ty_ref[...], zt_ref[...]),
        )

    @pl.when(i == xl - 1)
    def _():
        x_sum(slab_ref, xt_ref.at[table], scatter[0])
        total.start()

    @pl.when(i >= xl)
    def _():
        for y0 in range(0, f_ref.shape[2], 2 * ROWS):
            put_pair(out_ref, y0, dot(kw_ref[...], tile_pair(f_ref, y0)))

    @pl.when(i == xl + (3 * xl) // 8)
    def _():
        total.forward(0)

    @pl.when(i == xl + (5 * xl) // 8)
    def _():
        total.forward(1)

    @pl.when(i == xl + (7 * xl) // 8)
    def _():
        total.forward(2)
        fetch.wait()
        swap.wait()

    @pl.when(i == 2 * xl - 1)
    def _():
        mapped(0)
        total.forward(3)
        mapped(1)
        mapped(2)
        passed(0)
        mapped(3)
        cross.start()
        for p in range(1, PIECES):
            passed(p)
        total.settle()
        cross.wait()
        both_ref[0] = in_ref[:half]
        both_ref[1] = got_ref[...]
        for p in range(PIECES):
            for j in range(zn):
                across(p, j).wait()
            for j in range(1, zn):
                along(p, j).wait_send()
        gathered_ref[...] = all_ref[...]


def grad_body(
    scale, cells, s_ref, g_ref, sums_ref, e_ref,
    out_ref, gw_ref, gq_ref, loss_ref, copy_ref
):
    _, PL, _, C, _ = out_ref.shape
    _, _, high, lanes = s_ref.shape
    KY, PK = PL // MZ, MZ // high
    copy_ref[...] = e_ref[...]

    @pl.when(pl.program_id(0) == 0)
    def _():
        total = sums_ref[...]
        gw_ref[...] = total[:, :C] * scale
        gq_ref[...] = (total[:, C : C + 8] * scale).T[:3]
        loss_ref[...] = total[:1, C + 3 : C + 4] * (1.0 / cells)

    def pieces(ref):
        high_part, low_part = split(ref[...].reshape(4, high, lanes))
        return high_part.astype(f32), low_part.astype(f32)

    f_high, f_low = pieces(s_ref)
    field = jnp.concatenate([f_high, f_low, f_high], axis=0).reshape(12 * high, lanes)
    field = field.astype(bf16)
    g_high, g_low = pieces(g_ref)
    grads = [g_high, g_high, g_low]
    swapped = [jnp.stack([g[1], -g[0], g[3], -g[2]], axis=0) for g in grads]
    turned = [
        jnp.concatenate(g, axis=0).reshape(12 * high, lanes).T for g in (grads, swapped)
    ]
    lane = lax.broadcasted_iota(jnp.int32, (C, 12 * high), 1) % high
    for pk in range(PK):
        for ky in range(KY):
            at = (pk * KY + ky) * C
            rows = [
                jnp.where(lane == h, turned[n][at : at + C], 0.0).astype(bf16)
                for h in range(high)
                for n in range(2)
            ]
            value = dot(jnp.concatenate(rows, axis=0), field[:, at : at + C])
            for h in range(high):
                for n in range(2):
                    row = (2 * h + n) * C
                    out_ref[0, ky * MZ + h * PK + pk, n] = value[row : row + C]


def tile_pair(ref, y0):
    count, nz = ref.shape[1], ref.shape[3]
    one = ref[0, :, pl.ds(y0, ROWS), :].reshape(count * ROWS, nz)
    two = ref[0, :, pl.ds(y0 + ROWS, ROWS), :].reshape(count * ROWS, nz)
    return jnp.concatenate([one, two], axis=1)


def put_pair(ref, y0, value):
    count, nz = ref.shape[1], ref.shape[3]
    ref[0, :, pl.ds(y0, ROWS), :] = value[:, :nz].reshape(count, ROWS, nz)
    ref[0, :, pl.ds(y0 + ROWS, ROWS), :] = value[:, nz:].reshape(count, ROWS, nz)


def local_body(f_ref, kw_ref, out_ref):
    for y0 in range(0, f_ref.shape[2], 2 * ROWS):
        put_pair(out_ref, y0, dot(kw_ref[...], tile_pair(f_ref, y0)))


def middle_body(scale, l_ref, m_ref, zi_ref, yi_ref, kp_ref, pre_ref, vel_ref):
    count, ny, nz = l_ref.shape[1], l_ref.shape[2], l_ref.shape[3]
    high, low = split(load_modes(m_ref, MY * count))
    wave = dot_tn(jnp.concatenate([high, high, low], axis=0), zi_ref[...])
    turned = jnp.swapaxes(wave.reshape(MY, count, 2 * nz), 0, 1)
    yi = yi_ref[...]
    for o in range(0, count, 2):
        pair = [
            jnp.concatenate([turned[i, :, :nz], turned[i, :, nz:]], axis=0) for i in (o, o + 1)
        ]
        both = dot(yi, jnp.concatenate(pair, axis=1).astype(bf16))
        pre_ref[0, o] = l_ref[0, o] + both[:, :nz] * scale
        pre_ref[0, o + 1] = l_ref[0, o + 1] + both[:, nz:] * scale

    for y0 in range(0, ny, 2 * ROWS):
        x = tile_pair(pre_ref, y0)
        t = jnp.tanh(x * (ROOT + (0.044715 * ROOT) * (x * x)))
        half = 0.5 * x
        hidden = (half + half * t).astype(bf16)
        put_pair(vel_ref, y0, dot(kp_ref[...], hidden))


def backward_body(
    f_ref, pre_ref, gv_ref, ty_ref, zt_ref, kpt_ref, out_ref, gw_ref, gq_ref, gp_ref, first=0
):
    count, ny, nz = f_ref.shape[1], f_ref.shape[2], f_ref.shape[3]

    @pl.when(pl.program_id(0) == first)
    def _():
        gw_ref[...] = jnp.zeros_like(gw_ref)
        gq_ref[...] = jnp.zeros_like(gq_ref)

    hiddens, grads, fields, slopes = [], [], [], []
    for y0 in range(0, ny, 2 * ROWS):
        gv = tile_pair(gv_ref, y0)
        x = tile_pair(pre_ref, y0)
        cubic = (0.044715 * ROOT) * (x * x)
        t = jnp.tanh(x * (ROOT + cubic))
        cdf = 0.5 + 0.5 * t
        hidden = (x * cdf).astype(bf16)
        slope = cdf + (x * (ROOT + 3.0 * cubic)) * (0.5 - 0.5 * (t * t))
        gp = (dot(kpt_ref[...], gv) * slope).astype(bf16)
        put_pair(gp_ref, y0, gp)
        hiddens.append(hidden)
        grads.append(gp)
        slopes.append(gv)
        fields.append(tile_pair(f_ref, y0))
    gw_ref[...] += dot_nt(jnp.concatenate(fields, axis=1), jnp.concatenate(grads, axis=1))
    gq_ref[...] += dot_nt(jnp.concatenate(hiddens, axis=1), jnp.concatenate(slopes, axis=1))

    store_modes(out_ref, plane_modes(lambda c: gp_ref[0, c], count, ty_ref[...], zt_ref[...]))


def fold(total, columns):
    rows, cols = total.shape
    row = lax.broadcasted_iota(jnp.int32, total.shape, 0) % ROWS
    col = lax.broadcasted_iota(jnp.int32, total.shape, 1) % ROWS
    kept = jnp.where(row == col, total, 0.0).reshape(rows // ROWS, ROWS, cols)
    lane = lax.broadcasted_iota(jnp.int32, (cols, 128), 1)
    block = lax.broadcasted_iota(jnp.int32, (cols, 128), 0) // ROWS
    gather = jnp.where(lane == block + columns, 1.0, 0.0)
    return jnp.dot(jnp.sum(kept, axis=1), gather, precision=precise, preferred_element_type=f32)


def gather_parts(all_ref, zs, zr, xs, xr):
    _, z, x = place()
    zn, rows = all_ref.shape[1], all_ref.shape[2]
    step = rows // PIECES

    def along(p, j):
        part = pl.ds(p * step, step)
        return pltpu.make_async_remote_copy(
            all_ref.at[x, z, part],
            all_ref.at[x, z, part],
            zs.at[p, j - 1],
            zr.at[p, j - 1],
            device_id={"gx": lax.rem(z + j, zn) * 2 + x},
            device_id_type=MESH,
        )

    def across(p, j):
        part = pl.ds(p * step, step)
        t = lax.rem(z - j + zn, zn)
        return pltpu.make_async_remote_copy(
            all_ref.at[x, t, part],
            all_ref.at[x, t, part],
            xs.at[p, j],
            xr.at[p, j],
            device_id={"gx": z * 2 + 1 - x},
            device_id_type=MESH,
        )

    return along, across


def inward(m, count):
    odd = m % 2
    return odd * (count - 1 - m // 2) + (1 - odd) * (m // 2)


def step_body(
    scale, xl, rep,
    f_ref, l_ref, all_ref, t_ref, mult_ref, pw_ref, xb_ref, zi_ref, yi_ref,
    ty_ref, zt_ref, xt_ref,
    e_ref, both_ref, sums_ref,
    kp_ref, kpt_ref,
    pre_ref, vel_ref, gv_ref, gp_ref, slab_ref, gw_ref, gq_ref, loss_ref,
    edge_ref, halo_ref, us, ur, ps, pr,
    pack_ref, ebuf, es, er, chunk_ref, turned_ref, got_ref, other_ref, cs, cr, *scatter
):
    i = pl.program_id(0)
    me, z, x = place()
    table, core = pair()
    gx = lax.axis_size("gx")
    right = {"gx": lax.rem(me + 1, gx)}
    left = {"gx": lax.rem(me + gx - 1, gx)}

    def halo(k, sems):
        return pltpu.make_async_remote_copy(
            edge_ref.at[k],
            halo_ref.at[k],
            sems[0].at[k % 2],
            sems[1].at[k % 2],
            device_id=left if k % 2 == 0 else right,
            device_id_type=MESH,
        )

    def penalty(p, before, after):
        u = vel_ref[p, 1], vel_ref[p, 2]
        rows, lanes = u[0].shape
        slope = (after - before) * 0.5
        slope = slope + (pltpu.roll(u[0], rows - 1, 0) - pltpu.roll(u[0], 1, 0)) * 0.5
        slope = slope + (pltpu.roll(u[1], lanes - 1, 1) - pltpu.roll(u[1], 1, 1)) * 0.5
        lam = mult_ref[p].astype(f32) / 64.0
        e_ref[p] = lam + penalty_weight * slope
        add_loss((lam + (0.5 * penalty_weight) * slope) * slope)

    def add_loss(value):
        rows, lanes = value.shape
        loss_ref[...] = loss_ref[...] + jnp.sum(value.reshape(rows // 8, 8, lanes), axis=0)

    @pl.when(i == 0)
    def _():
        loss_ref[...] = jnp.zeros_like(loss_ref)
        greet(True, True)
        kp_ref[...] = spread_weight(pw_ref[...], False)
        kpt_ref[...] = spread_weight(pw_ref[...], True)
        x_spread(all_ref, xb_ref.at[table], slab_ref)

    @pl.when(i < xl)
    def _():
        p = inward(i, xl)
        plane_ref = pre_ref.at[pl.ds(p, 1)]
        modes_ref = slab_ref.at[:, pl.ds(p, 1)]
        middle_body(
            scale, l_ref, modes_ref, zi_ref, yi_ref, kp_ref, plane_ref,
            vel_ref.at[pl.ds(p, 1)],
        )

    @pl.when(i == 1)
    def _():
        edge_ref[0] = vel_ref[0, 0]
        edge_ref[1] = vel_ref[xl - 1, 0]
        for k in (0, 1):
            halo(k, (us, ur)).start()

    @pl.when(i == xl // 2)
    def _():
        for k in (0, 1):
            halo(k, (us, ur)).wait()
        penalty(0, halo_ref[1], vel_ref[1, 0])
        penalty(xl - 1, vel_ref[xl - 2, 0], halo_ref[0])
        edge_ref[2] = e_ref[0]
        edge_ref[3] = e_ref[xl - 1]
        for k in (2, 3):
            halo(k, (ps, pr)).start()

    @pl.when(i == xl - 1)
    def _():
        def one(p, carry):
            penalty(p, vel_ref[p - 1, 0], vel_ref[p + 1, 0])
            return carry

        lax.fori_loop(1, xl - 1, one, 0)
        for k in (2, 3):
            halo(k, (ps, pr)).wait()

    @pl.when(i >= xl)
    def _():
        p = i - xl
        e = e_ref[p]
        rows, lanes = e.shape
        before = lax.select(
            jnp.broadcast_to(p == 0, e.shape), halo_ref[3], e_ref[lax.rem(p + xl - 1, xl)]
        )
        after = lax.select(
            jnp.broadcast_to(p == xl - 1, e.shape), halo_ref[2], e_ref[lax.rem(p + 1, xl)]
        )
        slopes = (
            (after - before) * 0.5,
            (pltpu.roll(e, rows - 1, 0) - pltpu.roll(e, 1, 0)) * 0.5,
            (pltpu.roll(e, lanes - 1, 1) - pltpu.roll(e, 1, 1)) * 0.5,
        )
        for j in range(3):
            misfit = vel_ref[p, j] - t_ref[0, j].astype(f32)
            add_loss(misfit * misfit)
            gv_ref[0, j] = ((2.0 * misfit - slopes[j]) / rep).astype(bf16)
        backward_body(
            f_ref, pre_ref.at[pl.ds(p, 1)], gv_ref, ty_ref, zt_ref, kpt_ref,
            slab_ref.at[:, pl.ds(p, 1)], gw_ref, gq_ref, gp_ref, first=xl,
        )

    @pl.when(i == pl.num_programs(0) - 1)
    def _():
        x_sum(slab_ref, xt_ref.at[table], scatter[0])
        count = f_ref.shape[1]
        lane = lax.broadcasted_iota(jnp.int32, (count, 128), 1)
        pack_ref[...] = (
            fold(gw_ref[...], 0)
            + fold(gq_ref[...], count)
            + jnp.where(lane == count + 3, jnp.sum(loss_ref[...]), 0.0)
        )
        scatter_sum(Scatter(scatter[0], chunk_ref, *scatter[1:]), pack_ref, ebuf, es, er)
        turn(chunk_ref, turned_ref)
        half = turned_ref.shape[0] // 2
        copies = [
            send(turned_ref.at[pl.ds(half, half)], got_ref, (cs.at[0], cr.at[0]), core),
            send(pack_ref, other_ref, (cs.at[1], cr.at[1]), core),
        ]
        for copy in copies:
            copy.wait()
        both_ref[0] = turned_ref[:half]
        both_ref[1] = got_ref[...]
        sums_ref[...] = pack_ref[...] + other_ref[...]


def whole(shape):
    return pl.BlockSpec(shape, lambda i: (0,) * len(shape))


def plane(shape):
    return pl.BlockSpec((1,) + tuple(shape), lambda i: (i,) + (0,) * len(shape))


params = pltpu.CompilerParams(
    dimension_semantics=("arbitrary",), vmem_limit_bytes=56 * 1024 * 1024
)


def extended(value, axis_name):
    count = lax.axis_size(axis_name)
    up = [(i, (i + 1) % count) for i in range(count)]
    down = [(j, i) for i, j in up]
    before = lax.ppermute(value[-1:], axis_name, up)
    after = lax.ppermute(value[:1], axis_name, down)
    return jnp.concatenate([before, value, after], axis=0)


def central(values, axis):
    return (jnp.roll(values, -1, axis) - jnp.roll(values, 1, axis)) * 0.5


def local(fields, targets, multipliers, local_weight, proj_weight, spectral_weight):
    gx = lax.axis_size("gx")
    rep = lax.axis_size("rep")
    _, xl, C, NY, NZ = fields.shape
    NX = xl * gx
    PL = MY * MZ // gx
    scale = 1.0 / math.sqrt(NX * NY * NZ)
    fields, targets, multipliers = fields[0], targets[0], multipliers[0]

    cos_y, sin_y = fourier_tables(NY, MY)
    ty = jnp.asarray(np.concatenate([cos_y.T, -sin_y.T], 0).astype(ml_dtypes.bfloat16))
    yi = jnp.asarray(np.concatenate([cos_y, -sin_y], 1).astype(ml_dtypes.bfloat16))
    cos_z, sin_z = fourier_tables(NZ, MZ)
    zt = np.concatenate(
        [np.concatenate([cos_z.T, sin_z.T], 1), np.concatenate([-sin_z.T, cos_z.T], 1)], 0
    )
    direct = gx == 8 and rep == 2 and C == 32
    KY = MY // gx if direct else 0
    PK = 128 // (KY * C) if direct else 1
    HZ = MZ // PK
    order = np.arange(2 * MZ).reshape(2, HZ, PK).transpose(2, 0, 1).reshape(-1)
    zt = zt[order]
    zi_high, zi_low = halves(zt)
    zt = jnp.asarray(np.concatenate([zi_high, zi_low], 0))
    zi = jnp.asarray(np.concatenate([zi_high, zi_low, zi_high], 0))
    cos_x, sin_x = fourier_tables(NX, MX)
    xt = np.stack(
        [np.stack([cos_x.T, sin_x.T], 1), np.stack([-sin_x.T, cos_x.T], 1)], 1
    )
    xt = xt.reshape(MX, 2, 2, gx, xl).transpose((0, 1, 3, 4, 2) if direct else (0, 1, 3, 2, 4))
    xt = xt.reshape(2 * MX, 2 * NX)
    x_forward = jnp.asarray(xt * np.float32(scale))
    x_back = jnp.asarray(np.ascontiguousarray(xt.T))

    def spread(weight):
        rows, columns = weight.shape
        left = jnp.asarray(np.kron(np.eye(rows), np.ones((ROWS, 1))), dtype=bf16)
        right = jnp.asarray(np.kron(np.eye(columns), np.ones((1, ROWS))), dtype=bf16)
        diagonal = jnp.asarray(np.kron(np.ones((rows, columns)), np.eye(ROWS)), dtype=bf16)
        return dot(dot(left, weight).astype(bf16), right).astype(bf16) * diagonal

    kw = spread(local_weight.T)
    kp = spread(proj_weight.T)
    kpt = spread(proj_weight)

    field_spec = plane((C, NY, NZ))
    modes_shape = jax.ShapeDtypeStruct((xl, 2 * MZ, MY * C), f32)
    modes_spec = plane((2 * MZ, MY * C))
    vel_spec = plane((3, NY, NZ))

    def to_owner(slab):
        slab = slab.reshape(xl, 2, MZ, MY, C).transpose(3, 2, 1, 0, 4)
        slab = slab.reshape(gx, PL, 2, xl, C).transpose(0, 2, 3, 1, 4)
        slab = slab.reshape(gx, 2 * xl, PL * C)
        slab = lax.all_to_all(slab, "gx", split_axis=0, concat_axis=0, tiled=True)
        out = jnp.dot(x_forward, slab.reshape(2 * NX, PL * C), precision=precise)
        return out.reshape(MX, 2, PL, C)

    def to_planes(modes):
        out = jnp.dot(x_back, modes.reshape(2 * MX, PL * C), precision=precise)
        out = out.reshape(gx, 2 * xl, PL * C)
        out = lax.all_to_all(out, "gx", split_axis=0, concat_axis=0, tiled=True)
        out = out.reshape(gx, 2, xl, PL, C).transpose(0, 3, 1, 2, 4)
        out = out.reshape(MY, MZ, 2, xl, C).transpose(3, 2, 1, 0, 4)
        return out.reshape(xl, 2 * MZ, MY * C)

    def both_samples(modes):
        part = modes.reshape(rep, MX // rep, 2, PL, C)
        return lax.all_to_all(part, "rep", split_axis=0, concat_axis=0, tiled=True)

    ZN = gx // 2
    QR = HZ * 2 * MX
    slab_scratch = pltpu.VMEM((gx, xl, 2, HZ, 128), f32)
    dma = pltpu.SemaphoreType.DMA

    def comm(number):
        return pltpu.CompilerParams(
            dimension_semantics=("arbitrary",),
            vmem_limit_bytes=60 * 1024 * 1024,
            collective_id=number,
            has_side_effects=True,
        )

    if direct:
        parts = xt.reshape(rep, MX, gx, 2 * xl)
        parts = np.stack([np.concatenate([parts[r], parts[1 - r]], 0) for r in range(rep)])
        parts = parts.transpose(0, 2, 1, 3).reshape(rep * gx, 2 * MX, 2 * xl)
        x_own = jnp.asarray(parts * np.float32(scale))
        x_out = jnp.asarray(np.ascontiguousarray(parts.transpose(0, 2, 1)))
        chunk_shape = jax.ShapeDtypeStruct((QR, 128), f32)
        weight_scratch = pltpu.VMEM(spectral_weight.shape, bf16)
        row_scratch = pltpu.VMEM((2 * MX, HZ, 128), f32)
        both_shape = jax.ShapeDtypeStruct((2, MX, HZ, 128), f32)
        half_scratch = pltpu.VMEM((MX, HZ, 128), f32)
        gathered_shape = jax.ShapeDtypeStruct((2, ZN, QR, 128), f32)
        wide = C * ROWS
        spectrum, gathered, mapped = pl.pallas_call(
            functools.partial(forward_sum_body, xl),
            grid=(2 * xl,),
            out_shape=(
                both_shape,
                gathered_shape,
                jax.ShapeDtypeStruct((xl, C, NY, NZ), f32),
            ),
            in_specs=[
                pl.BlockSpec((1, C, NY, NZ), lambda i: (i % xl, 0, 0, 0)),
                whole(ty.shape),
                whole(zt.shape),
                whole(x_own.shape),
                whole((C, C)),
                pl.BlockSpec(memory_space=pl.ANY),
            ],
            out_specs=(
                whole(both_shape.shape),
                whole(gathered_shape.shape),
                pl.BlockSpec((1, C, NY, NZ), lambda i: ((i % xl) * (i // xl), 0, 0, 0)),
            ),
            scratch_shapes=[slab_scratch, weight_scratch, weight_scratch]
            + [pltpu.VMEM((QR, 128), f32), row_scratch, row_scratch, half_scratch]
            + [pltpu.VMEM((wide, wide), bf16), pltpu.VMEM(gathered_shape.shape, f32)]
            + [dma] * 5
            + [dma((PIECES, ZN - 1))] * 2
            + [dma((PIECES, ZN))] * 2
            + scatter_scratch(ZN, QR),
            compiler_params=comm(1),
        )(fields, ty, zt, x_own, local_weight, spectral_weight)
    else:
        slab = pl.pallas_call(
            forward_body,
            grid=(xl,),
            out_shape=modes_shape,
            in_specs=[field_spec, whole(ty.shape), whole(zt.shape)],
            out_specs=modes_spec,
            compiler_params=params,
        )(fields, ty, zt)
        mapped = pl.pallas_call(
            local_body,
            grid=(xl,),
            out_shape=jax.ShapeDtypeStruct((xl, C, NY, NZ), f32),
            in_specs=[field_spec, whole(kw.shape)],
            out_specs=field_spec,
            compiler_params=pltpu.CompilerParams(vmem_limit_bytes=20 * 1024 * 1024),
        )(fields, kw)
    middle_shape = (
        jax.ShapeDtypeStruct((xl, C, NY, NZ), f32),
        jax.ShapeDtypeStruct((xl, 3, NY, NZ), f32),
    )
    wide = C * ROWS
    if direct:
        tables = [proj_weight.T, x_out, zi, yi, ty, zt, x_own]

        def once(shape):
            return pl.BlockSpec(
                shape, lambda i: (0,) * len(shape), pipeline_mode=pl.Buffered(1)
            )

        penalty, chunk, sums = pl.pallas_call(
            functools.partial(step_body, scale, xl, rep),
            grid=(2 * xl,),
            out_shape=(
                jax.ShapeDtypeStruct((xl, NY, NZ), f32),
                both_shape,
                jax.ShapeDtypeStruct((C, 128), f32),
            ),
            in_specs=[
                pl.BlockSpec(
                    (1, C, NY, NZ),
                    lambda i: ((i % xl) * (i // xl), 0, 0, 0),
                ),
                pl.BlockSpec(
                    (1, C, NY, NZ),
                    lambda i: (
                        inward(i % xl, xl) * (1 - i // xl) + inward(xl - 1, xl) * (i // xl),
                        0,
                        0,
                        0,
                    ),
                ),
                once(gathered_shape.shape),
                pl.BlockSpec((1, 3, NY, NZ), lambda i: ((i % xl) * (i // xl), 0, 0, 0)),
                once((xl, NY, NZ)),
            ]
            + [once(t.shape) for t in tables],
            out_specs=(whole((xl, NY, NZ)), whole(both_shape.shape), whole((C, 128))),
            scratch_shapes=[
                pltpu.VMEM((3 * ROWS, wide), bf16),
                pltpu.VMEM((wide, 3 * ROWS), bf16),
                pltpu.VMEM((xl, C, NY, NZ), f32),
                pltpu.VMEM((xl, 3, NY, NZ), f32),
                pltpu.VMEM((1, 3, NY, NZ), bf16),
                pltpu.VMEM((1, C, NY, NZ), bf16),
                slab_scratch,
                pltpu.VMEM((wide, wide), f32),
                pltpu.VMEM((wide, 3 * ROWS), f32),
                pltpu.VMEM((8, NZ), f32),
                pltpu.VMEM((4, NY, NZ), f32),
                pltpu.VMEM((4, NY, NZ), f32),
            ]
            + [dma((2,))] * 4
            + [pltpu.VMEM((C, 128), f32), pltpu.VMEM((ZN, C, 128), f32), dma((ZN,)), dma((ZN,))]
            + [pltpu.VMEM((QR, 128), f32), row_scratch, half_scratch]
            + [pltpu.VMEM((C, 128), f32), dma((2,)), dma((2,))]
            + scatter_scratch(ZN, QR),
            compiler_params=comm(2),
        )(fields, mapped, gathered, targets, multipliers, *tables)
        KX = MX // rep
        modes_of = pl.BlockSpec((2, 2, HZ, 128), lambda i: (0, i, 0, 0))
        planes = pl.BlockSpec((xl // KX, NY, NZ), lambda i: (i, 0, 0))
        grad_r, grad_w, grad_q, loss, penalty = pl.pallas_call(
            functools.partial(grad_body, scale, rep * NX * NY * NZ),
            grid=(KX,),
            out_shape=(
                jax.ShapeDtypeStruct(spectral_weight.shape, f32),
                jax.ShapeDtypeStruct((C, C), f32),
                jax.ShapeDtypeStruct((3, C), f32),
                jax.ShapeDtypeStruct((1, 1), f32),
                jax.ShapeDtypeStruct(penalty.shape, f32),
            ),
            in_specs=[modes_of, modes_of, whole((C, 128)), planes],
            out_specs=(
                plane((PL, 2, C, C)),
                whole((C, C)),
                whole((3, C)),
                whole((1, 1)),
                planes,
            ),
            compiler_params=params,
        )(spectrum, chunk, sums, penalty)
        return (penalty[None], grad_r, grad_w, grad_q.T, loss[0])
    else:
        weights = spectral_weight
        weights = weights.transpose(2, 3, 4, 0, 1).reshape(1, 2, C, C, MX // rep * PL)
        weights = lax.all_gather(weights, "rep", axis=0, tiled=True)
        spectrum = to_owner(slab)
        KX = MX // rep
        turned = spectrum.reshape(rep, KX, 2, PL, C).transpose(0, 2, 4, 1, 3)
        turned = turned.reshape(rep, 2, 1, C, KX * PL)
        w_re, w_im = weights[:, 0].astype(f32), weights[:, 1].astype(f32)
        s_re, s_im = turned[:, 0], turned[:, 1]
        product = jnp.stack(
            [jnp.sum(w_re * s_re - w_im * s_im, axis=2), jnp.sum(w_re * s_im + w_im * s_re, axis=2)],
            axis=1,
        )
        product = product.reshape(rep, 2, C, KX, PL).transpose(0, 3, 1, 4, 2)
        product = product.reshape(MX, 2, PL, C)
        spectra = both_samples(spectrum)
        wave = to_planes(product)
        pre, velocity = pl.pallas_call(
            functools.partial(middle_body, scale),
            grid=(xl,),
            out_shape=middle_shape,
            in_specs=[field_spec, modes_spec, whole(zi.shape), whole(yi.shape), whole(kp.shape)],
            out_specs=(field_spec, vel_spec),
            compiler_params=params,
        )(mapped, wave, zi, yi, kp)
        padded = extended(velocity[:, 0].astype(bf16), "gx").astype(f32)
        slope_x = (padded[2:] - padded[:-2]) * 0.5
        divergence = slope_x + central(velocity[:, 1], 1) + central(velocity[:, 2], 2)
        lam = multipliers.astype(f32) / 64.0
        penalty = lam + penalty_weight * divergence
        misfit = velocity - targets.astype(f32)
        loss_sum = (
            jnp.sum(misfit * misfit)
            + jnp.sum(lam * divergence)
            + 0.5 * penalty_weight * jnp.sum(divergence * divergence)
        )
        padded = extended(penalty.astype(bf16), "gx").astype(f32)
        pen_x = (padded[2:] - padded[:-2]) * 0.5
        slopes = jnp.stack([pen_x, central(penalty, 1), central(penalty, 2)], axis=1)
        grad_vel = ((2.0 * misfit - slopes) / rep).astype(bf16)
        grad_slab, gw, gq = pl.pallas_call(
            backward_body,
            grid=(xl,),
            out_shape=(
                modes_shape,
                jax.ShapeDtypeStruct((wide, wide), f32),
                jax.ShapeDtypeStruct((wide, 3 * ROWS), f32),
            ),
            in_specs=[field_spec, field_spec, vel_spec]
            + [whole(ty.shape), whole(zt.shape), whole(kpt.shape)],
            out_specs=(modes_spec, whole((wide, wide)), whole((wide, 3 * ROWS))),
            scratch_shapes=[pltpu.VMEM((1, C, NY, NZ), bf16)],
            compiler_params=params,
        )(fields, pre, grad_vel, ty, zt, kpt)
        gather = jnp.asarray(np.kron(np.eye(C), np.ones((1, ROWS))).astype(np.float32))
        gather_q = jnp.asarray(np.kron(np.eye(3), np.ones((ROWS, 1))).astype(np.float32))
        mask = jnp.asarray(np.kron(np.ones((C, C)), np.eye(ROWS)).astype(np.float32))
        mask_q = jnp.asarray(np.kron(np.ones((C, 3)), np.eye(ROWS)).astype(np.float32))
        grad_w = jnp.dot(gather, gw * mask, precision=precise)
        grad_w = jnp.dot(grad_w, gather.T, precision=precise)
        grad_q = jnp.dot(gather, gq * mask_q, precision=precise)
        grad_q = jnp.dot(grad_q, gather_q, precision=precise)
        grads = both_samples(to_owner(grad_slab))
        packed = jnp.concatenate([grad_w.reshape(-1), grad_q.reshape(-1), loss_sum.reshape(1)])
        packed = lax.psum(packed, ("gx", "rep"))
        grad_w = packed[: C * C].reshape(C, C)
        grad_q = packed[C * C : C * C + 3 * C].reshape(C, 3)
        loss = packed[-1:]
    loss = loss / (rep * NX * NY * NZ)

    g_re, g_im = grads[:, :, 0], grads[:, :, 1]
    across = jnp.stack([jnp.stack([g_re, g_im], 3), jnp.stack([g_im, -g_re], 3)], 1)
    terms = [
        across[b, t][..., None] * spectra[b, :, t][:, :, None, None, :]
        for b in range(rep)
        for t in range(2)
    ]
    grad_r = sum(terms[1:], terms[0])
    return (penalty[None], grad_r, grad_w * scale, grad_q * scale, loss)


def solution(mesh):
    in_specs = (
        P(("grp", "rep"), "gx", None, None, None),
        P(("grp", "rep"), "gx", None, None, None),
        P(("grp", "rep"), "gx", None, None),
        P(),
        P(),
        P("rep", "gx", None, None, None),
    )
    out_specs = (
        P(("grp", "rep"), "gx", None, None),
        P(("grp", "rep"), "gx", None, None, None),
        P("grp", None),
        P("grp", None),
        P("grp"),
    )
    return jax.shard_map(local, mesh=mesh, in_specs=in_specs, out_specs=out_specs, check_vma=False)
```

```python
import functools
import math

import jax
import jax.numpy as jnp
import ml_dtypes
import numpy as np
from jax import lax
from jax.experimental import pallas as pl
from jax.experimental.pallas import tpu as pltpu
from jax.sharding import PartitionSpec as P

MX = 16
MY = 16
MZ = 16
ROWS = 16

penalty_weight = 0.5
precise = lax.Precision.HIGHEST
bf16 = jnp.bfloat16
f32 = jnp.float32
ROOT = math.sqrt(2.0 / math.pi)


def fourier_tables(length, count):
    position = np.arange(count)
    modes = np.where(position < count // 2, position, position - count)
    phase = np.mod(np.arange(length)[:, None] * modes[None, :], length)
    angle = phase.astype(np.float32) * np.float32(2.0 * math.pi / length)
    return np.cos(angle), np.sin(angle)


def halves(table):
    high = table.astype(ml_dtypes.bfloat16)
    low = (table - high.astype(np.float32)).astype(ml_dtypes.bfloat16)
    return high, low


def split(value):
    high = value.astype(bf16)
    return high, (value - high.astype(f32)).astype(bf16)


def dot(a, b):
    return jnp.dot(a, b, preferred_element_type=f32)


def dot_nt(a, b):
    return lax.dot_general(a, b, (((1,), (1,)), ((), ())), preferred_element_type=f32)


def dot_tn(a, b):
    return lax.dot_general(a, b, (((0,), (0,)), ((), ())), preferred_element_type=f32)


def plane_modes(load, count, ty, zt):
    parts = []
    for c in range(0, count, 2):
        pair = dot(ty, jnp.concatenate([load(c), load(c + 1)], axis=1))
        nz = pair.shape[1] // 2
        parts += [pair[:, :nz], pair[:, nz:]]
    turned = jnp.swapaxes(jnp.stack(parts, axis=0), 0, 1)
    real = turned[:MY].reshape(MY * count, nz)
    imag = turned[MY:].reshape(MY * count, nz)
    high, low = split(jnp.concatenate([real, imag], axis=1))
    both = dot_nt(zt, high)
    n = 2 * MZ
    return both[:n] + both[n:] + dot_nt(zt[:n], low)


def store_modes(out_ref, modes):
    if len(out_ref.shape) == 3:
        out_ref[0] = modes
        return
    owners, _, _, high, lanes = out_ref.shape
    width = modes.shape[1] // owners
    rows = 2 * high
    for d in range(owners):
        parts = [
            modes[j * rows : (j + 1) * rows, d * width : (d + 1) * width]
            for j in range(lanes // width)
        ]
        out_ref[d, 0] = jnp.concatenate(parts, axis=1).reshape(2, high, lanes)


def load_modes(m_ref, columns):
    if len(m_ref.shape) == 3:
        return m_ref[0]
    owners, _, _, high, lanes = m_ref.shape
    width = columns // owners
    blocks = [m_ref[d, 0].reshape(2 * high, lanes) for d in range(owners)]
    rows = [
        jnp.concatenate([block[:, j * width : (j + 1) * width] for block in blocks], axis=1)
        for j in range(lanes // width)
    ]
    return jnp.concatenate(rows, axis=0)


def forward_body(f_ref, ty_ref, zt_ref, out_ref):
    count = f_ref.shape[1]
    store_modes(out_ref, plane_modes(lambda c: f_ref[0, c], count, ty_ref[...], zt_ref[...]))


MESH = pl.DeviceIdType.MESH
PIECES = 4


def place():
    me = lax.axis_index("gx")
    return me, me // 2, lax.rem(me, 2)


def pair():
    r = lax.axis_index("rep")
    return r * lax.axis_size("gx") + lax.axis_index("gx"), {"rep": 1 - r}


def greet(ring=False, core=False):
    _, z, x = place()
    zn = lax.axis_size("gx") // 2
    barrier = pltpu.get_barrier_semaphore()
    pl.semaphore_signal(barrier, inc=1, device_id={"gx": z * 2 + 1 - x}, device_id_type=MESH)
    for j in range(1, zn):
        t = lax.rem(z + j, zn)
        pl.semaphore_signal(barrier, inc=1, device_id={"gx": t * 2 + x}, device_id_type=MESH)
    if ring:
        me = z * 2 + x
        t = lax.rem(me + 2 * x - 1 + 2 * zn, 2 * zn)
        pl.semaphore_signal(barrier, inc=1, device_id={"gx": t}, device_id_type=MESH)
    if core:
        pl.semaphore_signal(barrier, inc=1, device_id=pair()[1], device_id_type=MESH)
    pl.semaphore_wait(barrier, zn + (1 if ring else 0) + (1 if core else 0))


def send(src, dst, sems, where):
    copy = pltpu.make_async_remote_copy(
        src, dst, sems[0], sems[1], device_id=where, device_id_type=MESH
    )
    copy.start()
    return copy


class Scatter:
    def __init__(self, a_ref, o_ref, xbuf, sbuf, zbuf, xs, xr, zs, zr):
        self.refs = a_ref, o_ref, xbuf, sbuf, zbuf
        self.sems = xs, xr, zs, zr
        _, self.z, self.x = place()
        self.zn = a_ref.shape[1]
        self.step = a_ref.shape[2] // PIECES
        self.to_x = {"gx": self.z * 2 + 1 - self.x}

    def part(self, p):
        return pl.ds(p * self.step, self.step)

    def copy(self, src, dst, sems, where):
        return pltpu.make_async_remote_copy(
            src, dst, sems[0], sems[1], device_id=where, device_id_type=MESH
        )

    def across(self, p):
        a_ref, _, xbuf, _, _ = self.refs
        xs, xr, _, _ = self.sems
        return self.copy(
            a_ref.at[1 - self.x, :, self.part(p)], xbuf.at[p], (xs.at[p], xr.at[p]), self.to_x
        )

    def along(self, p, j):
        _, _, _, sbuf, zbuf = self.refs
        _, _, zs, zr = self.sems
        t = lax.rem(self.z + j, self.zn)
        return self.copy(
            sbuf.at[p, j - 1],
            zbuf.at[p, j - 1],
            (zs.at[p, j - 1], zr.at[p, j - 1]),
            {"gx": t * 2 + self.x},
        )

    def start(self):
        for p in range(PIECES):
            self.across(p).start()

    def forward(self, p):
        a_ref, o_ref, xbuf, sbuf, _ = self.refs
        self.across(p).wait_recv()
        for j in (2, 1, 3):
            t = lax.rem(self.z + j, self.zn)
            sbuf[p, j - 1] = a_ref[self.x, t, self.part(p)] + xbuf[p, t]
            self.along(p, j).start()
        o_ref[self.part(p)] = a_ref[self.x, self.z, self.part(p)] + xbuf[p, self.z]

    def finish(self, p):
        _, o_ref, _, _, zbuf = self.refs
        for j in range(1, self.zn):
            self.along(p, j).wait_recv()
        total = (zbuf[p, 0] + zbuf[p, 1]) + zbuf[p, 2]
        o_ref[self.part(p)] = o_ref[self.part(p)] + total

    def settle(self):
        for p in range(PIECES):
            self.across(p).wait_send()
            for j in range(1, self.zn):
                self.along(p, j).wait_send()


def scatter_sum(scatter, e_ref, ebuf, es, er):
    z, x, zn = scatter.z, scatter.x, scatter.zn
    swap = send(e_ref, ebuf.at[0], (es.at[0], er.at[0]), scatter.to_x)
    scatter.start()
    swap.wait()
    e_ref[...] = e_ref[...] + ebuf[0]
    spread = [
        send(e_ref, ebuf.at[j], (es.at[j], er.at[j]), {"gx": lax.rem(z + j, zn) * 2 + x})
        for j in range(1, zn)
    ]
    for p in range(PIECES):
        scatter.forward(p)
    for p in range(PIECES):
        scatter.finish(p)
    scatter.settle()
    for copy in spread:
        copy.wait()
    e_ref[...] = (e_ref[...] + ebuf[1]) + (ebuf[2] + ebuf[3])


def scatter_scratch(zn, rows):
    step = rows // PIECES
    dma = pltpu.SemaphoreType.DMA
    return [
        pltpu.VMEM((2, zn, rows, 128), f32),
        pltpu.VMEM((PIECES, zn, step, 128), f32),
        pltpu.VMEM((PIECES, zn - 1, step, 128), f32),
        pltpu.VMEM((PIECES, zn - 1, step, 128), f32),
        dma((PIECES,)),
        dma((PIECES,)),
        dma((PIECES, zn - 1)),
        dma((PIECES, zn - 1)),
    ]


def x_sum(slab_ref, table_ref, a_ref):
    owners, xl, _, high, lanes = slab_ref.shape
    rows = table_ref.shape[0]
    for d in range(owners):
        turned = jnp.swapaxes(slab_ref[d].reshape(2 * xl, high, lanes), 0, 1)
        for k in range(high):
            a_ref[d % 2, d // 2, k * rows : (k + 1) * rows] = jnp.dot(
                table_ref[...], turned[k], precision=precise, preferred_element_type=f32
            )


def x_spread(all_ref, table_ref, slab_ref):
    owners, xl, _, high, lanes = slab_ref.shape
    rows = table_ref.shape[1]
    for d in range(owners):
        parts = [
            jnp.dot(
                table_ref[...],
                all_ref[d % 2, d // 2, k * rows : (k + 1) * rows],
                precision=precise,
                preferred_element_type=f32,
            )
            for k in range(high)
        ]
        turned = jnp.swapaxes(jnp.stack(parts, axis=0), 0, 1)
        slab_ref[d] = turned.reshape(xl, 2, high, lanes)


def spread_weight(weight, turned):
    rows, cols = weight.shape[::-1] if turned else weight.shape

    def match(shape, low, high):
        a = lax.broadcasted_iota(jnp.int32, shape, 0)
        b = lax.broadcasted_iota(jnp.int32, shape, 1)
        return low(a) == high(b)

    tall = match((rows * ROWS, rows), lambda a: a // ROWS, lambda b: b)
    wide = match((cols, cols * ROWS), lambda a: a, lambda b: b // ROWS)
    tall = jnp.where(tall, 1.0, 0.0).astype(bf16)
    wide = jnp.where(wide, 1.0, 0.0).astype(bf16)
    half = (dot_nt if turned else dot)(tall, weight).astype(bf16)
    diagonal = match((rows * ROWS, cols * ROWS), lambda a: a % ROWS, lambda b: b % ROWS)
    return jnp.where(diagonal, dot(half, wide), 0.0).astype(bf16)


def turn(chunk_ref, out_ref):
    steps, high, lanes = out_ref.shape
    out_ref[...] = jnp.swapaxes(chunk_ref[...].reshape(high, steps, lanes), 0, 1)


def multiply(weights, in_ref, res_ref, first, count):
    steps, high, lanes = in_ref.shape
    KX, PL, _, _, C = weights[0].shape
    KY, PK = PL // MZ, MZ // high
    row = lax.broadcasted_iota(jnp.int32, (high, lanes), 0)
    lane = lax.broadcasted_iota(jnp.int32, (high, lanes), 1)
    low = (lane // C) % 2 == 0

    for half, w_ref in enumerate(weights):

        def one(k, half=half, w_ref=w_ref):
            at = 2 * (half * KX + k)
            rest = in_ref[at : at + 2]
            pieces = []
            for _ in range(3):
                pieces.append(rest.astype(bf16).astype(f32))
                rest = rest - pieces[-1]
            results = []
            for ky in range(KY):
                rows = [
                    piece[ri][:, (pk * KY + ky) * C : (pk * KY + ky + 1) * C]
                    for piece in pieces
                    for ri in range(2)
                    for pk in range(PK)
                ]
                base = ky * MZ + first * PK
                w = w_ref[k, base : base + count * PK].reshape(count * PK * 2 * C, C)
                terms = dot_nt(jnp.concatenate(rows, axis=0).astype(bf16), w)
                terms = terms.reshape(3, 2, PK, high, count * lanes)
                terms = (terms[2] + terms[1]) + terms[0]
                kept = []
                for ri in range(2):
                    value = None
                    for h in range(count):
                        own = slice(h * lanes, (h + 1) * lanes)
                        here = jnp.where(
                            lane < 2 * C, terms[ri, 0][:, own], terms[ri, 1][:, own]
                        )
                        value = here if value is None else jnp.where(row == first + h, here, value)
                    kept.append(value)
                real, imag = kept
                imag = jnp.where(low, -pltpu.roll(imag, lanes - C, 1), pltpu.roll(imag, C, 1))
                results.append(real + imag)
            one_, two = results
            real = jnp.where(low, one_, pltpu.roll(two, C, 1))
            imag = jnp.where(low, pltpu.roll(one_, lanes - C, 1), two)
            res_ref[at] = jnp.where(row < first, res_ref[at], real)
            res_ref[at + 1] = jnp.where(row < first, res_ref[at + 1], imag)

        for k in range(KX):
            one(k)


def forward_sum_body(
    xl,
    f_ref, ty_ref, zt_ref, xt_ref, lw_ref, w_ref,
    both_ref, gathered_ref, out_ref,
    slab_ref, wown_ref, woth_ref, chunk_ref, in_ref, res_ref, got_ref, kw_ref, all_ref,
    own_sem, ws, wr, ss, sr, gzs, gzr, gxs, gxr, *scatter
):
    i = pl.program_id(0)
    count = f_ref.shape[1]
    table, core = pair()
    _, z, x = place()
    zn = lax.axis_size("gx") // 2
    steps, high, _ = in_ref.shape
    fetch = pltpu.make_async_copy(w_ref, wown_ref, own_sem)
    swap = pltpu.make_async_remote_copy(
        w_ref, woth_ref, ws, wr, device_id=core, device_id_type=MESH
    )
    half = steps // 2
    cross = pltpu.make_async_remote_copy(
        in_ref.at[pl.ds(half, half)], got_ref, ss, sr, device_id=core, device_id_type=MESH
    )
    total = Scatter(scatter[0], chunk_ref, *scatter[1:])
    along, across = gather_parts(all_ref, gzs, gzr, gxs, gxr)
    rows = high // PIECES

    def mapped(p):
        total.finish(p)
        for h in range(rows * p, rows * (p + 1)):
            in_ref[:, h, :] = chunk_ref[h * steps : (h + 1) * steps]
        multiply((wown_ref, woth_ref), in_ref, res_ref, rows * p, rows)
        for h in range(rows * p, rows * (p + 1)):
            all_ref[x, z, h * steps : (h + 1) * steps] = res_ref[:, h, :]
        for j in (2, 1, 3):
            along(p, j).start()
        across(p, 0).start()

    def passed(p):
        for j in range(1, zn):
            along(p, j).wait_recv()
            across(p, j).start()

    @pl.when(i == 0)
    def _():
        greet(core=True)
        fetch.start()
        swap.start()
        in_ref[...] = jnp.zeros_like(in_ref)
        res_ref[...] = jnp.zeros_like(res_ref)
        kw_ref[...] = spread_weight(lw_ref[...], True)

    @pl.when(i < xl)
    def _():
        store_modes(
            slab_ref.at[:, pl.ds(i, 1)],
            plane_modes(lambda c: f_ref[0, c], count, ty_ref[...], zt_ref[...]),
        )

    @pl.when(i == xl - 1)
    def _():
        x_sum(slab_ref, xt_ref.at[table], scatter[0])
        total.start()

    @pl.when(i >= xl)
    def _():
        for y0 in range(0, f_ref.shape[2], 2 * ROWS):
            put_pair(out_ref, y0, dot(kw_ref[...], tile_pair(f_ref, y0)))

    @pl.when(i == xl + (3 * xl) // 16)
    def _():
        total.forward(0)

    @pl.when(i == xl + (5 * xl) // 16)
    def _():
        total.forward(1)

    @pl.when(i == xl + (7 * xl) // 16)
    def _():
        total.forward(2)
        fetch.wait()
        swap.wait()
        mapped(0)

    @pl.when(i == xl + (10 * xl) // 16)
    def _():
        total.forward(3)
        mapped(1)

    @pl.when(i == 2 * xl - 1)
    def _():
        mapped(2)
        passed(0)
        mapped(3)
        cross.start()
        for p in range(1, PIECES):
            passed(p)
        total.settle()
        cross.wait()
        both_ref[0] = in_ref[:half]
        both_ref[1] = got_ref[...]
        for p in range(PIECES):
            for j in range(zn):
                across(p, j).wait()
            for j in range(1, zn):
                along(p, j).wait_send()
        gathered_ref[...] = all_ref[...]


def grad_body(
    scale, cells, s_ref, g_ref, sums_ref, e_ref,
    out_ref, gw_ref, gq_ref, loss_ref, copy_ref
):
    _, PL, _, C, _ = out_ref.shape
    _, _, high, lanes = s_ref.shape
    KY, PK = PL // MZ, MZ // high
    copy_ref[...] = e_ref[...]

    @pl.when(pl.program_id(0) == 0)
    def _():
        total = sums_ref[...]
        gw_ref[...] = total[:, :C] * scale
        gq_ref[...] = (total[:, C : C + 8] * scale).T[:3]
        loss_ref[...] = total[:1, C + 3 : C + 4] * (1.0 / cells)

    def pieces(ref):
        high_part, low_part = split(ref[...].reshape(4, high, lanes))
        return high_part.astype(f32), low_part.astype(f32)

    f_high, f_low = pieces(s_ref)
    field = jnp.concatenate([f_high, f_low, f_high], axis=0).reshape(12 * high, lanes)
    field = field.astype(bf16)
    g_high, g_low = pieces(g_ref)
    grads = [g_high, g_high, g_low]
    swapped = [jnp.stack([g[1], -g[0], g[3], -g[2]], axis=0) for g in grads]
    turned = [
        jnp.concatenate(g, axis=0).reshape(12 * high, lanes).T for g in (grads, swapped)
    ]
    lane = lax.broadcasted_iota(jnp.int32, (C, 12 * high), 1) % high
    for pk in range(PK):
        for ky in range(KY):
            at = (pk * KY + ky) * C
            rows = [
                jnp.where(lane == h, turned[n][at : at + C], 0.0).astype(bf16)
                for h in range(high)
                for n in range(2)
            ]
            value = dot(jnp.concatenate(rows, axis=0), field[:, at : at + C])
            for h in range(high):
                for n in range(2):
                    row = (2 * h + n) * C
                    out_ref[0, ky * MZ + h * PK + pk, n] = value[row : row + C]


def tile_pair(ref, y0):
    count, nz = ref.shape[1], ref.shape[3]
    one = ref[0, :, pl.ds(y0, ROWS), :].reshape(count * ROWS, nz)
    two = ref[0, :, pl.ds(y0 + ROWS, ROWS), :].reshape(count * ROWS, nz)
    return jnp.concatenate([one, two], axis=1)


def put_pair(ref, y0, value):
    count, nz = ref.shape[1], ref.shape[3]
    ref[0, :, pl.ds(y0, ROWS), :] = value[:, :nz].reshape(count, ROWS, nz)
    ref[0, :, pl.ds(y0 + ROWS, ROWS), :] = value[:, nz:].reshape(count, ROWS, nz)


def local_body(f_ref, kw_ref, out_ref):
    for y0 in range(0, f_ref.shape[2], 2 * ROWS):
        put_pair(out_ref, y0, dot(kw_ref[...], tile_pair(f_ref, y0)))


def middle_body(scale, l_ref, m_ref, zi_ref, yi_ref, kp_ref, pre_ref, vel_ref):
    count, ny, nz = l_ref.shape[1], l_ref.shape[2], l_ref.shape[3]
    high, low = split(load_modes(m_ref, MY * count))
    wave = dot_tn(jnp.concatenate([high, high, low], axis=0), zi_ref[...])
    turned = jnp.swapaxes(wave.reshape(MY, count, 2 * nz), 0, 1)
    yi = yi_ref[...]
    for o in range(0, count, 2):
        pair = [
            jnp.concatenate([turned[i, :, :nz], turned[i, :, nz:]], axis=0) for i in (o, o + 1)
        ]
        both = dot(yi, jnp.concatenate(pair, axis=1).astype(bf16))
        pre_ref[0, o] = l_ref[0, o] + both[:, :nz] * scale
        pre_ref[0, o + 1] = l_ref[0, o + 1] + both[:, nz:] * scale

    for y0 in range(0, ny, 2 * ROWS):
        x = tile_pair(pre_ref, y0)
        t = jnp.tanh(x * (ROOT + (0.044715 * ROOT) * (x * x)))
        half = 0.5 * x
        hidden = (half + half * t).astype(bf16)
        put_pair(vel_ref, y0, dot(kp_ref[...], hidden))


def backward_body(
    f_ref, pre_ref, gv_ref, ty_ref, zt_ref, kpt_ref, out_ref, gw_ref, gq_ref, gp_ref, first=0
):
    count, ny, nz = f_ref.shape[1], f_ref.shape[2], f_ref.shape[3]

    @pl.when(pl.program_id(0) == first)
    def _():
        gw_ref[...] = jnp.zeros_like(gw_ref)
        gq_ref[...] = jnp.zeros_like(gq_ref)

    hiddens, grads, fields, slopes = [], [], [], []
    for y0 in range(0, ny, 2 * ROWS):
        gv = tile_pair(gv_ref, y0)
        x = tile_pair(pre_ref, y0)
        cubic = (0.044715 * ROOT) * (x * x)
        t = jnp.tanh(x * (ROOT + cubic))
        cdf = 0.5 + 0.5 * t
        hidden = (x * cdf).astype(bf16)
        slope = cdf + (x * (ROOT + 3.0 * cubic)) * (0.5 - 0.5 * (t * t))
        gp = (dot(kpt_ref[...], gv) * slope).astype(bf16)
        put_pair(gp_ref, y0, gp)
        hiddens.append(hidden)
        grads.append(gp)
        slopes.append(gv)
        fields.append(tile_pair(f_ref, y0))
    gw_ref[...] += dot_nt(jnp.concatenate(fields, axis=1), jnp.concatenate(grads, axis=1))
    gq_ref[...] += dot_nt(jnp.concatenate(hiddens, axis=1), jnp.concatenate(slopes, axis=1))

    store_modes(out_ref, plane_modes(lambda c: gp_ref[0, c], count, ty_ref[...], zt_ref[...]))


def fold(total, columns):
    rows, cols = total.shape
    row = lax.broadcasted_iota(jnp.int32, total.shape, 0) % ROWS
    col = lax.broadcasted_iota(jnp.int32, total.shape, 1) % ROWS
    kept = jnp.where(row == col, total, 0.0).reshape(rows // ROWS, ROWS, cols)
    lane = lax.broadcasted_iota(jnp.int32, (cols, 128), 1)
    block = lax.broadcasted_iota(jnp.int32, (cols, 128), 0) // ROWS
    gather = jnp.where(lane == block + columns, 1.0, 0.0)
    return jnp.dot(jnp.sum(kept, axis=1), gather, precision=precise, preferred_element_type=f32)


def gather_parts(all_ref, zs, zr, xs, xr):
    _, z, x = place()
    zn, rows = all_ref.shape[1], all_ref.shape[2]
    step = rows // PIECES

    def along(p, j):
        part = pl.ds(p * step, step)
        return pltpu.make_async_remote_copy(
            all_ref.at[x, z, part],
            all_ref.at[x, z, part],
            zs.at[p, j - 1],
            zr.at[p, j - 1],
            device_id={"gx": lax.rem(z + j, zn) * 2 + x},
            device_id_type=MESH,
        )

    def across(p, j):
        part = pl.ds(p * step, step)
        t = lax.rem(z - j + zn, zn)
        return pltpu.make_async_remote_copy(
            all_ref.at[x, t, part],
            all_ref.at[x, t, part],
            xs.at[p, j],
            xr.at[p, j],
            device_id={"gx": z * 2 + 1 - x},
            device_id_type=MESH,
        )

    return along, across


def inward(m, count):
    odd = m % 2
    return odd * (count - 1 - m // 2) + (1 - odd) * (m // 2)


def step_body(
    scale, xl, rep,
    f_ref, l_ref, all_ref, t_ref, mult_ref, pw_ref, xb_ref, zi_ref, yi_ref,
    ty_ref, zt_ref, xt_ref,
    e_ref, both_ref, sums_ref,
    kp_ref, kpt_ref,
    pre_ref, vel_ref, gv_ref, gp_ref, slab_ref, gw_ref, gq_ref, loss_ref,
    edge_ref, halo_ref, us, ur, ps, pr,
    pack_ref, ebuf, es, er, chunk_ref, turned_ref, got_ref, other_ref, cs, cr, *scatter
):
    i = pl.program_id(0)
    me, z, x = place()
    table, core = pair()
    gx = lax.axis_size("gx")
    right = {"gx": lax.rem(me + 1, gx)}
    left = {"gx": lax.rem(me + gx - 1, gx)}

    def halo(k, sems):
        return pltpu.make_async_remote_copy(
            edge_ref.at[k],
            halo_ref.at[k],
            sems[0].at[k % 2],
            sems[1].at[k % 2],
            device_id=left if k % 2 == 0 else right,
            device_id_type=MESH,
        )

    def penalty(p, before, after):
        u = vel_ref[p, 1], vel_ref[p, 2]
        rows, lanes = u[0].shape
        slope = (after - before) * 0.5
        slope = slope + (pltpu.roll(u[0], rows - 1, 0) - pltpu.roll(u[0], 1, 0)) * 0.5
        slope = slope + (pltpu.roll(u[1], lanes - 1, 1) - pltpu.roll(u[1], 1, 1)) * 0.5
        lam = mult_ref[p].astype(f32) / 64.0
        e_ref[p] = lam + penalty_weight * slope
        add_loss((lam + (0.5 * penalty_weight) * slope) * slope)

    def add_loss(value):
        rows, lanes = value.shape
        loss_ref[...] = loss_ref[...] + jnp.sum(value.reshape(rows // 8, 8, lanes), axis=0)

    @pl.when(i == 0)
    def _():
        loss_ref[...] = jnp.zeros_like(loss_ref)
        greet(True, True)
        kp_ref[...] = spread_weight(pw_ref[...], False)
        kpt_ref[...] = spread_weight(pw_ref[...], True)
        x_spread(all_ref, xb_ref.at[table], slab_ref)

    @pl.when(i < xl)
    def _():
        p = inward(i, xl)
        plane_ref = pre_ref.at[pl.ds(p, 1)]
        modes_ref = slab_ref.at[:, pl.ds(p, 1)]
        middle_body(
            scale, l_ref, modes_ref, zi_ref, yi_ref, kp_ref, plane_ref,
            vel_ref.at[pl.ds(p, 1)],
        )

    @pl.when(i == 1)
    def _():
        edge_ref[0] = vel_ref[0, 0]
        edge_ref[1] = vel_ref[xl - 1, 0]
        for k in (0, 1):
            halo(k, (us, ur)).start()

    @pl.when(i == xl // 2)
    def _():
        for k in (0, 1):
            halo(k, (us, ur)).wait()
        penalty(0, halo_ref[1], vel_ref[1, 0])
        penalty(xl - 1, vel_ref[xl - 2, 0], halo_ref[0])
        edge_ref[2] = e_ref[0]
        edge_ref[3] = e_ref[xl - 1]
        for k in (2, 3):
            halo(k, (ps, pr)).start()

    @pl.when(i == xl - 1)
    def _():
        def one(p, carry):
            penalty(p, vel_ref[p - 1, 0], vel_ref[p + 1, 0])
            return carry

        lax.fori_loop(1, xl - 1, one, 0)
        for k in (2, 3):
            halo(k, (ps, pr)).wait()

    @pl.when(i >= xl)
    def _():
        p = i - xl
        e = e_ref[p]
        rows, lanes = e.shape
        before = lax.select(
            jnp.broadcast_to(p == 0, e.shape), halo_ref[3], e_ref[lax.rem(p + xl - 1, xl)]
        )
        after = lax.select(
            jnp.broadcast_to(p == xl - 1, e.shape), halo_ref[2], e_ref[lax.rem(p + 1, xl)]
        )
        slopes = (
            (after - before) * 0.5,
            (pltpu.roll(e, rows - 1, 0) - pltpu.roll(e, 1, 0)) * 0.5,
            (pltpu.roll(e, lanes - 1, 1) - pltpu.roll(e, 1, 1)) * 0.5,
        )
        for j in range(3):
            misfit = vel_ref[p, j] - t_ref[0, j].astype(f32)
            add_loss(misfit * misfit)
            gv_ref[0, j] = ((2.0 * misfit - slopes[j]) / rep).astype(bf16)
        backward_body(
            f_ref, pre_ref.at[pl.ds(p, 1)], gv_ref, ty_ref, zt_ref, kpt_ref,
            slab_ref.at[:, pl.ds(p, 1)], gw_ref, gq_ref, gp_ref, first=xl,
        )

    @pl.when(i == pl.num_programs(0) - 1)
    def _():
        x_sum(slab_ref, xt_ref.at[table], scatter[0])
        count = f_ref.shape[1]
        lane = lax.broadcasted_iota(jnp.int32, (count, 128), 1)
        pack_ref[...] = (
            fold(gw_ref[...], 0)
            + fold(gq_ref[...], count)
            + jnp.where(lane == count + 3, jnp.sum(loss_ref[...]), 0.0)
        )
        scatter_sum(Scatter(scatter[0], chunk_ref, *scatter[1:]), pack_ref, ebuf, es, er)
        turn(chunk_ref, turned_ref)
        half = turned_ref.shape[0] // 2
        copies = [
            send(turned_ref.at[pl.ds(half, half)], got_ref, (cs.at[0], cr.at[0]), core),
            send(pack_ref, other_ref, (cs.at[1], cr.at[1]), core),
        ]
        for copy in copies:
            copy.wait()
        both_ref[0] = turned_ref[:half]
        both_ref[1] = got_ref[...]
        sums_ref[...] = pack_ref[...] + other_ref[...]


def whole(shape):
    return pl.BlockSpec(shape, lambda i: (0,) * len(shape))


def plane(shape):
    return pl.BlockSpec((1,) + tuple(shape), lambda i: (i,) + (0,) * len(shape))


params = pltpu.CompilerParams(
    dimension_semantics=("arbitrary",), vmem_limit_bytes=56 * 1024 * 1024
)


def extended(value, axis_name):
    count = lax.axis_size(axis_name)
    up = [(i, (i + 1) % count) for i in range(count)]
    down = [(j, i) for i, j in up]
    before = lax.ppermute(value[-1:], axis_name, up)
    after = lax.ppermute(value[:1], axis_name, down)
    return jnp.concatenate([before, value, after], axis=0)


def central(values, axis):
    return (jnp.roll(values, -1, axis) - jnp.roll(values, 1, axis)) * 0.5


def local(fields, targets, multipliers, local_weight, proj_weight, spectral_weight):
    gx = lax.axis_size("gx")
    rep = lax.axis_size("rep")
    _, xl, C, NY, NZ = fields.shape
    NX = xl * gx
    PL = MY * MZ // gx
    scale = 1.0 / math.sqrt(NX * NY * NZ)
    fields, targets, multipliers = fields[0], targets[0], multipliers[0]

    cos_y, sin_y = fourier_tables(NY, MY)
    ty = jnp.asarray(np.concatenate([cos_y.T, -sin_y.T], 0).astype(ml_dtypes.bfloat16))
    yi = jnp.asarray(np.concatenate([cos_y, -sin_y], 1).astype(ml_dtypes.bfloat16))
    cos_z, sin_z = fourier_tables(NZ, MZ)
    zt = np.concatenate(
        [np.concatenate([cos_z.T, sin_z.T], 1), np.concatenate([-sin_z.T, cos_z.T], 1)], 0
    )
    direct = gx == 8 and rep == 2 and C == 32
    KY = MY // gx if direct else 0
    PK = 128 // (KY * C) if direct else 1
    HZ = MZ // PK
    order = np.arange(2 * MZ).reshape(2, HZ, PK).transpose(2, 0, 1).reshape(-1)
    zt = zt[order]
    zi_high, zi_low = halves(zt)
    zt = jnp.asarray(np.concatenate([zi_high, zi_low], 0))
    zi = jnp.asarray(np.concatenate([zi_high, zi_low, zi_high], 0))
    cos_x, sin_x = fourier_tables(NX, MX)
    xt = np.stack(
        [np.stack([cos_x.T, sin_x.T], 1), np.stack([-sin_x.T, cos_x.T], 1)], 1
    )
    xt = xt.reshape(MX, 2, 2, gx, xl).transpose((0, 1, 3, 4, 2) if direct else (0, 1, 3, 2, 4))
    xt = xt.reshape(2 * MX, 2 * NX)
    x_forward = jnp.asarray(xt * np.float32(scale))
    x_back = jnp.asarray(np.ascontiguousarray(xt.T))

    def spread(weight):
        rows, columns = weight.shape
        left = jnp.asarray(np.kron(np.eye(rows), np.ones((ROWS, 1))), dtype=bf16)
        right = jnp.asarray(np.kron(np.eye(columns), np.ones((1, ROWS))), dtype=bf16)
        diagonal = jnp.asarray(np.kron(np.ones((rows, columns)), np.eye(ROWS)), dtype=bf16)
        return dot(dot(left, weight).astype(bf16), right).astype(bf16) * diagonal

    kw = spread(local_weight.T)
    kp = spread(proj_weight.T)
    kpt = spread(proj_weight)

    field_spec = plane((C, NY, NZ))
    modes_shape = jax.ShapeDtypeStruct((xl, 2 * MZ, MY * C), f32)
    modes_spec = plane((2 * MZ, MY * C))
    vel_spec = plane((3, NY, NZ))

    def to_owner(slab):
        slab = slab.reshape(xl, 2, MZ, MY, C).transpose(3, 2, 1, 0, 4)
        slab = slab.reshape(gx, PL, 2, xl, C).transpose(0, 2, 3, 1, 4)
        slab = slab.reshape(gx, 2 * xl, PL * C)
        slab = lax.all_to_all(slab, "gx", split_axis=0, concat_axis=0, tiled=True)
        out = jnp.dot(x_forward, slab.reshape(2 * NX, PL * C), precision=precise)
        return out.reshape(MX, 2, PL, C)

    def to_planes(modes):
        out = jnp.dot(x_back, modes.reshape(2 * MX, PL * C), precision=precise)
        out = out.reshape(gx, 2 * xl, PL * C)
        out = lax.all_to_all(out, "gx", split_axis=0, concat_axis=0, tiled=True)
        out = out.reshape(gx, 2, xl, PL, C).transpose(0, 3, 1, 2, 4)
        out = out.reshape(MY, MZ, 2, xl, C).transpose(3, 2, 1, 0, 4)
        return out.reshape(xl, 2 * MZ, MY * C)

    def both_samples(modes):
        part = modes.reshape(rep, MX // rep, 2, PL, C)
        return lax.all_to_all(part, "rep", split_axis=0, concat_axis=0, tiled=True)

    ZN = gx // 2
    QR = HZ * 2 * MX
    slab_scratch = pltpu.VMEM((gx, xl, 2, HZ, 128), f32)
    dma = pltpu.SemaphoreType.DMA

    def comm(number):
        return pltpu.CompilerParams(
            dimension_semantics=("arbitrary",),
            vmem_limit_bytes=60 * 1024 * 1024,
            collective_id=number,
            has_side_effects=True,
        )

    if direct:
        parts = xt.reshape(rep, MX, gx, 2 * xl)
        parts = np.stack([np.concatenate([parts[r], parts[1 - r]], 0) for r in range(rep)])
        parts = parts.transpose(0, 2, 1, 3).reshape(rep * gx, 2 * MX, 2 * xl)
        x_own = jnp.asarray(parts * np.float32(scale))
        x_out = jnp.asarray(np.ascontiguousarray(parts.transpose(0, 2, 1)))
        chunk_shape = jax.ShapeDtypeStruct((QR, 128), f32)
        weight_scratch = pltpu.VMEM(spectral_weight.shape, bf16)
        row_scratch = pltpu.VMEM((2 * MX, HZ, 128), f32)
        both_shape = jax.ShapeDtypeStruct((2, MX, HZ, 128), f32)
        half_scratch = pltpu.VMEM((MX, HZ, 128), f32)
        gathered_shape = jax.ShapeDtypeStruct((2, ZN, QR, 128), f32)
        wide = C * ROWS
        spectrum, gathered, mapped = pl.pallas_call(
            functools.partial(forward_sum_body, xl),
            grid=(2 * xl,),
            out_shape=(
                both_shape,
                gathered_shape,
                jax.ShapeDtypeStruct((xl, C, NY, NZ), f32),
            ),
            in_specs=[
                pl.BlockSpec((1, C, NY, NZ), lambda i: (i % xl, 0, 0, 0)),
                whole(ty.shape),
                whole(zt.shape),
                whole(x_own.shape),
                whole((C, C)),
                pl.BlockSpec(memory_space=pl.ANY),
            ],
            out_specs=(
                whole(both_shape.shape),
                whole(gathered_shape.shape),
                pl.BlockSpec((1, C, NY, NZ), lambda i: ((i % xl) * (i // xl), 0, 0, 0)),
            ),
            scratch_shapes=[slab_scratch, weight_scratch, weight_scratch]
            + [pltpu.VMEM((QR, 128), f32), row_scratch, row_scratch, half_scratch]
            + [pltpu.VMEM((wide, wide), bf16), pltpu.VMEM(gathered_shape.shape, f32)]
            + [dma] * 5
            + [dma((PIECES, ZN - 1))] * 2
            + [dma((PIECES, ZN))] * 2
            + scatter_scratch(ZN, QR),
            compiler_params=comm(1),
        )(fields, ty, zt, x_own, local_weight, spectral_weight)
    else:
        slab = pl.pallas_call(
            forward_body,
            grid=(xl,),
            out_shape=modes_shape,
            in_specs=[field_spec, whole(ty.shape), whole(zt.shape)],
            out_specs=modes_spec,
            compiler_params=params,
        )(fields, ty, zt)
        mapped = pl.pallas_call(
            local_body,
            grid=(xl,),
            out_shape=jax.ShapeDtypeStruct((xl, C, NY, NZ), f32),
            in_specs=[field_spec, whole(kw.shape)],
            out_specs=field_spec,
            compiler_params=pltpu.CompilerParams(vmem_limit_bytes=20 * 1024 * 1024),
        )(fields, kw)
    middle_shape = (
        jax.ShapeDtypeStruct((xl, C, NY, NZ), f32),
        jax.ShapeDtypeStruct((xl, 3, NY, NZ), f32),
    )
    wide = C * ROWS
    if direct:
        tables = [proj_weight.T, x_out, zi, yi, ty, zt, x_own]

        def once(shape):
            return pl.BlockSpec(
                shape, lambda i: (0,) * len(shape), pipeline_mode=pl.Buffered(1)
            )

        penalty, chunk, sums = pl.pallas_call(
            functools.partial(step_body, scale, xl, rep),
            grid=(2 * xl,),
            out_shape=(
                jax.ShapeDtypeStruct((xl, NY, NZ), f32),
                both_shape,
                jax.ShapeDtypeStruct((C, 128), f32),
            ),
            in_specs=[
                pl.BlockSpec(
                    (1, C, NY, NZ),
                    lambda i: ((i % xl) * (i // xl), 0, 0, 0),
                ),
                pl.BlockSpec(
                    (1, C, NY, NZ),
                    lambda i: (
                        inward(i % xl, xl) * (1 - i // xl) + inward(xl - 1, xl) * (i // xl),
                        0,
                        0,
                        0,
                    ),
                ),
                once(gathered_shape.shape),
                pl.BlockSpec((1, 3, NY, NZ), lambda i: ((i % xl) * (i // xl), 0, 0, 0)),
                once((xl, NY, NZ)),
            ]
            + [once(t.shape) for t in tables],
            out_specs=(whole((xl, NY, NZ)), whole(both_shape.shape), whole((C, 128))),
            scratch_shapes=[
                pltpu.VMEM((3 * ROWS, wide), bf16),
                pltpu.VMEM((wide, 3 * ROWS), bf16),
                pltpu.VMEM((xl, C, NY, NZ), f32),
                pltpu.VMEM((xl, 3, NY, NZ), f32),
                pltpu.VMEM((1, 3, NY, NZ), bf16),
                pltpu.VMEM((1, C, NY, NZ), bf16),
                slab_scratch,
                pltpu.VMEM((wide, wide), f32),
                pltpu.VMEM((wide, 3 * ROWS), f32),
                pltpu.VMEM((8, NZ), f32),
                pltpu.VMEM((4, NY, NZ), f32),
                pltpu.VMEM((4, NY, NZ), f32),
            ]
            + [dma((2,))] * 4
            + [pltpu.VMEM((C, 128), f32), pltpu.VMEM((ZN, C, 128), f32), dma((ZN,)), dma((ZN,))]
            + [pltpu.VMEM((QR, 128), f32), row_scratch, half_scratch]
            + [pltpu.VMEM((C, 128), f32), dma((2,)), dma((2,))]
            + scatter_scratch(ZN, QR),
            compiler_params=comm(2),
        )(fields, mapped, gathered, targets, multipliers, *tables)
        KX = MX // rep
        modes_of = pl.BlockSpec((2, 2, HZ, 128), lambda i: (0, i, 0, 0))
        planes = pl.BlockSpec((xl // KX, NY, NZ), lambda i: (i, 0, 0))
        grad_r, grad_w, grad_q, loss, penalty = pl.pallas_call(
            functools.partial(grad_body, scale, rep * NX * NY * NZ),
            grid=(KX,),
            out_shape=(
                jax.ShapeDtypeStruct(spectral_weight.shape, f32),
                jax.ShapeDtypeStruct((C, C), f32),
                jax.ShapeDtypeStruct((3, C), f32),
                jax.ShapeDtypeStruct((1, 1), f32),
                jax.ShapeDtypeStruct(penalty.shape, f32),
            ),
            in_specs=[modes_of, modes_of, whole((C, 128)), planes],
            out_specs=(
                plane((PL, 2, C, C)),
                whole((C, C)),
                whole((3, C)),
                whole((1, 1)),
                planes,
            ),
            compiler_params=params,
        )(spectrum, chunk, sums, penalty)
        return (penalty[None], grad_r, grad_w, grad_q.T, loss[0])
    else:
        weights = spectral_weight
        weights = weights.transpose(2, 3, 4, 0, 1).reshape(1, 2, C, C, MX // rep * PL)
        weights = lax.all_gather(weights, "rep", axis=0, tiled=True)
        spectrum = to_owner(slab)
        KX = MX // rep
        turned = spectrum.reshape(rep, KX, 2, PL, C).transpose(0, 2, 4, 1, 3)
        turned = turned.reshape(rep, 2, 1, C, KX * PL)
        w_re, w_im = weights[:, 0].astype(f32), weights[:, 1].astype(f32)
        s_re, s_im = turned[:, 0], turned[:, 1]
        product = jnp.stack(
            [jnp.sum(w_re * s_re - w_im * s_im, axis=2), jnp.sum(w_re * s_im + w_im * s_re, axis=2)],
            axis=1,
        )
        product = product.reshape(rep, 2, C, KX, PL).transpose(0, 3, 1, 4, 2)
        product = product.reshape(MX, 2, PL, C)
        spectra = both_samples(spectrum)
        wave = to_planes(product)
        pre, velocity = pl.pallas_call(
            functools.partial(middle_body, scale),
            grid=(xl,),
            out_shape=middle_shape,
            in_specs=[field_spec, modes_spec, whole(zi.shape), whole(yi.shape), whole(kp.shape)],
            out_specs=(field_spec, vel_spec),
            compiler_params=params,
        )(mapped, wave, zi, yi, kp)
        padded = extended(velocity[:, 0].astype(bf16), "gx").astype(f32)
        slope_x = (padded[2:] - padded[:-2]) * 0.5
        divergence = slope_x + central(velocity[:, 1], 1) + central(velocity[:, 2], 2)
        lam = multipliers.astype(f32) / 64.0
        penalty = lam + penalty_weight * divergence
        misfit = velocity - targets.astype(f32)
        loss_sum = (
            jnp.sum(misfit * misfit)
            + jnp.sum(lam * divergence)
            + 0.5 * penalty_weight * jnp.sum(divergence * divergence)
        )
        padded = extended(penalty.astype(bf16), "gx").astype(f32)
        pen_x = (padded[2:] - padded[:-2]) * 0.5
        slopes = jnp.stack([pen_x, central(penalty, 1), central(penalty, 2)], axis=1)
        grad_vel = ((2.0 * misfit - slopes) / rep).astype(bf16)
        grad_slab, gw, gq = pl.pallas_call(
            backward_body,
            grid=(xl,),
            out_shape=(
                modes_shape,
                jax.ShapeDtypeStruct((wide, wide), f32),
                jax.ShapeDtypeStruct((wide, 3 * ROWS), f32),
            ),
            in_specs=[field_spec, field_spec, vel_spec]
            + [whole(ty.shape), whole(zt.shape), whole(kpt.shape)],
            out_specs=(modes_spec, whole((wide, wide)), whole((wide, 3 * ROWS))),
            scratch_shapes=[pltpu.VMEM((1, C, NY, NZ), bf16)],
            compiler_params=params,
        )(fields, pre, grad_vel, ty, zt, kpt)
        gather = jnp.asarray(np.kron(np.eye(C), np.ones((1, ROWS))).astype(np.float32))
        gather_q = jnp.asarray(np.kron(np.eye(3), np.ones((ROWS, 1))).astype(np.float32))
        mask = jnp.asarray(np.kron(np.ones((C, C)), np.eye(ROWS)).astype(np.float32))
        mask_q = jnp.asarray(np.kron(np.ones((C, 3)), np.eye(ROWS)).astype(np.float32))
        grad_w = jnp.dot(gather, gw * mask, precision=precise)
        grad_w = jnp.dot(grad_w, gather.T, precision=precise)
        grad_q = jnp.dot(gather, gq * mask_q, precision=precise)
        grad_q = jnp.dot(grad_q, gather_q, precision=precise)
        grads = both_samples(to_owner(grad_slab))
        packed = jnp.concatenate([grad_w.reshape(-1), grad_q.reshape(-1), loss_sum.reshape(1)])
        packed = lax.psum(packed, ("gx", "rep"))
        grad_w = packed[: C * C].reshape(C, C)
        grad_q = packed[C * C : C * C + 3 * C].reshape(C, 3)
        loss = packed[-1:]
    loss = loss / (rep * NX * NY * NZ)

    g_re, g_im = grads[:, :, 0], grads[:, :, 1]
    across = jnp.stack([jnp.stack([g_re, g_im], 3), jnp.stack([g_im, -g_re], 3)], 1)
    terms = [
        across[b, t][..., None] * spectra[b, :, t][:, :, None, None, :]
        for b in range(rep)
        for t in range(2)
    ]
    grad_r = sum(terms[1:], terms[0])
    return (penalty[None], grad_r, grad_w * scale, grad_q * scale, loss)


def solution(mesh):
    in_specs = (
        P(("grp", "rep"), "gx", None, None, None),
        P(("grp", "rep"), "gx", None, None, None),
        P(("grp", "rep"), "gx", None, None),
        P(),
        P(),
        P("rep", "gx", None, None, None),
    )
    out_specs = (
        P(("grp", "rep"), "gx", None, None),
        P(("grp", "rep"), "gx", None, None, None),
        P("grp", None),
        P("grp", None),
        P("grp"),
    )
    return jax.shard_map(local, mesh=mesh, in_specs=in_specs, out_specs=out_specs, check_vma=False)
```

```python
import functools
import math

import jax
import jax.numpy as jnp
import ml_dtypes
import numpy as np
from jax import lax
from jax.experimental import pallas as pl
from jax.experimental.pallas import tpu as pltpu
from jax.sharding import PartitionSpec as P

MX = 16
MY = 16
MZ = 16
ROWS = 16

penalty_weight = 0.5
precise = lax.Precision.HIGHEST
bf16 = jnp.bfloat16
f32 = jnp.float32
ROOT = math.sqrt(2.0 / math.pi)


def fourier_tables(length, count):
    position = np.arange(count)
    modes = np.where(position < count // 2, position, position - count)
    phase = np.mod(np.arange(length)[:, None] * modes[None, :], length)
    angle = phase.astype(np.float32) * np.float32(2.0 * math.pi / length)
    return np.cos(angle), np.sin(angle)


def halves(table):
    high = table.astype(ml_dtypes.bfloat16)
    low = (table - high.astype(np.float32)).astype(ml_dtypes.bfloat16)
    return high, low


def split(value):
    high = value.astype(bf16)
    return high, (value - high.astype(f32)).astype(bf16)


def dot(a, b):
    return jnp.dot(a, b, preferred_element_type=f32)


def dot_nt(a, b):
    return lax.dot_general(a, b, (((1,), (1,)), ((), ())), preferred_element_type=f32)


def dot_tn(a, b):
    return lax.dot_general(a, b, (((0,), (0,)), ((), ())), preferred_element_type=f32)


def plane_modes(load, count, ty, zt):
    parts = []
    for c in range(0, count, 2):
        pair = dot(ty, jnp.concatenate([load(c), load(c + 1)], axis=1))
        nz = pair.shape[1] // 2
        parts += [pair[:, :nz], pair[:, nz:]]
    turned = jnp.swapaxes(jnp.stack(parts, axis=0), 0, 1)
    real = turned[:MY].reshape(MY * count, nz)
    imag = turned[MY:].reshape(MY * count, nz)
    high, low = split(jnp.concatenate([real, imag], axis=1))
    both = dot_nt(zt, high)
    n = 2 * MZ
    return both[:n] + both[n:] + dot_nt(zt[:n], low)


def store_modes(out_ref, modes):
    if len(out_ref.shape) == 3:
        out_ref[0] = modes
        return
    owners, _, _, high, lanes = out_ref.shape
    width = modes.shape[1] // owners
    rows = 2 * high
    for d in range(owners):
        parts = [
            modes[j * rows : (j + 1) * rows, d * width : (d + 1) * width]
            for j in range(lanes // width)
        ]
        out_ref[d, 0] = jnp.concatenate(parts, axis=1).reshape(2, high, lanes)


def load_modes(m_ref, columns):
    if len(m_ref.shape) == 3:
        return m_ref[0]
    owners, _, _, high, lanes = m_ref.shape
    width = columns // owners
    blocks = [m_ref[d, 0].reshape(2 * high, lanes) for d in range(owners)]
    rows = [
        jnp.concatenate([block[:, j * width : (j + 1) * width] for block in blocks], axis=1)
        for j in range(lanes // width)
    ]
    return jnp.concatenate(rows, axis=0)


def forward_body(f_ref, ty_ref, zt_ref, out_ref):
    count = f_ref.shape[1]
    store_modes(out_ref, plane_modes(lambda c: f_ref[0, c], count, ty_ref[...], zt_ref[...]))


MESH = pl.DeviceIdType.MESH
PIECES = 4


def place():
    me = lax.axis_index("gx")
    return me, me // 2, lax.rem(me, 2)


def pair():
    r = lax.axis_index("rep")
    return r * lax.axis_size("gx") + lax.axis_index("gx"), {"rep": 1 - r}


def greet(ring=False, core=False):
    _, z, x = place()
    zn = lax.axis_size("gx") // 2
    barrier = pltpu.get_barrier_semaphore()
    pl.semaphore_signal(barrier, inc=1, device_id={"gx": z * 2 + 1 - x}, device_id_type=MESH)
    for j in range(1, zn):
        t = lax.rem(z + j, zn)
        pl.semaphore_signal(barrier, inc=1, device_id={"gx": t * 2 + x}, device_id_type=MESH)
    if ring:
        me = z * 2 + x
        t = lax.rem(me + 2 * x - 1 + 2 * zn, 2 * zn)
        pl.semaphore_signal(barrier, inc=1, device_id={"gx": t}, device_id_type=MESH)
    if core:
        pl.semaphore_signal(barrier, inc=1, device_id=pair()[1], device_id_type=MESH)
    pl.semaphore_wait(barrier, zn + (1 if ring else 0) + (1 if core else 0))


def send(src, dst, sems, where):
    copy = pltpu.make_async_remote_copy(
        src, dst, sems[0], sems[1], device_id=where, device_id_type=MESH
    )
    copy.start()
    return copy


class Scatter:
    def __init__(self, a_ref, o_ref, xbuf, sbuf, zbuf, xs, xr, zs, zr):
        self.refs = a_ref, o_ref, xbuf, sbuf, zbuf
        self.sems = xs, xr, zs, zr
        _, self.z, self.x = place()
        self.zn = a_ref.shape[1]
        self.step = a_ref.shape[2] // PIECES
        self.to_x = {"gx": self.z * 2 + 1 - self.x}

    def part(self, p):
        return pl.ds(p * self.step, self.step)

    def copy(self, src, dst, sems, where):
        return pltpu.make_async_remote_copy(
            src, dst, sems[0], sems[1], device_id=where, device_id_type=MESH
        )

    def across(self, p):
        a_ref, _, xbuf, _, _ = self.refs
        xs, xr, _, _ = self.sems
        return self.copy(
            a_ref.at[1 - self.x, :, self.part(p)], xbuf.at[p], (xs.at[p], xr.at[p]), self.to_x
        )

    def along(self, p, j):
        _, _, _, sbuf, zbuf = self.refs
        _, _, zs, zr = self.sems
        t = lax.rem(self.z + j, self.zn)
        return self.copy(
            sbuf.at[p, j - 1],
            zbuf.at[p, j - 1],
            (zs.at[p, j - 1], zr.at[p, j - 1]),
            {"gx": t * 2 + self.x},
        )

    def start(self):
        for p in range(PIECES):
            self.across(p).start()

    def forward(self, p):
        a_ref, o_ref, xbuf, sbuf, _ = self.refs
        self.across(p).wait_recv()
        for j in (2, 1, 3):
            t = lax.rem(self.z + j, self.zn)
            sbuf[p, j - 1] = a_ref[self.x, t, self.part(p)] + xbuf[p, t]
            self.along(p, j).start()
        o_ref[self.part(p)] = a_ref[self.x, self.z, self.part(p)] + xbuf[p, self.z]

    def finish(self, p):
        _, o_ref, _, _, zbuf = self.refs
        for j in range(1, self.zn):
            self.along(p, j).wait_recv()
        total = (zbuf[p, 0] + zbuf[p, 1]) + zbuf[p, 2]
        o_ref[self.part(p)] = o_ref[self.part(p)] + total

    def settle(self):
        for p in range(PIECES):
            self.across(p).wait_send()
            for j in range(1, self.zn):
                self.along(p, j).wait_send()


def scatter_scratch(zn, rows):
    step = rows // PIECES
    dma = pltpu.SemaphoreType.DMA
    return [
        pltpu.VMEM((2, zn, rows, 128), f32),
        pltpu.VMEM((PIECES, zn, step, 128), f32),
        pltpu.VMEM((PIECES, zn - 1, step, 128), f32),
        pltpu.VMEM((PIECES, zn - 1, step, 128), f32),
        dma((PIECES,)),
        dma((PIECES,)),
        dma((PIECES, zn - 1)),
        dma((PIECES, zn - 1)),
    ]


def x_sum(slab_ref, table_ref, a_ref):
    owners, xl, _, high, lanes = slab_ref.shape
    rows = table_ref.shape[0]
    for d in range(owners):
        turned = jnp.swapaxes(slab_ref[d].reshape(2 * xl, high, lanes), 0, 1)
        for k in range(high):
            a_ref[d % 2, d // 2, k * rows : (k + 1) * rows] = jnp.dot(
                table_ref[...], turned[k], precision=precise, preferred_element_type=f32
            )


def x_spread(all_ref, table_ref, slab_ref):
    owners, xl, _, high, lanes = slab_ref.shape
    rows = table_ref.shape[1]
    for d in range(owners):
        parts = [
            jnp.dot(
                table_ref[...],
                all_ref[d % 2, d // 2, k * rows : (k + 1) * rows],
                precision=precise,
                preferred_element_type=f32,
            )
            for k in range(high)
        ]
        turned = jnp.swapaxes(jnp.stack(parts, axis=0), 0, 1)
        slab_ref[d] = turned.reshape(xl, 2, high, lanes)


def spread_weight(weight, turned):
    rows, cols = weight.shape[::-1] if turned else weight.shape

    def match(shape, low, high):
        a = lax.broadcasted_iota(jnp.int32, shape, 0)
        b = lax.broadcasted_iota(jnp.int32, shape, 1)
        return low(a) == high(b)

    tall = match((rows * ROWS, rows), lambda a: a // ROWS, lambda b: b)
    wide = match((cols, cols * ROWS), lambda a: a, lambda b: b // ROWS)
    tall = jnp.where(tall, 1.0, 0.0).astype(bf16)
    wide = jnp.where(wide, 1.0, 0.0).astype(bf16)
    half = (dot_nt if turned else dot)(tall, weight).astype(bf16)
    diagonal = match((rows * ROWS, cols * ROWS), lambda a: a % ROWS, lambda b: b % ROWS)
    return jnp.where(diagonal, dot(half, wide), 0.0).astype(bf16)


def turn(chunk_ref, out_ref):
    steps, high, lanes = out_ref.shape
    out_ref[...] = jnp.swapaxes(chunk_ref[...].reshape(high, steps, lanes), 0, 1)


def multiply(weights, in_ref, res_ref, first, count):
    steps, high, lanes = in_ref.shape
    KX, PL, _, _, C = weights[0].shape
    KY, PK = PL // MZ, MZ // high
    row = lax.broadcasted_iota(jnp.int32, (high, lanes), 0)
    lane = lax.broadcasted_iota(jnp.int32, (high, lanes), 1)
    low = (lane // C) % 2 == 0

    for half, w_ref in enumerate(weights):

        def one(k, half=half, w_ref=w_ref):
            at = 2 * (half * KX + k)
            rest = in_ref[at : at + 2]
            pieces = []
            for _ in range(3):
                pieces.append(rest.astype(bf16).astype(f32))
                rest = rest - pieces[-1]
            results = []
            for ky in range(KY):
                rows = [
                    piece[ri][:, (pk * KY + ky) * C : (pk * KY + ky + 1) * C]
                    for piece in pieces
                    for ri in range(2)
                    for pk in range(PK)
                ]
                base = ky * MZ + first * PK
                w = w_ref[k, base : base + count * PK].reshape(count * PK * 2 * C, C)
                terms = dot_nt(jnp.concatenate(rows, axis=0).astype(bf16), w)
                terms = terms.reshape(3, 2, PK, high, count * lanes)
                terms = (terms[2] + terms[1]) + terms[0]
                kept = []
                for ri in range(2):
                    value = None
                    for h in range(count):
                        own = slice(h * lanes, (h + 1) * lanes)
                        here = jnp.where(
                            lane < 2 * C, terms[ri, 0][:, own], terms[ri, 1][:, own]
                        )
                        value = here if value is None else jnp.where(row == first + h, here, value)
                    kept.append(value)
                real, imag = kept
                imag = jnp.where(low, -pltpu.roll(imag, lanes - C, 1), pltpu.roll(imag, C, 1))
                results.append(real + imag)
            one_, two = results
            real = jnp.where(low, one_, pltpu.roll(two, C, 1))
            imag = jnp.where(low, pltpu.roll(one_, lanes - C, 1), two)
            res_ref[at] = jnp.where(row < first, res_ref[at], real)
            res_ref[at + 1] = jnp.where(row < first, res_ref[at + 1], imag)

        for k in range(KX):
            one(k)


def forward_sum_body(
    xl,
    f_ref, ty_ref, zt_ref, xt_ref, lw_ref, w_ref,
    both_ref, gathered_ref, out_ref,
    slab_ref, wown_ref, woth_ref, chunk_ref, in_ref, res_ref, got_ref, kw_ref, all_ref,
    own_sem, ws, wr, ss, sr, gzs, gzr, gxs, gxr, *scatter
):
    i = pl.program_id(0)
    count = f_ref.shape[1]
    table, core = pair()
    _, z, x = place()
    zn = lax.axis_size("gx") // 2
    steps, high, _ = in_ref.shape
    fetch = pltpu.make_async_copy(w_ref, wown_ref, own_sem)
    swap = pltpu.make_async_remote_copy(
        w_ref, woth_ref, ws, wr, device_id=core, device_id_type=MESH
    )
    half = steps // 2
    cross = pltpu.make_async_remote_copy(
        in_ref.at[pl.ds(half, half)], got_ref, ss, sr, device_id=core, device_id_type=MESH
    )
    total = Scatter(scatter[0], chunk_ref, *scatter[1:])
    along, across = gather_parts(all_ref, gzs, gzr, gxs, gxr)
    rows = high // PIECES

    def mapped(p):
        total.finish(p)
        for h in range(rows * p, rows * (p + 1)):
            in_ref[:, h, :] = chunk_ref[h * steps : (h + 1) * steps]
        multiply((wown_ref, woth_ref), in_ref, res_ref, rows * p, rows)
        for h in range(rows * p, rows * (p + 1)):
            all_ref[x, z, h * steps : (h + 1) * steps] = res_ref[:, h, :]
        for j in (2, 1, 3):
            along(p, j).start()
        across(p, 0).start()

    def passed(p):
        for j in range(1, zn):
            along(p, j).wait_recv()
            across(p, j).start()

    @pl.when(i == 0)
    def _():
        greet(core=True)
        fetch.start()
        swap.start()
        in_ref[...] = jnp.zeros_like(in_ref)
        res_ref[...] = jnp.zeros_like(res_ref)
        kw_ref[...] = spread_weight(lw_ref[...], True)

    @pl.when(i < xl)
    def _():
        store_modes(
            slab_ref.at[:, pl.ds(i, 1)],
            plane_modes(lambda c: f_ref[0, c], count, ty_ref[...], zt_ref[...]),
        )

    @pl.when(i == xl - 1)
    def _():
        x_sum(slab_ref, xt_ref.at[table], scatter[0])
        total.start()

    @pl.when(i >= xl)
    def _():
        for y0 in range(0, f_ref.shape[2], 2 * ROWS):
            put_pair(out_ref, y0, dot(kw_ref[...], tile_pair(f_ref, y0)))

    @pl.when(i == xl + (3 * xl) // 16)
    def _():
        total.forward(0)

    @pl.when(i == xl + (5 * xl) // 16)
    def _():
        total.forward(1)

    @pl.when(i == xl + (7 * xl) // 16)
    def _():
        total.forward(2)
        fetch.wait()
        swap.wait()
        mapped(0)

    @pl.when(i == xl + (10 * xl) // 16)
    def _():
        total.forward(3)
        mapped(1)

    @pl.when(i == 2 * xl - 1)
    def _():
        mapped(2)
        passed(0)
        mapped(3)
        cross.start()
        for p in range(1, PIECES):
            passed(p)
        total.settle()
        cross.wait()
        both_ref[0] = in_ref[:half]
        both_ref[1] = got_ref[...]
        for p in range(PIECES):
            for j in range(zn):
                across(p, j).wait()
            for j in range(1, zn):
                along(p, j).wait_send()
        gathered_ref[...] = all_ref[...]


def grad_body(
    scale, cells, s_ref, g_ref, sums_ref, e_ref,
    out_ref, gw_ref, gq_ref, loss_ref, copy_ref
):
    _, PL, _, C, _ = out_ref.shape
    _, _, high, lanes = s_ref.shape
    KY, PK = PL // MZ, MZ // high
    copy_ref[...] = e_ref[...]

    @pl.when(pl.program_id(0) == 0)
    def _():
        total = sums_ref[...]
        gw_ref[...] = total[:, :C] * scale
        gq_ref[...] = (total[:, C : C + 8] * scale).T[:3]
        loss_ref[...] = total[:1, C + 3 : C + 4] * (1.0 / cells)

    def pieces(ref):
        high_part, low_part = split(ref[...].reshape(4, high, lanes))
        return high_part.astype(f32), low_part.astype(f32)

    f_high, f_low = pieces(s_ref)
    field = jnp.concatenate([f_high, f_low, f_high], axis=0).reshape(12 * high, lanes)
    field = field.astype(bf16)
    g_high, g_low = pieces(g_ref)
    grads = [g_high, g_high, g_low]
    swapped = [jnp.stack([g[1], -g[0], g[3], -g[2]], axis=0) for g in grads]
    turned = [
        jnp.concatenate(g, axis=0).reshape(12 * high, lanes).T for g in (grads, swapped)
    ]
    lane = lax.broadcasted_iota(jnp.int32, (C, 12 * high), 1) % high
    for pk in range(PK):
        for ky in range(KY):
            at = (pk * KY + ky) * C
            rows = [
                jnp.where(lane == h, turned[n][at : at + C], 0.0).astype(bf16)
                for h in range(high)
                for n in range(2)
            ]
            value = dot(jnp.concatenate(rows, axis=0), field[:, at : at + C])
            for h in range(high):
                for n in range(2):
                    row = (2 * h + n) * C
                    out_ref[0, ky * MZ + h * PK + pk, n] = value[row : row + C]


def tile_pair(ref, y0):
    count, nz = ref.shape[1], ref.shape[3]
    one = ref[0, :, pl.ds(y0, ROWS), :].reshape(count * ROWS, nz)
    two = ref[0, :, pl.ds(y0 + ROWS, ROWS), :].reshape(count * ROWS, nz)
    return jnp.concatenate([one, two], axis=1)


def put_pair(ref, y0, value):
    count, nz = ref.shape[1], ref.shape[3]
    ref[0, :, pl.ds(y0, ROWS), :] = value[:, :nz].reshape(count, ROWS, nz)
    ref[0, :, pl.ds(y0 + ROWS, ROWS), :] = value[:, nz:].reshape(count, ROWS, nz)


def local_body(f_ref, kw_ref, out_ref):
    for y0 in range(0, f_ref.shape[2], 2 * ROWS):
        put_pair(out_ref, y0, dot(kw_ref[...], tile_pair(f_ref, y0)))


def middle_body(scale, l_ref, m_ref, zi_ref, yi_ref, kp_ref, pre_ref, vel_ref):
    count, ny, nz = l_ref.shape[1], l_ref.shape[2], l_ref.shape[3]
    high, low = split(load_modes(m_ref, MY * count))
    wave = dot_tn(jnp.concatenate([high, high, low], axis=0), zi_ref[...])
    turned = jnp.swapaxes(wave.reshape(MY, count, 2 * nz), 0, 1)
    yi = yi_ref[...]
    for o in range(0, count, 2):
        pair = [
            jnp.concatenate([turned[i, :, :nz], turned[i, :, nz:]], axis=0) for i in (o, o + 1)
        ]
        both = dot(yi, jnp.concatenate(pair, axis=1).astype(bf16))
        pre_ref[0, o] = l_ref[0, o] + both[:, :nz] * scale
        pre_ref[0, o + 1] = l_ref[0, o + 1] + both[:, nz:] * scale

    for y0 in range(0, ny, 2 * ROWS):
        x = tile_pair(pre_ref, y0)
        t = jnp.tanh(x * (ROOT + (0.044715 * ROOT) * (x * x)))
        half = 0.5 * x
        hidden = (half + half * t).astype(bf16)
        put_pair(vel_ref, y0, dot(kp_ref[...], hidden))


def backward_body(
    f_ref, pre_ref, gv_ref, ty_ref, zt_ref, kpt_ref, out_ref, gw_ref, gq_ref, gp_ref, first=0
):
    count, ny, nz = pre_ref.shape[1], pre_ref.shape[2], pre_ref.shape[3]

    @pl.when(pl.program_id(0) == first)
    def _():
        gw_ref[...] = jnp.zeros_like(gw_ref)
        gq_ref[...] = jnp.zeros_like(gq_ref)

    hiddens, grads, fields, slopes = [], [], [], []
    for y0 in range(0, ny, 2 * ROWS):
        gv = tile_pair(gv_ref, y0)
        x = tile_pair(pre_ref, y0)
        cubic = (0.044715 * ROOT) * (x * x)
        t = jnp.tanh(x * (ROOT + cubic))
        cdf = 0.5 + 0.5 * t
        hidden = (x * cdf).astype(bf16)
        slope = cdf + (x * (ROOT + 3.0 * cubic)) * (0.5 - 0.5 * (t * t))
        gp = (dot(kpt_ref[...], gv) * slope).astype(bf16)
        put_pair(gp_ref, y0, gp)
        hiddens.append(hidden)
        slopes.append(gv)
        if f_ref is None:
            put_pair(pre_ref, y0, gp.astype(f32))
        else:
            grads.append(gp)
            fields.append(tile_pair(f_ref, y0))
    if f_ref is not None:
        gw_ref[...] += dot_nt(jnp.concatenate(fields, axis=1), jnp.concatenate(grads, axis=1))
    gq_ref[...] += dot_nt(jnp.concatenate(hiddens, axis=1), jnp.concatenate(slopes, axis=1))

    store_modes(out_ref, plane_modes(lambda c: gp_ref[0, c], count, ty_ref[...], zt_ref[...]))


def fold(total, columns):
    rows, cols = total.shape
    row = lax.broadcasted_iota(jnp.int32, total.shape, 0) % ROWS
    col = lax.broadcasted_iota(jnp.int32, total.shape, 1) % ROWS
    kept = jnp.where(row == col, total, 0.0).reshape(rows // ROWS, ROWS, cols)
    lane = lax.broadcasted_iota(jnp.int32, (cols, 128), 1)
    block = lax.broadcasted_iota(jnp.int32, (cols, 128), 0) // ROWS
    gather = jnp.where(lane == block + columns, 1.0, 0.0)
    return jnp.dot(jnp.sum(kept, axis=1), gather, precision=precise, preferred_element_type=f32)


def gather_parts(all_ref, zs, zr, xs, xr):
    _, z, x = place()
    zn, rows = all_ref.shape[1], all_ref.shape[2]
    step = rows // PIECES

    def along(p, j):
        part = pl.ds(p * step, step)
        return pltpu.make_async_remote_copy(
            all_ref.at[x, z, part],
            all_ref.at[x, z, part],
            zs.at[p, j - 1],
            zr.at[p, j - 1],
            device_id={"gx": lax.rem(z + j, zn) * 2 + x},
            device_id_type=MESH,
        )

    def across(p, j):
        part = pl.ds(p * step, step)
        t = lax.rem(z - j + zn, zn)
        return pltpu.make_async_remote_copy(
            all_ref.at[x, t, part],
            all_ref.at[x, t, part],
            xs.at[p, j],
            xr.at[p, j],
            device_id={"gx": z * 2 + 1 - x},
            device_id_type=MESH,
        )

    return along, across


def inward(m, count):
    odd = m % 2
    return odd * (count - 1 - m // 2) + (1 - odd) * (m // 2)


def step_body(
    scale, xl, rep,
    f_ref, l_ref, all_ref, t_ref, mult_ref, pw_ref, xb_ref, zi_ref, yi_ref,
    ty_ref, zt_ref, xt_ref,
    e_ref, both_ref, sums_ref,
    kp_ref, kpt_ref,
    pre_ref, vel_ref, gv_ref, gp_ref, slab_ref, gw_ref, gq_ref, loss_ref,
    edge_ref, halo_ref, us, ur, ps, pr,
    pack_ref, ebuf, es, er, chunk_ref, turned_ref, got_ref, other_ref, cs, cr, *scatter
):
    i = pl.program_id(0)
    me, z, x = place()
    table, core = pair()
    gx = lax.axis_size("gx")
    right = {"gx": lax.rem(me + 1, gx)}
    left = {"gx": lax.rem(me + gx - 1, gx)}

    def halo(k, sems):
        return pltpu.make_async_remote_copy(
            edge_ref.at[k],
            halo_ref.at[k],
            sems[0].at[k % 2],
            sems[1].at[k % 2],
            device_id=left if k % 2 == 0 else right,
            device_id_type=MESH,
        )

    def penalty(p, before, after):
        u = vel_ref[p, 1], vel_ref[p, 2]
        rows, lanes = u[0].shape
        slope = (after - before) * 0.5
        slope = slope + (pltpu.roll(u[0], rows - 1, 0) - pltpu.roll(u[0], 1, 0)) * 0.5
        slope = slope + (pltpu.roll(u[1], lanes - 1, 1) - pltpu.roll(u[1], 1, 1)) * 0.5
        lam = mult_ref[p].astype(f32) / 64.0
        e_ref[p] = lam + penalty_weight * slope
        add_loss((lam + (0.5 * penalty_weight) * slope) * slope)

    def add_loss(value):
        rows, lanes = value.shape
        loss_ref[...] = loss_ref[...] + jnp.sum(value.reshape(rows // 8, 8, lanes), axis=0)

    @pl.when(i == 0)
    def _():
        loss_ref[...] = jnp.zeros_like(loss_ref)
        greet(True, True)
        kp_ref[...] = spread_weight(pw_ref[...], False)
        kpt_ref[...] = spread_weight(pw_ref[...], True)
        x_spread(all_ref, xb_ref.at[table], slab_ref)

    @pl.when(i < xl)
    def _():
        p = inward(i, xl)
        plane_ref = pre_ref.at[pl.ds(p, 1)]
        modes_ref = slab_ref.at[:, pl.ds(p, 1)]
        middle_body(
            scale, l_ref, modes_ref, zi_ref, yi_ref, kp_ref, plane_ref,
            vel_ref.at[pl.ds(p, 1)],
        )

    @pl.when(i == 1)
    def _():
        edge_ref[0] = vel_ref[0, 0]
        edge_ref[1] = vel_ref[xl - 1, 0]
        for k in (0, 1):
            halo(k, (us, ur)).start()

    @pl.when(i == xl // 2)
    def _():
        for k in (0, 1):
            halo(k, (us, ur)).wait()
        penalty(0, halo_ref[1], vel_ref[1, 0])
        penalty(xl - 1, vel_ref[xl - 2, 0], halo_ref[0])
        edge_ref[2] = e_ref[0]
        edge_ref[3] = e_ref[xl - 1]
        for k in (2, 3):
            halo(k, (ps, pr)).start()

    @pl.when(i == xl - 1)
    def _():
        def one(p, carry):
            penalty(p, vel_ref[p - 1, 0], vel_ref[p + 1, 0])
            return carry

        lax.fori_loop(1, xl - 1, one, 0)
        for k in (2, 3):
            halo(k, (ps, pr)).wait()

    @pl.when((i >= xl) & (i < 2 * xl))
    def _():
        p = i - xl
        e = e_ref[p]
        rows, lanes = e.shape
        before = lax.select(
            jnp.broadcast_to(p == 0, e.shape), halo_ref[3], e_ref[lax.rem(p + xl - 1, xl)]
        )
        after = lax.select(
            jnp.broadcast_to(p == xl - 1, e.shape), halo_ref[2], e_ref[lax.rem(p + 1, xl)]
        )
        slopes = (
            (after - before) * 0.5,
            (pltpu.roll(e, rows - 1, 0) - pltpu.roll(e, 1, 0)) * 0.5,
            (pltpu.roll(e, lanes - 1, 1) - pltpu.roll(e, 1, 1)) * 0.5,
        )
        for j in range(3):
            misfit = vel_ref[p, j] - t_ref[0, j].astype(f32)
            add_loss(misfit * misfit)
            gv_ref[0, j] = ((2.0 * misfit - slopes[j]) / rep).astype(bf16)
        backward_body(
            None, pre_ref.at[pl.ds(p, 1)], gv_ref, ty_ref, zt_ref, kpt_ref,
            slab_ref.at[:, pl.ds(p, 1)], gw_ref, gq_ref, gp_ref, first=xl,
        )

    total = Scatter(scatter[0], chunk_ref, *scatter[1:])

    @pl.when(i == 2 * xl - 1)
    def _():
        x_sum(slab_ref, xt_ref.at[table], scatter[0])
        total.start()

    @pl.when(i >= 2 * xl)
    def _():
        plane_ref = pre_ref.at[pl.ds(i - 2 * xl, 1)]
        starts = range(0, f_ref.shape[2], 2 * ROWS)
        fields = [tile_pair(f_ref, y0) for y0 in starts]
        grads = [tile_pair(plane_ref, y0).astype(bf16) for y0 in starts]
        gw_ref[...] += dot_nt(jnp.concatenate(fields, axis=1), jnp.concatenate(grads, axis=1))

    for p in range(PIECES):

        @pl.when(i == 2 * xl + ((p + 1) * 3 * xl) // 16 + (2 * xl) // 16)
        def _(p=p):
            total.forward(p)

    @pl.when(i == pl.num_programs(0) - 1)
    def _():
        count = f_ref.shape[1]
        zn = total.zn
        lane = lax.broadcasted_iota(jnp.int32, (count, 128), 1)
        pack_ref[...] = (
            fold(gw_ref[...], 0)
            + fold(gq_ref[...], count)
            + jnp.where(lane == count + 3, jnp.sum(loss_ref[...]), 0.0)
        )
        swap = send(pack_ref, ebuf.at[0], (es.at[0], er.at[0]), total.to_x)
        for p in range(PIECES - 1):
            total.finish(p)
        swap.wait()
        pack_ref[...] = pack_ref[...] + ebuf[0]
        spread = [
            send(
                pack_ref,
                ebuf.at[j],
                (es.at[j], er.at[j]),
                {"gx": lax.rem(z + j, zn) * 2 + x},
            )
            for j in range(1, zn)
        ]
        total.finish(PIECES - 1)
        turn(chunk_ref, turned_ref)
        half = turned_ref.shape[0] // 2
        cross = send(turned_ref.at[pl.ds(half, half)], got_ref, (cs.at[0], cr.at[0]), core)
        for copy in spread:
            copy.wait()
        pack_ref[...] = (pack_ref[...] + ebuf[1]) + (ebuf[2] + ebuf[3])
        other = send(pack_ref, other_ref, (cs.at[1], cr.at[1]), core)
        total.settle()
        cross.wait()
        other.wait()
        both_ref[0] = turned_ref[:half]
        both_ref[1] = got_ref[...]
        sums_ref[...] = pack_ref[...] + other_ref[...]


def whole(shape):
    return pl.BlockSpec(shape, lambda i: (0,) * len(shape))


def plane(shape):
    return pl.BlockSpec((1,) + tuple(shape), lambda i: (i,) + (0,) * len(shape))


params = pltpu.CompilerParams(
    dimension_semantics=("arbitrary",), vmem_limit_bytes=56 * 1024 * 1024
)


def extended(value, axis_name):
    count = lax.axis_size(axis_name)
    up = [(i, (i + 1) % count) for i in range(count)]
    down = [(j, i) for i, j in up]
    before = lax.ppermute(value[-1:], axis_name, up)
    after = lax.ppermute(value[:1], axis_name, down)
    return jnp.concatenate([before, value, after], axis=0)


def central(values, axis):
    return (jnp.roll(values, -1, axis) - jnp.roll(values, 1, axis)) * 0.5


def local(fields, targets, multipliers, local_weight, proj_weight, spectral_weight):
    gx = lax.axis_size("gx")
    rep = lax.axis_size("rep")
    _, xl, C, NY, NZ = fields.shape
    NX = xl * gx
    PL = MY * MZ // gx
    scale = 1.0 / math.sqrt(NX * NY * NZ)
    fields, targets, multipliers = fields[0], targets[0], multipliers[0]

    cos_y, sin_y = fourier_tables(NY, MY)
    ty = jnp.asarray(np.concatenate([cos_y.T, -sin_y.T], 0).astype(ml_dtypes.bfloat16))
    yi = jnp.asarray(np.concatenate([cos_y, -sin_y], 1).astype(ml_dtypes.bfloat16))
    cos_z, sin_z = fourier_tables(NZ, MZ)
    zt = np.concatenate(
        [np.concatenate([cos_z.T, sin_z.T], 1), np.concatenate([-sin_z.T, cos_z.T], 1)], 0
    )
    direct = gx == 8 and rep == 2 and C == 32
    KY = MY // gx if direct else 0
    PK = 128 // (KY * C) if direct else 1
    HZ = MZ // PK
    order = np.arange(2 * MZ).reshape(2, HZ, PK).transpose(2, 0, 1).reshape(-1)
    zt = zt[order]
    zi_high, zi_low = halves(zt)
    zt = jnp.asarray(np.concatenate([zi_high, zi_low], 0))
    zi = jnp.asarray(np.concatenate([zi_high, zi_low, zi_high], 0))
    cos_x, sin_x = fourier_tables(NX, MX)
    xt = np.stack(
        [np.stack([cos_x.T, sin_x.T], 1), np.stack([-sin_x.T, cos_x.T], 1)], 1
    )
    xt = xt.reshape(MX, 2, 2, gx, xl).transpose((0, 1, 3, 4, 2) if direct else (0, 1, 3, 2, 4))
    xt = xt.reshape(2 * MX, 2 * NX)
    x_forward = jnp.asarray(xt * np.float32(scale))
    x_back = jnp.asarray(np.ascontiguousarray(xt.T))

    def spread(weight):
        rows, columns = weight.shape
        left = jnp.asarray(np.kron(np.eye(rows), np.ones((ROWS, 1))), dtype=bf16)
        right = jnp.asarray(np.kron(np.eye(columns), np.ones((1, ROWS))), dtype=bf16)
        diagonal = jnp.asarray(np.kron(np.ones((rows, columns)), np.eye(ROWS)), dtype=bf16)
        return dot(dot(left, weight).astype(bf16), right).astype(bf16) * diagonal

    kw = spread(local_weight.T)
    kp = spread(proj_weight.T)
    kpt = spread(proj_weight)

    field_spec = plane((C, NY, NZ))
    modes_shape = jax.ShapeDtypeStruct((xl, 2 * MZ, MY * C), f32)
    modes_spec = plane((2 * MZ, MY * C))
    vel_spec = plane((3, NY, NZ))

    def to_owner(slab):
        slab = slab.reshape(xl, 2, MZ, MY, C).transpose(3, 2, 1, 0, 4)
        slab = slab.reshape(gx, PL, 2, xl, C).transpose(0, 2, 3, 1, 4)
        slab = slab.reshape(gx, 2 * xl, PL * C)
        slab = lax.all_to_all(slab, "gx", split_axis=0, concat_axis=0, tiled=True)
        out = jnp.dot(x_forward, slab.reshape(2 * NX, PL * C), precision=precise)
        return out.reshape(MX, 2, PL, C)

    def to_planes(modes):
        out = jnp.dot(x_back, modes.reshape(2 * MX, PL * C), precision=precise)
        out = out.reshape(gx, 2 * xl, PL * C)
        out = lax.all_to_all(out, "gx", split_axis=0, concat_axis=0, tiled=True)
        out = out.reshape(gx, 2, xl, PL, C).transpose(0, 3, 1, 2, 4)
        out = out.reshape(MY, MZ, 2, xl, C).transpose(3, 2, 1, 0, 4)
        return out.reshape(xl, 2 * MZ, MY * C)

    def both_samples(modes):
        part = modes.reshape(rep, MX // rep, 2, PL, C)
        return lax.all_to_all(part, "rep", split_axis=0, concat_axis=0, tiled=True)

    ZN = gx // 2
    QR = HZ * 2 * MX
    slab_scratch = pltpu.VMEM((gx, xl, 2, HZ, 128), f32)
    dma = pltpu.SemaphoreType.DMA

    def comm(number):
        return pltpu.CompilerParams(
            dimension_semantics=("arbitrary",),
            vmem_limit_bytes=60 * 1024 * 1024,
            collective_id=number,
            has_side_effects=True,
        )

    if direct:
        parts = xt.reshape(rep, MX, gx, 2 * xl)
        parts = np.stack([np.concatenate([parts[r], parts[1 - r]], 0) for r in range(rep)])
        parts = parts.transpose(0, 2, 1, 3).reshape(rep * gx, 2 * MX, 2 * xl)
        x_own = jnp.asarray(parts * np.float32(scale))
        x_out = jnp.asarray(np.ascontiguousarray(parts.transpose(0, 2, 1)))
        chunk_shape = jax.ShapeDtypeStruct((QR, 128), f32)
        weight_scratch = pltpu.VMEM(spectral_weight.shape, bf16)
        row_scratch = pltpu.VMEM((2 * MX, HZ, 128), f32)
        both_shape = jax.ShapeDtypeStruct((2, MX, HZ, 128), f32)
        half_scratch = pltpu.VMEM((MX, HZ, 128), f32)
        gathered_shape = jax.ShapeDtypeStruct((2, ZN, QR, 128), f32)
        wide = C * ROWS
        spectrum, gathered, mapped = pl.pallas_call(
            functools.partial(forward_sum_body, xl),
            grid=(2 * xl,),
            out_shape=(
                both_shape,
                gathered_shape,
                jax.ShapeDtypeStruct((xl, C, NY, NZ), f32),
            ),
            in_specs=[
                pl.BlockSpec((1, C, NY, NZ), lambda i: (i % xl, 0, 0, 0)),
                whole(ty.shape),
                whole(zt.shape),
                whole(x_own.shape),
                whole((C, C)),
                pl.BlockSpec(memory_space=pl.ANY),
            ],
            out_specs=(
                whole(both_shape.shape),
                whole(gathered_shape.shape),
                pl.BlockSpec((1, C, NY, NZ), lambda i: ((i % xl) * (i // xl), 0, 0, 0)),
            ),
            scratch_shapes=[slab_scratch, weight_scratch, weight_scratch]
            + [pltpu.VMEM((QR, 128), f32), row_scratch, row_scratch, half_scratch]
            + [pltpu.VMEM((wide, wide), bf16), pltpu.VMEM(gathered_shape.shape, f32)]
            + [dma] * 5
            + [dma((PIECES, ZN - 1))] * 2
            + [dma((PIECES, ZN))] * 2
            + scatter_scratch(ZN, QR),
            compiler_params=comm(1),
        )(fields, ty, zt, x_own, local_weight, spectral_weight)
    else:
        slab = pl.pallas_call(
            forward_body,
            grid=(xl,),
            out_shape=modes_shape,
            in_specs=[field_spec, whole(ty.shape), whole(zt.shape)],
            out_specs=modes_spec,
            compiler_params=params,
        )(fields, ty, zt)
        mapped = pl.pallas_call(
            local_body,
            grid=(xl,),
            out_shape=jax.ShapeDtypeStruct((xl, C, NY, NZ), f32),
            in_specs=[field_spec, whole(kw.shape)],
            out_specs=field_spec,
            compiler_params=pltpu.CompilerParams(vmem_limit_bytes=20 * 1024 * 1024),
        )(fields, kw)
    middle_shape = (
        jax.ShapeDtypeStruct((xl, C, NY, NZ), f32),
        jax.ShapeDtypeStruct((xl, 3, NY, NZ), f32),
    )
    wide = C * ROWS
    if direct:
        tables = [proj_weight.T, x_out, zi, yi, ty, zt, x_own]

        def once(shape):
            return pl.BlockSpec(
                shape, lambda i: (0,) * len(shape), pipeline_mode=pl.Buffered(1)
            )

        penalty, chunk, sums = pl.pallas_call(
            functools.partial(step_body, scale, xl, rep),
            grid=(3 * xl,),
            out_shape=(
                jax.ShapeDtypeStruct((xl, NY, NZ), f32),
                both_shape,
                jax.ShapeDtypeStruct((C, 128), f32),
            ),
            in_specs=[
                pl.BlockSpec(
                    (1, C, NY, NZ),
                    lambda i: ((i % xl) * (i // (2 * xl)), 0, 0, 0),
                ),
                pl.BlockSpec(
                    (1, C, NY, NZ),
                    lambda i: (
                        inward(i % xl, xl) * (1 - (i // xl + 1) // 2)
                        + inward(xl - 1, xl) * ((i // xl + 1) // 2),
                        0,
                        0,
                        0,
                    ),
                ),
                once(gathered_shape.shape),
                pl.BlockSpec(
                    (1, 3, NY, NZ),
                    lambda i: (
                        (i % xl) * ((i // xl) % 2) + (xl - 1) * (i // (2 * xl)),
                        0,
                        0,
                        0,
                    ),
                ),
                once((xl, NY, NZ)),
            ]
            + [once(t.shape) for t in tables],
            out_specs=(whole((xl, NY, NZ)), whole(both_shape.shape), whole((C, 128))),
            scratch_shapes=[
                pltpu.VMEM((3 * ROWS, wide), bf16),
                pltpu.VMEM((wide, 3 * ROWS), bf16),
                pltpu.VMEM((xl, C, NY, NZ), f32),
                pltpu.VMEM((xl, 3, NY, NZ), f32),
                pltpu.VMEM((1, 3, NY, NZ), bf16),
                pltpu.VMEM((1, C, NY, NZ), bf16),
                slab_scratch,
                pltpu.VMEM((wide, wide), f32),
                pltpu.VMEM((wide, 3 * ROWS), f32),
                pltpu.VMEM((8, NZ), f32),
                pltpu.VMEM((4, NY, NZ), f32),
                pltpu.VMEM((4, NY, NZ), f32),
            ]
            + [dma((2,))] * 4
            + [pltpu.VMEM((C, 128), f32), pltpu.VMEM((ZN, C, 128), f32), dma((ZN,)), dma((ZN,))]
            + [pltpu.VMEM((QR, 128), f32), row_scratch, half_scratch]
            + [pltpu.VMEM((C, 128), f32), dma((2,)), dma((2,))]
            + scatter_scratch(ZN, QR),
            compiler_params=comm(2),
        )(fields, mapped, gathered, targets, multipliers, *tables)
        KX = MX // rep
        modes_of = pl.BlockSpec((2, 2, HZ, 128), lambda i: (0, i, 0, 0))
        planes = pl.BlockSpec((xl // KX, NY, NZ), lambda i: (i, 0, 0))
        grad_r, grad_w, grad_q, loss, penalty = pl.pallas_call(
            functools.partial(grad_body, scale, rep * NX * NY * NZ),
            grid=(KX,),
            out_shape=(
                jax.ShapeDtypeStruct(spectral_weight.shape, f32),
                jax.ShapeDtypeStruct((C, C), f32),
                jax.ShapeDtypeStruct((3, C), f32),
                jax.ShapeDtypeStruct((1, 1), f32),
                jax.ShapeDtypeStruct(penalty.shape, f32),
            ),
            in_specs=[modes_of, modes_of, whole((C, 128)), planes],
            out_specs=(
                plane((PL, 2, C, C)),
                whole((C, C)),
                whole((3, C)),
                whole((1, 1)),
                planes,
            ),
            compiler_params=params,
        )(spectrum, chunk, sums, penalty)
        return (penalty[None], grad_r, grad_w, grad_q.T, loss[0])
    else:
        weights = spectral_weight
        weights = weights.transpose(2, 3, 4, 0, 1).reshape(1, 2, C, C, MX // rep * PL)
        weights = lax.all_gather(weights, "rep", axis=0, tiled=True)
        spectrum = to_owner(slab)
        KX = MX // rep
        turned = spectrum.reshape(rep, KX, 2, PL, C).transpose(0, 2, 4, 1, 3)
        turned = turned.reshape(rep, 2, 1, C, KX * PL)
        w_re, w_im = weights[:, 0].astype(f32), weights[:, 1].astype(f32)
        s_re, s_im = turned[:, 0], turned[:, 1]
        product = jnp.stack(
            [jnp.sum(w_re * s_re - w_im * s_im, axis=2), jnp.sum(w_re * s_im + w_im * s_re, axis=2)],
            axis=1,
        )
        product = product.reshape(rep, 2, C, KX, PL).transpose(0, 3, 1, 4, 2)
        product = product.reshape(MX, 2, PL, C)
        spectra = both_samples(spectrum)
        wave = to_planes(product)
        pre, velocity = pl.pallas_call(
            functools.partial(middle_body, scale),
            grid=(xl,),
            out_shape=middle_shape,
            in_specs=[field_spec, modes_spec, whole(zi.shape), whole(yi.shape), whole(kp.shape)],
            out_specs=(field_spec, vel_spec),
            compiler_params=params,
        )(mapped, wave, zi, yi, kp)
        padded = extended(velocity[:, 0].astype(bf16), "gx").astype(f32)
        slope_x = (padded[2:] - padded[:-2]) * 0.5
        divergence = slope_x + central(velocity[:, 1], 1) + central(velocity[:, 2], 2)
        lam = multipliers.astype(f32) / 64.0
        penalty = lam + penalty_weight * divergence
        misfit = velocity - targets.astype(f32)
        loss_sum = (
            jnp.sum(misfit * misfit)
            + jnp.sum(lam * divergence)
            + 0.5 * penalty_weight * jnp.sum(divergence * divergence)
        )
        padded = extended(penalty.astype(bf16), "gx").astype(f32)
        pen_x = (padded[2:] - padded[:-2]) * 0.5
        slopes = jnp.stack([pen_x, central(penalty, 1), central(penalty, 2)], axis=1)
        grad_vel = ((2.0 * misfit - slopes) / rep).astype(bf16)
        grad_slab, gw, gq = pl.pallas_call(
            backward_body,
            grid=(xl,),
            out_shape=(
                modes_shape,
                jax.ShapeDtypeStruct((wide, wide), f32),
                jax.ShapeDtypeStruct((wide, 3 * ROWS), f32),
            ),
            in_specs=[field_spec, field_spec, vel_spec]
            + [whole(ty.shape), whole(zt.shape), whole(kpt.shape)],
            out_specs=(modes_spec, whole((wide, wide)), whole((wide, 3 * ROWS))),
            scratch_shapes=[pltpu.VMEM((1, C, NY, NZ), bf16)],
            compiler_params=params,
        )(fields, pre, grad_vel, ty, zt, kpt)
        gather = jnp.asarray(np.kron(np.eye(C), np.ones((1, ROWS))).astype(np.float32))
        gather_q = jnp.asarray(np.kron(np.eye(3), np.ones((ROWS, 1))).astype(np.float32))
        mask = jnp.asarray(np.kron(np.ones((C, C)), np.eye(ROWS)).astype(np.float32))
        mask_q = jnp.asarray(np.kron(np.ones((C, 3)), np.eye(ROWS)).astype(np.float32))
        grad_w = jnp.dot(gather, gw * mask, precision=precise)
        grad_w = jnp.dot(grad_w, gather.T, precision=precise)
        grad_q = jnp.dot(gather, gq * mask_q, precision=precise)
        grad_q = jnp.dot(grad_q, gather_q, precision=precise)
        grads = both_samples(to_owner(grad_slab))
        packed = jnp.concatenate([grad_w.reshape(-1), grad_q.reshape(-1), loss_sum.reshape(1)])
        packed = lax.psum(packed, ("gx", "rep"))
        grad_w = packed[: C * C].reshape(C, C)
        grad_q = packed[C * C : C * C + 3 * C].reshape(C, 3)
        loss = packed[-1:]
    loss = loss / (rep * NX * NY * NZ)

    g_re, g_im = grads[:, :, 0], grads[:, :, 1]
    across = jnp.stack([jnp.stack([g_re, g_im], 3), jnp.stack([g_im, -g_re], 3)], 1)
    terms = [
        across[b, t][..., None] * spectra[b, :, t][:, :, None, None, :]
        for b in range(rep)
        for t in range(2)
    ]
    grad_r = sum(terms[1:], terms[0])
    return (penalty[None], grad_r, grad_w * scale, grad_q * scale, loss)


def solution(mesh):
    in_specs = (
        P(("grp", "rep"), "gx", None, None, None),
        P(("grp", "rep"), "gx", None, None, None),
        P(("grp", "rep"), "gx", None, None),
        P(),
        P(),
        P("rep", "gx", None, None, None),
    )
    out_specs = (
        P(("grp", "rep"), "gx", None, None),
        P(("grp", "rep"), "gx", None, None, None),
        P("grp", None),
        P("grp", None),
        P("grp"),
    )
    return jax.shard_map(local, mesh=mesh, in_specs=in_specs, out_specs=out_specs, check_vma=False)
```

```python
import functools
import math

import jax
import jax.numpy as jnp
import ml_dtypes
import numpy as np
from jax import lax
from jax.experimental import pallas as pl
from jax.experimental.pallas import tpu as pltpu
from jax.sharding import PartitionSpec as P

MX = 16
MY = 16
MZ = 16
ROWS = 16

penalty_weight = 0.5
precise = lax.Precision.HIGHEST
bf16 = jnp.bfloat16
f32 = jnp.float32
ROOT = math.sqrt(2.0 / math.pi)


def fourier_tables(length, count):
    position = np.arange(count)
    modes = np.where(position < count // 2, position, position - count)
    phase = np.mod(np.arange(length)[:, None] * modes[None, :], length)
    angle = phase.astype(np.float32) * np.float32(2.0 * math.pi / length)
    return np.cos(angle), np.sin(angle)


def halves(table):
    high = table.astype(ml_dtypes.bfloat16)
    low = (table - high.astype(np.float32)).astype(ml_dtypes.bfloat16)
    return high, low


def split(value):
    high = value.astype(bf16)
    return high, (value - high.astype(f32)).astype(bf16)


def dot(a, b):
    return jnp.dot(a, b, preferred_element_type=f32)


def dot_nt(a, b):
    return lax.dot_general(a, b, (((1,), (1,)), ((), ())), preferred_element_type=f32)


def dot_tn(a, b):
    return lax.dot_general(a, b, (((0,), (0,)), ((), ())), preferred_element_type=f32)


def plane_modes(load, count, ty, zt):
    parts = []
    for c in range(0, count, 2):
        pair = dot(ty, jnp.concatenate([load(c), load(c + 1)], axis=1))
        nz = pair.shape[1] // 2
        parts += [pair[:, :nz], pair[:, nz:]]
    turned = jnp.swapaxes(jnp.stack(parts, axis=0), 0, 1)
    real = turned[:MY].reshape(MY * count, nz)
    imag = turned[MY:].reshape(MY * count, nz)
    high, low = split(jnp.concatenate([real, imag], axis=1))
    both = dot_nt(zt, high)
    n = 2 * MZ
    return both[:n] + both[n:] + dot_nt(zt[:n], low)


def store_modes(out_ref, modes):
    if len(out_ref.shape) == 3:
        out_ref[0] = modes
        return
    owners, _, _, high, lanes = out_ref.shape
    width = modes.shape[1] // owners
    rows = 2 * high
    for d in range(owners):
        parts = [
            modes[j * rows : (j + 1) * rows, d * width : (d + 1) * width]
            for j in range(lanes // width)
        ]
        out_ref[d, 0] = jnp.concatenate(parts, axis=1).reshape(2, high, lanes)


def load_modes(m_ref, columns):
    if len(m_ref.shape) == 3:
        return m_ref[0]
    owners, _, _, high, lanes = m_ref.shape
    width = columns // owners
    blocks = [m_ref[d, 0].reshape(2 * high, lanes) for d in range(owners)]
    rows = [
        jnp.concatenate([block[:, j * width : (j + 1) * width] for block in blocks], axis=1)
        for j in range(lanes // width)
    ]
    return jnp.concatenate(rows, axis=0)


def forward_body(f_ref, ty_ref, zt_ref, out_ref):
    count = f_ref.shape[1]
    store_modes(out_ref, plane_modes(lambda c: f_ref[0, c], count, ty_ref[...], zt_ref[...]))


MESH = pl.DeviceIdType.MESH
PIECES = 4


def place():
    me = lax.axis_index("gx")
    return me, me // 2, lax.rem(me, 2)


def pair():
    r = lax.axis_index("rep")
    return r * lax.axis_size("gx") + lax.axis_index("gx"), {"rep": 1 - r}


def greet(ring=False, core=False):
    _, z, x = place()
    zn = lax.axis_size("gx") // 2
    barrier = pltpu.get_barrier_semaphore()
    pl.semaphore_signal(barrier, inc=1, device_id={"gx": z * 2 + 1 - x}, device_id_type=MESH)
    for j in range(1, zn):
        t = lax.rem(z + j, zn)
        pl.semaphore_signal(barrier, inc=1, device_id={"gx": t * 2 + x}, device_id_type=MESH)
    if ring:
        me = z * 2 + x
        t = lax.rem(me + 2 * x - 1 + 2 * zn, 2 * zn)
        pl.semaphore_signal(barrier, inc=1, device_id={"gx": t}, device_id_type=MESH)
    if core:
        pl.semaphore_signal(barrier, inc=1, device_id=pair()[1], device_id_type=MESH)
    pl.semaphore_wait(barrier, zn + (1 if ring else 0) + (1 if core else 0))


def send(src, dst, sems, where):
    copy = pltpu.make_async_remote_copy(
        src, dst, sems[0], sems[1], device_id=where, device_id_type=MESH
    )
    copy.start()
    return copy


class Scatter:
    def __init__(self, a_ref, o_ref, xbuf, sbuf, zbuf, xs, xr, zs, zr):
        self.refs = a_ref, o_ref, xbuf, sbuf, zbuf
        self.sems = xs, xr, zs, zr
        _, self.z, self.x = place()
        self.zn = a_ref.shape[1]
        self.step = a_ref.shape[2] // PIECES
        self.to_x = {"gx": self.z * 2 + 1 - self.x}

    def part(self, p):
        return pl.ds(p * self.step, self.step)

    def copy(self, src, dst, sems, where):
        return pltpu.make_async_remote_copy(
            src, dst, sems[0], sems[1], device_id=where, device_id_type=MESH
        )

    def across(self, p):
        a_ref, _, xbuf, _, _ = self.refs
        xs, xr, _, _ = self.sems
        return self.copy(
            a_ref.at[1 - self.x, :, self.part(p)], xbuf.at[p], (xs.at[p], xr.at[p]), self.to_x
        )

    def along(self, p, j):
        _, _, _, sbuf, zbuf = self.refs
        _, _, zs, zr = self.sems
        t = lax.rem(self.z + j, self.zn)
        return self.copy(
            sbuf.at[p, j - 1],
            zbuf.at[p, j - 1],
            (zs.at[p, j - 1], zr.at[p, j - 1]),
            {"gx": t * 2 + self.x},
        )

    def start(self):
        for p in range(PIECES):
            self.across(p).start()

    def forward(self, p):
        a_ref, o_ref, xbuf, sbuf, _ = self.refs
        self.across(p).wait_recv()
        for j in (2, 1, 3):
            t = lax.rem(self.z + j, self.zn)
            sbuf[p, j - 1] = a_ref[self.x, t, self.part(p)] + xbuf[p, t]
            self.along(p, j).start()
        o_ref[self.part(p)] = a_ref[self.x, self.z, self.part(p)] + xbuf[p, self.z]

    def finish(self, p):
        _, o_ref, _, _, zbuf = self.refs
        for j in range(1, self.zn):
            self.along(p, j).wait_recv()
        total = (zbuf[p, 0] + zbuf[p, 1]) + zbuf[p, 2]
        o_ref[self.part(p)] = o_ref[self.part(p)] + total

    def settle(self):
        for p in range(PIECES):
            self.across(p).wait_send()
            for j in range(1, self.zn):
                self.along(p, j).wait_send()


def scatter_sum(scatter, e_ref, ebuf, es, er):
    z, x, zn = scatter.z, scatter.x, scatter.zn
    swap = send(e_ref, ebuf.at[0], (es.at[0], er.at[0]), scatter.to_x)
    for p in range(PIECES):
        scatter.forward(p)
    swap.wait()
    e_ref[...] = e_ref[...] + ebuf[0]
    spread = [
        send(e_ref, ebuf.at[j], (es.at[j], er.at[j]), {"gx": lax.rem(z + j, zn) * 2 + x})
        for j in range(1, zn)
    ]
    for p in range(PIECES):
        scatter.finish(p)
    scatter.settle()
    for copy in spread:
        copy.wait()
    e_ref[...] = (e_ref[...] + ebuf[1]) + (ebuf[2] + ebuf[3])


def scatter_scratch(zn, rows):
    step = rows // PIECES
    dma = pltpu.SemaphoreType.DMA
    return [
        pltpu.VMEM((2, zn, rows, 128), f32),
        pltpu.VMEM((PIECES, zn, step, 128), f32),
        pltpu.VMEM((PIECES, zn - 1, step, 128), f32),
        pltpu.VMEM((PIECES, zn - 1, step, 128), f32),
        dma((PIECES,)),
        dma((PIECES,)),
        dma((PIECES, zn - 1)),
        dma((PIECES, zn - 1)),
    ]


def x_sum(slab_ref, table_ref, a_ref):
    owners, xl, _, high, lanes = slab_ref.shape
    rows = table_ref.shape[0]
    for d in range(owners):
        turned = jnp.swapaxes(slab_ref[d].reshape(2 * xl, high, lanes), 0, 1)
        for k in range(high):
            a_ref[d % 2, d // 2, k * rows : (k + 1) * rows] = jnp.dot(
                table_ref[...], turned[k], precision=precise, preferred_element_type=f32
            )


def x_spread(all_ref, table_ref, slab_ref):
    owners, xl, _, high, lanes = slab_ref.shape
    rows = table_ref.shape[1]
    for d in range(owners):
        parts = [
            jnp.dot(
                table_ref[...],
                all_ref[d % 2, d // 2, k * rows : (k + 1) * rows],
                precision=precise,
                preferred_element_type=f32,
            )
            for k in range(high)
        ]
        turned = jnp.swapaxes(jnp.stack(parts, axis=0), 0, 1)
        slab_ref[d] = turned.reshape(xl, 2, high, lanes)


def spread_weight(weight, turned):
    rows, cols = weight.shape[::-1] if turned else weight.shape

    def match(shape, low, high):
        a = lax.broadcasted_iota(jnp.int32, shape, 0)
        b = lax.broadcasted_iota(jnp.int32, shape, 1)
        return low(a) == high(b)

    tall = match((rows * ROWS, rows), lambda a: a // ROWS, lambda b: b)
    wide = match((cols, cols * ROWS), lambda a: a, lambda b: b // ROWS)
    tall = jnp.where(tall, 1.0, 0.0).astype(bf16)
    wide = jnp.where(wide, 1.0, 0.0).astype(bf16)
    half = (dot_nt if turned else dot)(tall, weight).astype(bf16)
    diagonal = match((rows * ROWS, cols * ROWS), lambda a: a % ROWS, lambda b: b % ROWS)
    return jnp.where(diagonal, dot(half, wide), 0.0).astype(bf16)


def turn(chunk_ref, out_ref):
    steps, high, lanes = out_ref.shape
    out_ref[...] = jnp.swapaxes(chunk_ref[...].reshape(high, steps, lanes), 0, 1)


def multiply(weights, in_ref, res_ref, first, count):
    steps, high, lanes = in_ref.shape
    KX, PL, _, _, C = weights[0].shape
    KY, PK = PL // MZ, MZ // high
    row = lax.broadcasted_iota(jnp.int32, (high, lanes), 0)
    lane = lax.broadcasted_iota(jnp.int32, (high, lanes), 1)
    low = (lane // C) % 2 == 0

    for half, w_ref in enumerate(weights):

        def one(k, half=half, w_ref=w_ref):
            at = 2 * (half * KX + k)
            rest = in_ref[at : at + 2]
            pieces = []
            for _ in range(3):
                pieces.append(rest.astype(bf16).astype(f32))
                rest = rest - pieces[-1]
            results = []
            for ky in range(KY):
                rows = [
                    piece[ri][:, (pk * KY + ky) * C : (pk * KY + ky + 1) * C]
                    for piece in pieces
                    for ri in range(2)
                    for pk in range(PK)
                ]
                base = ky * MZ + first * PK
                w = w_ref[k, base : base + count * PK].reshape(count * PK * 2 * C, C)
                terms = dot_nt(jnp.concatenate(rows, axis=0).astype(bf16), w)
                terms = terms.reshape(3, 2, PK, high, count * lanes)
                terms = (terms[2] + terms[1]) + terms[0]
                kept = []
                for ri in range(2):
                    value = None
                    for h in range(count):
                        own = slice(h * lanes, (h + 1) * lanes)
                        here = jnp.where(
                            lane < 2 * C, terms[ri, 0][:, own], terms[ri, 1][:, own]
                        )
                        value = here if value is None else jnp.where(row == first + h, here, value)
                    kept.append(value)
                real, imag = kept
                imag = jnp.where(low, -pltpu.roll(imag, lanes - C, 1), pltpu.roll(imag, C, 1))
                results.append(real + imag)
            one_, two = results
            real = jnp.where(low, one_, pltpu.roll(two, C, 1))
            imag = jnp.where(low, pltpu.roll(one_, lanes - C, 1), two)
            res_ref[at] = jnp.where(row < first, res_ref[at], real)
            res_ref[at + 1] = jnp.where(row < first, res_ref[at + 1], imag)

        for k in range(KX):
            one(k)


def forward_sum_body(
    xl,
    f_ref, ty_ref, zt_ref, xt_ref, lw_ref, w_ref,
    both_ref, gathered_ref, out_ref,
    slab_ref, wown_ref, woth_ref, chunk_ref, in_ref, res_ref, got_ref, kw_ref, all_ref,
    own_sem, ws, wr, ss, sr, gzs, gzr, gxs, gxr, *scatter
):
    i = pl.program_id(0)
    count = f_ref.shape[1]
    table, core = pair()
    _, z, x = place()
    zn = lax.axis_size("gx") // 2
    steps, high, _ = in_ref.shape
    fetch = pltpu.make_async_copy(w_ref, wown_ref, own_sem)
    swap = pltpu.make_async_remote_copy(
        w_ref, woth_ref, ws, wr, device_id=core, device_id_type=MESH
    )
    half = steps // 2
    cross = pltpu.make_async_remote_copy(
        in_ref.at[pl.ds(half, half)], got_ref, ss, sr, device_id=core, device_id_type=MESH
    )
    total = Scatter(scatter[0], chunk_ref, *scatter[1:])
    along, across = gather_parts(all_ref, gzs, gzr, gxs, gxr)
    rows = high // PIECES

    def mapped(p):
        total.finish(p)
        for h in range(rows * p, rows * (p + 1)):
            in_ref[:, h, :] = chunk_ref[h * steps : (h + 1) * steps]
        multiply((wown_ref, woth_ref), in_ref, res_ref, rows * p, rows)
        for h in range(rows * p, rows * (p + 1)):
            all_ref[x, z, h * steps : (h + 1) * steps] = res_ref[:, h, :]
        for j in (2, 1, 3):
            along(p, j).start()
        across(p, 0).start()

    def passed(p):
        for j in range(1, zn):
            along(p, j).wait_recv()
            across(p, j).start()

    @pl.when(i == 0)
    def _():
        greet(core=True)
        fetch.start()
        swap.start()
        in_ref[...] = jnp.zeros_like(in_ref)
        res_ref[...] = jnp.zeros_like(res_ref)
        kw_ref[...] = spread_weight(lw_ref[...], True)

    @pl.when(i < xl)
    def _():
        store_modes(
            slab_ref.at[:, pl.ds(i, 1)],
            plane_modes(lambda c: f_ref[0, c], count, ty_ref[...], zt_ref[...]),
        )

    @pl.when(i == xl - 1)
    def _():
        x_sum(slab_ref, xt_ref.at[table], scatter[0])
        total.start()

    @pl.when(i >= xl)
    def _():
        for y0 in range(0, f_ref.shape[2], 2 * ROWS):
            put_pair(out_ref, y0, dot(kw_ref[...], tile_pair(f_ref, y0)))

    @pl.when(i == xl + (3 * xl) // 16)
    def _():
        total.forward(0)

    @pl.when(i == xl + (5 * xl) // 16)
    def _():
        total.forward(1)

    @pl.when(i == xl + (7 * xl) // 16)
    def _():
        total.forward(2)
        fetch.wait()
        swap.wait()
        mapped(0)

    @pl.when(i == xl + (10 * xl) // 16)
    def _():
        total.forward(3)
        mapped(1)

    @pl.when(i == xl + (12 * xl) // 16)
    def _():
        mapped(2)

    @pl.when(i == xl + (14 * xl) // 16)
    def _():
        passed(0)

    @pl.when(i == 2 * xl - 1)
    def _():
        mapped(3)
        cross.start()
        for p in range(1, PIECES):
            passed(p)
        total.settle()
        cross.wait()
        both_ref[0] = in_ref[:half]
        both_ref[1] = got_ref[...]
        for p in range(PIECES):
            for j in range(zn):
                across(p, j).wait()
            for j in range(1, zn):
                along(p, j).wait_send()
        gathered_ref[...] = all_ref[...]


def grad_body(
    scale, cells, s_ref, g_ref, sums_ref, e_ref,
    out_ref, gw_ref, gq_ref, loss_ref, copy_ref
):
    _, PL, _, C, _ = out_ref.shape
    _, _, high, lanes = s_ref.shape
    KY, PK = PL // MZ, MZ // high
    copy_ref[...] = e_ref[...]

    @pl.when(pl.program_id(0) == 0)
    def _():
        total = sums_ref[...]
        gw_ref[...] = total[:, :C] * scale
        gq_ref[...] = (total[:, C : C + 8] * scale).T[:3]
        loss_ref[...] = total[:1, C + 3 : C + 4] * (1.0 / cells)

    def pieces(ref):
        high_part, low_part = split(ref[...].reshape(4, high, lanes))
        return high_part.astype(f32), low_part.astype(f32)

    f_high, f_low = pieces(s_ref)
    field = jnp.concatenate([f_high, f_low, f_high], axis=0).reshape(12 * high, lanes)
    field = field.astype(bf16)
    g_high, g_low = pieces(g_ref)
    grads = [g_high, g_high, g_low]
    swapped = [jnp.stack([g[1], -g[0], g[3], -g[2]], axis=0) for g in grads]
    turned = [
        jnp.concatenate(g, axis=0).reshape(12 * high, lanes).T for g in (grads, swapped)
    ]
    lane = lax.broadcasted_iota(jnp.int32, (C, 12 * high), 1) % high
    for pk in range(PK):
        for ky in range(KY):
            at = (pk * KY + ky) * C
            rows = [
                jnp.where(lane == h, turned[n][at : at + C], 0.0).astype(bf16)
                for h in range(high)
                for n in range(2)
            ]
            value = dot(jnp.concatenate(rows, axis=0), field[:, at : at + C])
            for h in range(high):
                for n in range(2):
                    row = (2 * h + n) * C
                    out_ref[0, ky * MZ + h * PK + pk, n] = value[row : row + C]


def tile_pair(ref, y0):
    count, nz = ref.shape[1], ref.shape[3]
    one = ref[0, :, pl.ds(y0, ROWS), :].reshape(count * ROWS, nz)
    two = ref[0, :, pl.ds(y0 + ROWS, ROWS), :].reshape(count * ROWS, nz)
    return jnp.concatenate([one, two], axis=1)


def put_pair(ref, y0, value):
    count, nz = ref.shape[1], ref.shape[3]
    ref[0, :, pl.ds(y0, ROWS), :] = value[:, :nz].reshape(count, ROWS, nz)
    ref[0, :, pl.ds(y0 + ROWS, ROWS), :] = value[:, nz:].reshape(count, ROWS, nz)


def local_body(f_ref, kw_ref, out_ref):
    for y0 in range(0, f_ref.shape[2], 2 * ROWS):
        put_pair(out_ref, y0, dot(kw_ref[...], tile_pair(f_ref, y0)))


def middle_body(scale, l_ref, m_ref, zi_ref, yi_ref, kp_ref, pre_ref, vel_ref):
    count, ny, nz = l_ref.shape[1], l_ref.shape[2], l_ref.shape[3]
    high, low = split(load_modes(m_ref, MY * count))
    wave = dot_tn(jnp.concatenate([high, high, low], axis=0), zi_ref[...])
    turned = jnp.swapaxes(wave.reshape(MY, count, 2 * nz), 0, 1)
    yi = yi_ref[...]
    for o in range(0, count, 2):
        pair = [
            jnp.concatenate([turned[i, :, :nz], turned[i, :, nz:]], axis=0) for i in (o, o + 1)
        ]
        both = dot(yi, jnp.concatenate(pair, axis=1).astype(bf16))
        pre_ref[0, o] = l_ref[0, o] + both[:, :nz] * scale
        pre_ref[0, o + 1] = l_ref[0, o + 1] + both[:, nz:] * scale

    for y0 in range(0, ny, 2 * ROWS):
        x = tile_pair(pre_ref, y0)
        t = jnp.tanh(x * (ROOT + (0.044715 * ROOT) * (x * x)))
        half = 0.5 * x
        hidden = (half + half * t).astype(bf16)
        put_pair(vel_ref, y0, dot(kp_ref[...], hidden))


def backward_body(
    f_ref, pre_ref, gv_ref, ty_ref, zt_ref, kpt_ref, out_ref, gw_ref, gq_ref, gp_ref, first=0
):
    count, ny, nz = f_ref.shape[1], f_ref.shape[2], f_ref.shape[3]

    @pl.when(pl.program_id(0) == first)
    def _():
        gw_ref[...] = jnp.zeros_like(gw_ref)
        gq_ref[...] = jnp.zeros_like(gq_ref)

    hiddens, grads, fields, slopes = [], [], [], []
    for y0 in range(0, ny, 2 * ROWS):
        gv = tile_pair(gv_ref, y0)
        x = tile_pair(pre_ref, y0)
        cubic = (0.044715 * ROOT) * (x * x)
        t = jnp.tanh(x * (ROOT + cubic))
        cdf = 0.5 + 0.5 * t
        hidden = (x * cdf).astype(bf16)
        slope = cdf + (x * (ROOT + 3.0 * cubic)) * (0.5 - 0.5 * (t * t))
        gp = (dot(kpt_ref[...], gv) * slope).astype(bf16)
        put_pair(gp_ref, y0, gp)
        hiddens.append(hidden)
        grads.append(gp)
        slopes.append(gv)
        fields.append(tile_pair(f_ref, y0))
    gw_ref[...] += dot_nt(jnp.concatenate(fields, axis=1), jnp.concatenate(grads, axis=1))
    gq_ref[...] += dot_nt(jnp.concatenate(hiddens, axis=1), jnp.concatenate(slopes, axis=1))

    store_modes(out_ref, plane_modes(lambda c: gp_ref[0, c], count, ty_ref[...], zt_ref[...]))


def fold(total, columns):
    rows, cols = total.shape
    row = lax.broadcasted_iota(jnp.int32, total.shape, 0) % ROWS
    col = lax.broadcasted_iota(jnp.int32, total.shape, 1) % ROWS
    kept = jnp.where(row == col, total, 0.0).reshape(rows // ROWS, ROWS, cols)
    lane = lax.broadcasted_iota(jnp.int32, (cols, 128), 1)
    block = lax.broadcasted_iota(jnp.int32, (cols, 128), 0) // ROWS
    gather = jnp.where(lane == block + columns, 1.0, 0.0)
    return jnp.dot(jnp.sum(kept, axis=1), gather, precision=precise, preferred_element_type=f32)


def gather_parts(all_ref, zs, zr, xs, xr):
    _, z, x = place()
    zn, rows = all_ref.shape[1], all_ref.shape[2]
    step = rows // PIECES

    def along(p, j):
        part = pl.ds(p * step, step)
        return pltpu.make_async_remote_copy(
            all_ref.at[x, z, part],
            all_ref.at[x, z, part],
            zs.at[p, j - 1],
            zr.at[p, j - 1],
            device_id={"gx": lax.rem(z + j, zn) * 2 + x},
            device_id_type=MESH,
        )

    def across(p, j):
        part = pl.ds(p * step, step)
        t = lax.rem(z - j + zn, zn)
        return pltpu.make_async_remote_copy(
            all_ref.at[x, t, part],
            all_ref.at[x, t, part],
            xs.at[p, j],
            xr.at[p, j],
            device_id={"gx": z * 2 + 1 - x},
            device_id_type=MESH,
        )

    return along, across


def inward(m, count):
    odd = m % 2
    return odd * (count - 1 - m // 2) + (1 - odd) * (m // 2)


def step_body(
    scale, xl, rep,
    f_ref, l_ref, all_ref, t_ref, mult_ref, pw_ref, xb_ref, zi_ref, yi_ref,
    ty_ref, zt_ref, xt_ref,
    e_ref, both_ref, sums_ref,
    kp_ref, kpt_ref,
    pre_ref, vel_ref, gv_ref, gp_ref, slab_ref, gw_ref, gq_ref, loss_ref,
    edge_ref, halo_ref, us, ur, ps, pr,
    pack_ref, ebuf, es, er, chunk_ref, turned_ref, got_ref, other_ref, cs, cr, *scatter
):
    i = pl.program_id(0)
    me, z, x = place()
    table, core = pair()
    gx = lax.axis_size("gx")
    right = {"gx": lax.rem(me + 1, gx)}
    left = {"gx": lax.rem(me + gx - 1, gx)}

    def halo(k, sems):
        return pltpu.make_async_remote_copy(
            edge_ref.at[k],
            halo_ref.at[k],
            sems[0].at[k % 2],
            sems[1].at[k % 2],
            device_id=left if k % 2 == 0 else right,
            device_id_type=MESH,
        )

    def penalty(p, before, after):
        u = vel_ref[p, 1], vel_ref[p, 2]
        rows, lanes = u[0].shape
        slope = (after - before) * 0.5
        slope = slope + (pltpu.roll(u[0], rows - 1, 0) - pltpu.roll(u[0], 1, 0)) * 0.5
        slope = slope + (pltpu.roll(u[1], lanes - 1, 1) - pltpu.roll(u[1], 1, 1)) * 0.5
        lam = mult_ref[p].astype(f32) / 64.0
        e_ref[p] = lam + penalty_weight * slope
        add_loss((lam + (0.5 * penalty_weight) * slope) * slope)

    def add_loss(value):
        rows, lanes = value.shape
        loss_ref[...] = loss_ref[...] + jnp.sum(value.reshape(rows // 8, 8, lanes), axis=0)

    @pl.when(i == 0)
    def _():
        loss_ref[...] = jnp.zeros_like(loss_ref)
        greet(True, True)
        kp_ref[...] = spread_weight(pw_ref[...], False)
        kpt_ref[...] = spread_weight(pw_ref[...], True)
        x_spread(all_ref, xb_ref.at[table], slab_ref)

    @pl.when(i < xl)
    def _():
        p = inward(i, xl)
        plane_ref = pre_ref.at[pl.ds(p, 1)]
        modes_ref = slab_ref.at[:, pl.ds(p, 1)]
        middle_body(
            scale, l_ref, modes_ref, zi_ref, yi_ref, kp_ref, plane_ref,
            vel_ref.at[pl.ds(p, 1)],
        )

    @pl.when(i == 1)
    def _():
        edge_ref[0] = vel_ref[0, 0]
        edge_ref[1] = vel_ref[xl - 1, 0]
        for k in (0, 1):
            halo(k, (us, ur)).start()

    @pl.when(i == xl // 2)
    def _():
        for k in (0, 1):
            halo(k, (us, ur)).wait()
        penalty(0, halo_ref[1], vel_ref[1, 0])
        penalty(xl - 1, vel_ref[xl - 2, 0], halo_ref[0])
        edge_ref[2] = e_ref[0]
        edge_ref[3] = e_ref[xl - 1]
        for k in (2, 3):
            halo(k, (ps, pr)).start()

    @pl.when(i == xl - 1)
    def _():
        def one(p, carry):
            penalty(p, vel_ref[p - 1, 0], vel_ref[p + 1, 0])
            return carry

        lax.fori_loop(1, xl - 1, one, 0)
        for k in (2, 3):
            halo(k, (ps, pr)).wait()

    @pl.when(i >= xl)
    def _():
        p = i - xl
        e = e_ref[p]
        rows, lanes = e.shape
        before = lax.select(
            jnp.broadcast_to(p == 0, e.shape), halo_ref[3], e_ref[lax.rem(p + xl - 1, xl)]
        )
        after = lax.select(
            jnp.broadcast_to(p == xl - 1, e.shape), halo_ref[2], e_ref[lax.rem(p + 1, xl)]
        )
        slopes = (
            (after - before) * 0.5,
            (pltpu.roll(e, rows - 1, 0) - pltpu.roll(e, 1, 0)) * 0.5,
            (pltpu.roll(e, lanes - 1, 1) - pltpu.roll(e, 1, 1)) * 0.5,
        )
        for j in range(3):
            misfit = vel_ref[p, j] - t_ref[0, j].astype(f32)
            add_loss(misfit * misfit)
            gv_ref[0, j] = ((2.0 * misfit - slopes[j]) / rep).astype(bf16)
        backward_body(
            f_ref, pre_ref.at[pl.ds(p, 1)], gv_ref, ty_ref, zt_ref, kpt_ref,
            slab_ref.at[:, pl.ds(p, 1)], gw_ref, gq_ref, gp_ref, first=xl,
        )

    @pl.when(i == pl.num_programs(0) - 1)
    def _():
        x_sum(slab_ref, xt_ref.at[table], scatter[0])
        total = Scatter(scatter[0], chunk_ref, *scatter[1:])
        total.start()
        count = f_ref.shape[1]
        lane = lax.broadcasted_iota(jnp.int32, (count, 128), 1)
        pack_ref[...] = (
            fold(gw_ref[...], 0)
            + fold(gq_ref[...], count)
            + jnp.where(lane == count + 3, jnp.sum(loss_ref[...]), 0.0)
        )
        scatter_sum(total, pack_ref, ebuf, es, er)
        turn(chunk_ref, turned_ref)
        half = turned_ref.shape[0] // 2
        copies = [
            send(turned_ref.at[pl.ds(half, half)], got_ref, (cs.at[0], cr.at[0]), core),
            send(pack_ref, other_ref, (cs.at[1], cr.at[1]), core),
        ]
        for copy in copies:
            copy.wait()
        both_ref[0] = turned_ref[:half]
        both_ref[1] = got_ref[...]
        sums_ref[...] = pack_ref[...] + other_ref[...]


def whole(shape):
    return pl.BlockSpec(shape, lambda i: (0,) * len(shape))


def plane(shape):
    return pl.BlockSpec((1,) + tuple(shape), lambda i: (i,) + (0,) * len(shape))


params = pltpu.CompilerParams(
    dimension_semantics=("arbitrary",), vmem_limit_bytes=56 * 1024 * 1024
)


def extended(value, axis_name):
    count = lax.axis_size(axis_name)
    up = [(i, (i + 1) % count) for i in range(count)]
    down = [(j, i) for i, j in up]
    before = lax.ppermute(value[-1:], axis_name, up)
    after = lax.ppermute(value[:1], axis_name, down)
    return jnp.concatenate([before, value, after], axis=0)


def central(values, axis):
    return (jnp.roll(values, -1, axis) - jnp.roll(values, 1, axis)) * 0.5


def local(fields, targets, multipliers, local_weight, proj_weight, spectral_weight):
    gx = lax.axis_size("gx")
    rep = lax.axis_size("rep")
    _, xl, C, NY, NZ = fields.shape
    NX = xl * gx
    PL = MY * MZ // gx
    scale = 1.0 / math.sqrt(NX * NY * NZ)
    fields, targets, multipliers = fields[0], targets[0], multipliers[0]

    cos_y, sin_y = fourier_tables(NY, MY)
    ty = jnp.asarray(np.concatenate([cos_y.T, -sin_y.T], 0).astype(ml_dtypes.bfloat16))
    yi = jnp.asarray(np.concatenate([cos_y, -sin_y], 1).astype(ml_dtypes.bfloat16))
    cos_z, sin_z = fourier_tables(NZ, MZ)
    zt = np.concatenate(
        [np.concatenate([cos_z.T, sin_z.T], 1), np.concatenate([-sin_z.T, cos_z.T], 1)], 0
    )
    direct = gx == 8 and rep == 2 and C == 32
    KY = MY // gx if direct else 0
    PK = 128 // (KY * C) if direct else 1
    HZ = MZ // PK
    order = np.arange(2 * MZ).reshape(2, HZ, PK).transpose(2, 0, 1).reshape(-1)
    zt = zt[order]
    zi_high, zi_low = halves(zt)
    zt = jnp.asarray(np.concatenate([zi_high, zi_low], 0))
    zi = jnp.asarray(np.concatenate([zi_high, zi_low, zi_high], 0))
    cos_x, sin_x = fourier_tables(NX, MX)
    xt = np.stack(
        [np.stack([cos_x.T, sin_x.T], 1), np.stack([-sin_x.T, cos_x.T], 1)], 1
    )
    xt = xt.reshape(MX, 2, 2, gx, xl).transpose((0, 1, 3, 4, 2) if direct else (0, 1, 3, 2, 4))
    xt = xt.reshape(2 * MX, 2 * NX)
    x_forward = jnp.asarray(xt * np.float32(scale))
    x_back = jnp.asarray(np.ascontiguousarray(xt.T))

    def spread(weight):
        rows, columns = weight.shape
        left = jnp.asarray(np.kron(np.eye(rows), np.ones((ROWS, 1))), dtype=bf16)
        right = jnp.asarray(np.kron(np.eye(columns), np.ones((1, ROWS))), dtype=bf16)
        diagonal = jnp.asarray(np.kron(np.ones((rows, columns)), np.eye(ROWS)), dtype=bf16)
        return dot(dot(left, weight).astype(bf16), right).astype(bf16) * diagonal

    kw = spread(local_weight.T)
    kp = spread(proj_weight.T)
    kpt = spread(proj_weight)

    field_spec = plane((C, NY, NZ))
    modes_shape = jax.ShapeDtypeStruct((xl, 2 * MZ, MY * C), f32)
    modes_spec = plane((2 * MZ, MY * C))
    vel_spec = plane((3, NY, NZ))

    def to_owner(slab):
        slab = slab.reshape(xl, 2, MZ, MY, C).transpose(3, 2, 1, 0, 4)
        slab = slab.reshape(gx, PL, 2, xl, C).transpose(0, 2, 3, 1, 4)
        slab = slab.reshape(gx, 2 * xl, PL * C)
        slab = lax.all_to_all(slab, "gx", split_axis=0, concat_axis=0, tiled=True)
        out = jnp.dot(x_forward, slab.reshape(2 * NX, PL * C), precision=precise)
        return out.reshape(MX, 2, PL, C)

    def to_planes(modes):
        out = jnp.dot(x_back, modes.reshape(2 * MX, PL * C), precision=precise)
        out = out.reshape(gx, 2 * xl, PL * C)
        out = lax.all_to_all(out, "gx", split_axis=0, concat_axis=0, tiled=True)
        out = out.reshape(gx, 2, xl, PL, C).transpose(0, 3, 1, 2, 4)
        out = out.reshape(MY, MZ, 2, xl, C).transpose(3, 2, 1, 0, 4)
        return out.reshape(xl, 2 * MZ, MY * C)

    def both_samples(modes):
        part = modes.reshape(rep, MX // rep, 2, PL, C)
        return lax.all_to_all(part, "rep", split_axis=0, concat_axis=0, tiled=True)

    ZN = gx // 2
    QR = HZ * 2 * MX
    slab_scratch = pltpu.VMEM((gx, xl, 2, HZ, 128), f32)
    dma = pltpu.SemaphoreType.DMA

    def comm(number):
        return pltpu.CompilerParams(
            dimension_semantics=("arbitrary",),
            vmem_limit_bytes=60 * 1024 * 1024,
            collective_id=number,
            has_side_effects=True,
        )

    if direct:
        parts = xt.reshape(rep, MX, gx, 2 * xl)
        parts = np.stack([np.concatenate([parts[r], parts[1 - r]], 0) for r in range(rep)])
        parts = parts.transpose(0, 2, 1, 3).reshape(rep * gx, 2 * MX, 2 * xl)
        x_own = jnp.asarray(parts * np.float32(scale))
        x_out = jnp.asarray(np.ascontiguousarray(parts.transpose(0, 2, 1)))
        chunk_shape = jax.ShapeDtypeStruct((QR, 128), f32)
        weight_scratch = pltpu.VMEM(spectral_weight.shape, bf16)
        row_scratch = pltpu.VMEM((2 * MX, HZ, 128), f32)
        both_shape = jax.ShapeDtypeStruct((2, MX, HZ, 128), f32)
        half_scratch = pltpu.VMEM((MX, HZ, 128), f32)
        gathered_shape = jax.ShapeDtypeStruct((2, ZN, QR, 128), f32)
        wide = C * ROWS
        spectrum, gathered, mapped = pl.pallas_call(
            functools.partial(forward_sum_body, xl),
            grid=(2 * xl,),
            out_shape=(
                both_shape,
                gathered_shape,
                jax.ShapeDtypeStruct((xl, C, NY, NZ), f32),
            ),
            in_specs=[
                pl.BlockSpec((1, C, NY, NZ), lambda i: (i % xl, 0, 0, 0)),
                whole(ty.shape),
                whole(zt.shape),
                whole(x_own.shape),
                whole((C, C)),
                pl.BlockSpec(memory_space=pl.ANY),
            ],
            out_specs=(
                whole(both_shape.shape),
                whole(gathered_shape.shape),
                pl.BlockSpec((1, C, NY, NZ), lambda i: ((i % xl) * (i // xl), 0, 0, 0)),
            ),
            scratch_shapes=[slab_scratch, weight_scratch, weight_scratch]
            + [pltpu.VMEM((QR, 128), f32), row_scratch, row_scratch, half_scratch]
            + [pltpu.VMEM((wide, wide), bf16), pltpu.VMEM(gathered_shape.shape, f32)]
            + [dma] * 5
            + [dma((PIECES, ZN - 1))] * 2
            + [dma((PIECES, ZN))] * 2
            + scatter_scratch(ZN, QR),
            compiler_params=comm(1),
        )(fields, ty, zt, x_own, local_weight, spectral_weight)
    else:
        slab = pl.pallas_call(
            forward_body,
            grid=(xl,),
            out_shape=modes_shape,
            in_specs=[field_spec, whole(ty.shape), whole(zt.shape)],
            out_specs=modes_spec,
            compiler_params=params,
        )(fields, ty, zt)
        mapped = pl.pallas_call(
            local_body,
            grid=(xl,),
            out_shape=jax.ShapeDtypeStruct((xl, C, NY, NZ), f32),
            in_specs=[field_spec, whole(kw.shape)],
            out_specs=field_spec,
            compiler_params=pltpu.CompilerParams(vmem_limit_bytes=20 * 1024 * 1024),
        )(fields, kw)
    middle_shape = (
        jax.ShapeDtypeStruct((xl, C, NY, NZ), f32),
        jax.ShapeDtypeStruct((xl, 3, NY, NZ), f32),
    )
    wide = C * ROWS
    if direct:
        tables = [proj_weight.T, x_out, zi, yi, ty, zt, x_own]

        def once(shape):
            return pl.BlockSpec(
                shape, lambda i: (0,) * len(shape), pipeline_mode=pl.Buffered(1)
            )

        penalty, chunk, sums = pl.pallas_call(
            functools.partial(step_body, scale, xl, rep),
            grid=(2 * xl,),
            out_shape=(
                jax.ShapeDtypeStruct((xl, NY, NZ), f32),
                both_shape,
                jax.ShapeDtypeStruct((C, 128), f32),
            ),
            in_specs=[
                pl.BlockSpec(
                    (1, C, NY, NZ),
                    lambda i: ((i % xl) * (i // xl), 0, 0, 0),
                ),
                pl.BlockSpec(
                    (1, C, NY, NZ),
                    lambda i: (
                        inward(i % xl, xl) * (1 - i // xl) + inward(xl - 1, xl) * (i // xl),
                        0,
                        0,
                        0,
                    ),
                ),
                once(gathered_shape.shape),
                pl.BlockSpec((1, 3, NY, NZ), lambda i: ((i % xl) * (i // xl), 0, 0, 0)),
                once((xl, NY, NZ)),
            ]
            + [once(t.shape) for t in tables],
            out_specs=(whole((xl, NY, NZ)), whole(both_shape.shape), whole((C, 128))),
            scratch_shapes=[
                pltpu.VMEM((3 * ROWS, wide), bf16),
                pltpu.VMEM((wide, 3 * ROWS), bf16),
                pltpu.VMEM((xl, C, NY, NZ), f32),
                pltpu.VMEM((xl, 3, NY, NZ), f32),
                pltpu.VMEM((1, 3, NY, NZ), bf16),
                pltpu.VMEM((1, C, NY, NZ), bf16),
                slab_scratch,
                pltpu.VMEM((wide, wide), f32),
                pltpu.VMEM((wide, 3 * ROWS), f32),
                pltpu.VMEM((8, NZ), f32),
                pltpu.VMEM((4, NY, NZ), f32),
                pltpu.VMEM((4, NY, NZ), f32),
            ]
            + [dma((2,))] * 4
            + [pltpu.VMEM((C, 128), f32), pltpu.VMEM((ZN, C, 128), f32), dma((ZN,)), dma((ZN,))]
            + [pltpu.VMEM((QR, 128), f32), row_scratch, half_scratch]
            + [pltpu.VMEM((C, 128), f32), dma((2,)), dma((2,))]
            + scatter_scratch(ZN, QR),
            compiler_params=comm(2),
        )(fields, mapped, gathered, targets, multipliers, *tables)
        KX = MX // rep
        modes_of = pl.BlockSpec((2, 2, HZ, 128), lambda i: (0, i, 0, 0))
        planes = pl.BlockSpec((xl // KX, NY, NZ), lambda i: (i, 0, 0))
        grad_r, grad_w, grad_q, loss, penalty = pl.pallas_call(
            functools.partial(grad_body, scale, rep * NX * NY * NZ),
            grid=(KX,),
            out_shape=(
                jax.ShapeDtypeStruct(spectral_weight.shape, f32),
                jax.ShapeDtypeStruct((C, C), f32),
                jax.ShapeDtypeStruct((3, C), f32),
                jax.ShapeDtypeStruct((1, 1), f32),
                jax.ShapeDtypeStruct(penalty.shape, f32),
            ),
            in_specs=[modes_of, modes_of, whole((C, 128)), planes],
            out_specs=(
                plane((PL, 2, C, C)),
                whole((C, C)),
                whole((3, C)),
                whole((1, 1)),
                planes,
            ),
            compiler_params=params,
        )(spectrum, chunk, sums, penalty)
        return (penalty[None], grad_r, grad_w, grad_q.T, loss[0])
    else:
        weights = spectral_weight
        weights = weights.transpose(2, 3, 4, 0, 1).reshape(1, 2, C, C, MX // rep * PL)
        weights = lax.all_gather(weights, "rep", axis=0, tiled=True)
        spectrum = to_owner(slab)
        KX = MX // rep
        turned = spectrum.reshape(rep, KX, 2, PL, C).transpose(0, 2, 4, 1, 3)
        turned = turned.reshape(rep, 2, 1, C, KX * PL)
        w_re, w_im = weights[:, 0].astype(f32), weights[:, 1].astype(f32)
        s_re, s_im = turned[:, 0], turned[:, 1]
        product = jnp.stack(
            [jnp.sum(w_re * s_re - w_im * s_im, axis=2), jnp.sum(w_re * s_im + w_im * s_re, axis=2)],
            axis=1,
        )
        product = product.reshape(rep, 2, C, KX, PL).transpose(0, 3, 1, 4, 2)
        product = product.reshape(MX, 2, PL, C)
        spectra = both_samples(spectrum)
        wave = to_planes(product)
        pre, velocity = pl.pallas_call(
            functools.partial(middle_body, scale),
            grid=(xl,),
            out_shape=middle_shape,
            in_specs=[field_spec, modes_spec, whole(zi.shape), whole(yi.shape), whole(kp.shape)],
            out_specs=(field_spec, vel_spec),
            compiler_params=params,
        )(mapped, wave, zi, yi, kp)
        padded = extended(velocity[:, 0].astype(bf16), "gx").astype(f32)
        slope_x = (padded[2:] - padded[:-2]) * 0.5
        divergence = slope_x + central(velocity[:, 1], 1) + central(velocity[:, 2], 2)
        lam = multipliers.astype(f32) / 64.0
        penalty = lam + penalty_weight * divergence
        misfit = velocity - targets.astype(f32)
        loss_sum = (
            jnp.sum(misfit * misfit)
            + jnp.sum(lam * divergence)
            + 0.5 * penalty_weight * jnp.sum(divergence * divergence)
        )
        padded = extended(penalty.astype(bf16), "gx").astype(f32)
        pen_x = (padded[2:] - padded[:-2]) * 0.5
        slopes = jnp.stack([pen_x, central(penalty, 1), central(penalty, 2)], axis=1)
        grad_vel = ((2.0 * misfit - slopes) / rep).astype(bf16)
        grad_slab, gw, gq = pl.pallas_call(
            backward_body,
            grid=(xl,),
            out_shape=(
                modes_shape,
                jax.ShapeDtypeStruct((wide, wide), f32),
                jax.ShapeDtypeStruct((wide, 3 * ROWS), f32),
            ),
            in_specs=[field_spec, field_spec, vel_spec]
            + [whole(ty.shape), whole(zt.shape), whole(kpt.shape)],
            out_specs=(modes_spec, whole((wide, wide)), whole((wide, 3 * ROWS))),
            scratch_shapes=[pltpu.VMEM((1, C, NY, NZ), bf16)],
            compiler_params=params,
        )(fields, pre, grad_vel, ty, zt, kpt)
        gather = jnp.asarray(np.kron(np.eye(C), np.ones((1, ROWS))).astype(np.float32))
        gather_q = jnp.asarray(np.kron(np.eye(3), np.ones((ROWS, 1))).astype(np.float32))
        mask = jnp.asarray(np.kron(np.ones((C, C)), np.eye(ROWS)).astype(np.float32))
        mask_q = jnp.asarray(np.kron(np.ones((C, 3)), np.eye(ROWS)).astype(np.float32))
        grad_w = jnp.dot(gather, gw * mask, precision=precise)
        grad_w = jnp.dot(grad_w, gather.T, precision=precise)
        grad_q = jnp.dot(gather, gq * mask_q, precision=precise)
        grad_q = jnp.dot(grad_q, gather_q, precision=precise)
        grads = both_samples(to_owner(grad_slab))
        packed = jnp.concatenate([grad_w.reshape(-1), grad_q.reshape(-1), loss_sum.reshape(1)])
        packed = lax.psum(packed, ("gx", "rep"))
        grad_w = packed[: C * C].reshape(C, C)
        grad_q = packed[C * C : C * C + 3 * C].reshape(C, 3)
        loss = packed[-1:]
    loss = loss / (rep * NX * NY * NZ)

    g_re, g_im = grads[:, :, 0], grads[:, :, 1]
    across = jnp.stack([jnp.stack([g_re, g_im], 3), jnp.stack([g_im, -g_re], 3)], 1)
    terms = [
        across[b, t][..., None] * spectra[b, :, t][:, :, None, None, :]
        for b in range(rep)
        for t in range(2)
    ]
    grad_r = sum(terms[1:], terms[0])
    return (penalty[None], grad_r, grad_w * scale, grad_q * scale, loss)


def solution(mesh):
    in_specs = (
        P(("grp", "rep"), "gx", None, None, None),
        P(("grp", "rep"), "gx", None, None, None),
        P(("grp", "rep"), "gx", None, None),
        P(),
        P(),
        P("rep", "gx", None, None, None),
    )
    out_specs = (
        P(("grp", "rep"), "gx", None, None),
        P(("grp", "rep"), "gx", None, None, None),
        P("grp", None),
        P("grp", None),
        P("grp"),
    )
    return jax.shard_map(local, mesh=mesh, in_specs=in_specs, out_specs=out_specs, check_vma=False)
```
